128 devices in a mesh: ctx: 64 (over y, x, z), head: 2 (over core).
Axes of the slice: x: 4, y: 4, z: 4, core: 2. Of those that a mesh axis runs over, the one named last changes fastest.
Arguments:
- queries: float32 [16384, 2048], P('ctx', 'head')
- keys: float32 [16384, 512], P(('ctx', 'head'))
- values: float32 [16384, 512], P(('ctx', 'head')), may hold values from -6 to 6
- cotangent: float32 [16384, 2048], P('ctx', 'head'), may hold values from -6 to 6
- selected: int32 [16, 3], replicated, may hold values from -1 to 15, as said below
Outputs:
- attended: float32 [16384, 2048], P('ctx', 'head')
- grad_queries: float32 [16384, 2048], P('ctx', 'head')
- grad_keys: float32 [16384, 512], P(('ctx', 'head'))
- grad_values: float32 [16384, 512], P(('ctx', 'head'))
The draws below stay inside these ranges and needn't reach their ends.
Inputs may be any that keep to these rules, and one draw needn't show every extreme that they name: selected[b, 0] = b; entries 1 and 2 of row b are different blocks before b, except that an entry is -1 when no further block before b is left: row 0 is [0, -1, -1] and row 1 is [1, 0, -1].
All inputs are finite; a program needn't handle non-finite values.
Results may differ from the reference program's by a relative error of at most 0.0003.
Values sent between devices are 32-bit elements; how exact they have to be, the bound alone decides.
No kernel may reach another device: no remote copies, remote signals or barrier semaphores. Data moves between devices by JAX's collectives and lax.ppermute only.
A program may use at most 192 MiB of HBM per device.

```python
import math
import jax
import jax.numpy as jnp
from jax import lax

QUERY_HEADS = 16
KEY_VALUE_HEADS = 4
HEAD_WIDTH = 128
BLOCK_TOKENS = 1024
TOPK = 3
SEQUENCE_LENGTH = 16384
NBLK = 16


def shared_keys(key):
    base_position = jax.random.fold_in(key, 11)
    unscaled_scores = jax.random.normal(jax.random.fold_in(base_position, 1), (SEQUENCE_LENGTH, KEY_VALUE_HEADS * HEAD_WIDTH), jnp.float32)
    unscaled_scores = jnp.clip(unscaled_scores, -5.0, 5.0)
    return unscaled_scores


def draw_keys(key, part):
    return shared_keys(key)


def draw_queries(key, part):
    base_position = jax.random.fold_in(key, 11)
    noise = jax.random.normal(jax.random.fold_in(base_position, 2), (SEQUENCE_LENGTH, QUERY_HEADS * HEAD_WIDTH), jnp.float32)
    noise = jnp.clip(noise, -5.0, 5.0)
    return noise


def draw_selected(key, part):
    base_position = jax.random.fold_in(key, 23)
    popular = jax.random.randint(jax.random.fold_in(base_position, 1), (NBLK,), 0, 4, jnp.int32)
    noise = jax.random.randint(jax.random.fold_in(base_position, 2), (NBLK, NBLK), 0, 65536, jnp.int32)
    column = jnp.arange(NBLK, dtype=jnp.int32)[None, :]
    row_index = jnp.arange(NBLK, dtype=jnp.int32)[:, None]
    ranking = (popular[None, :] * 65536 + noise) * NBLK + column
    ranking = jnp.where(column < row_index, ranking, -1)
    best, picks = lax.top_k(ranking, TOPK - 1)
    picks = jnp.where(best >= 0, picks.astype(jnp.int32), -1)
    return jnp.concatenate([row_index, picks], axis=1).astype(jnp.int32)


def block_levels(key, dims, split, least, top_value):
    def one(position, blocks):
        steps = jax.random.uniform(jax.random.fold_in(jax.random.fold_in(key, 6), position), (blocks,), jnp.float32, least / len(split), top_value / len(split))
        return jnp.repeat(jnp.exp(steps), dims[position] // blocks).reshape((-1,) + (1,) * (len(dims) - position - 1))

    loudness = one(*split[0])
    for cut in split[1:]:
        loudness = loudness * one(*cut)
    return loudness


def normal_values(stream_key, dims, scale, limit, cuts=(), kind=jnp.bfloat16):
    drawn = scale * jax.random.normal(stream_key, dims, jnp.float32)
    if cuts:
        drawn = drawn * block_levels(stream_key, dims, cuts, -0.22, 0.18)
    return jnp.clip(drawn, -limit, limit).astype(kind)


def setup_inputs(seed: int = 0) -> dict:
    streams_of = jax.random.split(jax.random.key(seed), 6)
    return {
        "queries": draw_queries(jax.random.fold_in(streams_of[5], 71), 0),
        "keys": draw_keys(jax.random.fold_in(streams_of[5], 71), 0),
        "values": normal_values(streams_of[2], (SEQUENCE_LENGTH, KEY_VALUE_HEADS * HEAD_WIDTH), 1.0, 6.0, ((0, 128),), jnp.float32),
        "cotangent": normal_values(streams_of[3], (SEQUENCE_LENGTH, QUERY_HEADS * HEAD_WIDTH), 1.0, 6.0, ((0, 64), (1, 2)), jnp.float32),
        "selected": draw_selected(jax.random.fold_in(streams_of[5], 71), 0),
    }


def reference(queries, keys, values, cotangent, selected):
    scaling = 1.0 / math.sqrt(HEAD_WIDTH)
    group_width = QUERY_HEADS // KEY_VALUE_HEADS
    heads_of_keys = keys.reshape(SEQUENCE_LENGTH, KEY_VALUE_HEADS, HEAD_WIDTH)
    heads_of_values = values.reshape(SEQUENCE_LENGTH, KEY_VALUE_HEADS, HEAD_WIDTH)
    highest = lax.Precision.HIGHEST

    def step(carry, block_index):
        key_gradient_total, value_gradient_total = carry
        first_position = (block_index * BLOCK_TOKENS).astype(jnp.int32)
        block_of_queries = lax.dynamic_slice_in_dim(queries, first_position, BLOCK_TOKENS, 0).reshape(BLOCK_TOKENS, KEY_VALUE_HEADS, group_width, HEAD_WIDTH)
        cotangent_block = lax.dynamic_slice_in_dim(cotangent, first_position, BLOCK_TOKENS, 0).reshape(BLOCK_TOKENS, KEY_VALUE_HEADS, group_width, HEAD_WIDTH)
        query_pos = first_position + jnp.arange(BLOCK_TOKENS, dtype=jnp.int32)
        key_parts, value_parts, masks, offsets = ([], [], [], [])
        for slot_index in range(TOPK):
            chosen = selected[block_index, slot_index]
            offset = (jnp.maximum(chosen, 0) * BLOCK_TOKENS).astype(jnp.int32)
            offsets.append(offset)
            key_parts.append(lax.dynamic_slice_in_dim(heads_of_keys, offset, BLOCK_TOKENS, 0))
            value_parts.append(lax.dynamic_slice_in_dim(heads_of_values, offset, BLOCK_TOKENS, 0))
            if slot_index == 0:
                key_pos = offset + jnp.arange(BLOCK_TOKENS, dtype=jnp.int32)
                masks.append(key_pos[None, :] <= query_pos[:, None])
            else:
                masks.append(jnp.broadcast_to(chosen >= 0, (BLOCK_TOKENS, BLOCK_TOKENS)))
        picked_keys = jnp.concatenate(key_parts, 0)
        picked_values = jnp.concatenate(value_parts, 0)
        allowed = jnp.concatenate(masks, 1)
        scores = scaling * jnp.einsum('thgd,shd->hgts', block_of_queries, picked_keys, precision=highest)
        scores = jnp.where(allowed[None, None], scores, -jnp.inf)
        maximum = lax.optimization_barrier(jnp.max(scores, axis=-1, keepdims=True))
        probs = jnp.exp(scores - maximum)
        probs = probs / lax.optimization_barrier(jnp.sum(probs, axis=-1, keepdims=True))
        attended = jnp.einsum('hgts,shd->thgd', probs, picked_values, precision=highest)
        row_dots = jnp.transpose(lax.optimization_barrier(jnp.sum(cotangent_block * attended, axis=-1)), (1, 2, 0))
        grad_probs = jnp.einsum('thgd,shd->hgts', cotangent_block, picked_values, precision=highest)
        grad_scores = probs * (grad_probs - row_dots[..., None])
        query_gradient = scaling * jnp.einsum('hgts,shd->thgd', grad_scores, picked_keys, precision=highest)
        grad_k_sel = scaling * jnp.einsum('hgts,thgd->shd', grad_scores, block_of_queries, precision=highest)
        grad_v_sel = jnp.einsum('hgts,thgd->shd', probs, cotangent_block, precision=highest)
        for slot_index in range(TOPK):
            offset = offsets[slot_index]
            piece_k = grad_k_sel[slot_index * BLOCK_TOKENS:(slot_index + 1) * BLOCK_TOKENS]
            piece_v = grad_v_sel[slot_index * BLOCK_TOKENS:(slot_index + 1) * BLOCK_TOKENS]
            key_gradient_total = lax.dynamic_update_slice_in_dim(key_gradient_total, lax.dynamic_slice_in_dim(key_gradient_total, offset, BLOCK_TOKENS, 0) + piece_k, offset, 0)
            value_gradient_total = lax.dynamic_update_slice_in_dim(value_gradient_total, lax.dynamic_slice_in_dim(value_gradient_total, offset, BLOCK_TOKENS, 0) + piece_v, offset, 0)
        return ((key_gradient_total, value_gradient_total), (attended.reshape(BLOCK_TOKENS, QUERY_HEADS * HEAD_WIDTH), query_gradient.reshape(BLOCK_TOKENS, QUERY_HEADS * HEAD_WIDTH)))
    start_token = (jnp.zeros((SEQUENCE_LENGTH, KEY_VALUE_HEADS, HEAD_WIDTH), jnp.float32), jnp.zeros((SEQUENCE_LENGTH, KEY_VALUE_HEADS, HEAD_WIDTH), jnp.float32))
    (key_gradient_total, value_gradient_total), (attended, query_gradient) = lax.scan(step, start_token, jnp.arange(NBLK, dtype=jnp.int32))
    return (attended.reshape(SEQUENCE_LENGTH, QUERY_HEADS * HEAD_WIDTH), query_gradient.reshape(SEQUENCE_LENGTH, QUERY_HEADS * HEAD_WIDTH), key_gradient_total.reshape(SEQUENCE_LENGTH, KEY_VALUE_HEADS * HEAD_WIDTH), value_gradient_total.reshape(SEQUENCE_LENGTH, KEY_VALUE_HEADS * HEAD_WIDTH))
```

```python
import math
import jax
import jax.numpy as jnp
from jax import lax
from jax.sharding import Mesh, PartitionSpec as P
from jax.experimental import pallas as pl
from jax.experimental.pallas import tpu as pltpu

W = 128
T = 256
BLK = 1024
NK = 3 * BLK
CH = 512
SCALE = 1.0 / math.sqrt(W)
LOG2E = math.log2(math.e)
LN2 = math.log(2.0)
BF = jnp.bfloat16
F32 = jnp.float32

def split(x):
    hi = x.astype(BF)
    return hi, (x - hi.astype(F32)).astype(BF)

def nn(a, b):
    return lax.dot_general(a, b, (((1,), (0,)), ((), ())), preferred_element_type=F32)

def nt(a, b):
    return lax.dot_general(a, b, (((1,), (1,)), ((), ())), preferred_element_type=F32)

def attn_kernel(info, q_ref, do_ref, kvs_ref, kvo_ref, o_ref, dq_ref, dkvs_ref, dkvo_ref,
                kc, vc, kt, vt, s_sc, phi, plo, oacc, oacc2):
    g = pl.program_id(0)
    qh = pl.program_id(1)
    kcol = pl.ds(pl.multiple_of(g * W, W), W)
    vcol = pl.ds(pl.multiple_of(2 * W + g * W, W), W)
    pieces = [(kvs_ref, (z, j), j * BLK + z * T) for j in range(2) for z in range(4)]
    pieces += [(kvo_ref, (z,), 2 * BLK + z * T) for z in range(4)]

    @pl.when(qh == 0)
    def _():
        for ref, idx, row in pieces:
            for col, cat, tr in ((kcol, kc, kt), (vcol, vc, vt)):
                x = ref[idx + (slice(None), col)]
                hi, lo = split(x)
                cat[row:row + T, 0:W] = hi
                cat[row:row + T, W:2 * W] = lo
                hit, lot = split(x.T)
                tr[0:W, row:row + T] = hit
                tr[W:2 * W, row:row + T] = lot

    qs = q_ref[...] * (SCALE * LOG2E)
    qhi, qlo = split(qs)
    qcat = jnp.concatenate([qhi, qhi, qlo, qlo], axis=1)

    def scores(c):
        k = kc[pl.ds(pl.multiple_of(c * CH, CH), CH), :]
        return nt(jnp.concatenate([k, k], axis=1), qcat)

    per = BLK // CH
    def sel_chunk(c, m):
        ok = info[2 + c // per] > 0
        s = jnp.where(ok, scores(c), -jnp.inf)
        s_sc[pl.ds(pl.multiple_of(c * CH, CH), CH), :] = s
        return jnp.maximum(m, jnp.max(s, axis=0, keepdims=True))

    def own_chunk(c, m):
        off = info[1] * T - (c - 2 * per) * CH
        d = lax.broadcasted_iota(jnp.int32, (CH, T), 0) - lax.broadcasted_iota(jnp.int32, (CH, T), 1)
        s = jnp.where(d <= off, scores(c), -jnp.inf)
        s_sc[pl.ds(pl.multiple_of(c * CH, CH), CH), :] = s
        return jnp.maximum(m, jnp.max(s, axis=0, keepdims=True))

    m = jnp.full((1, T), -jnp.inf, F32)
    m = lax.fori_loop(0, 2 * per, sel_chunk, m)
    m = lax.fori_loop(2 * per, 3 * per, own_chunk, m)

    oacc[...] = jnp.zeros_like(oacc)
    oacc2[...] = jnp.zeros_like(oacc2)

    def out_chunk(c, l):
        rows = pl.ds(pl.multiple_of(c * CH, CH), CH)
        p = jnp.exp2(s_sc[rows, :] - m)
        s_sc[rows, :] = p
        hi, lo = split(p)
        phi[rows, :] = hi
        plo[rows, :] = lo
        v = vt[:, rows]
        oacc[...] += nn(v, hi)
        oacc2[...] += nn(v[0:W], lo)
        return l + jnp.sum(p, axis=0, keepdims=True)

    l = lax.fori_loop(0, NK // CH, out_chunk, jnp.zeros((1, T), F32))
    inv = 1.0 / l
    ot = (oacc[0:W, :] + oacc[W:2 * W, :] + oacc2[...]) * inv
    o_ref[...] = ot.T
    dot = do_ref[...].T * inv
    rd = jnp.sum(dot * ot, axis=0, keepdims=True)
    dhi, dlo = split(dot.T)
    dcat = jnp.concatenate([dhi, dhi, dlo, dlo], axis=1)
    dc = jnp.concatenate([dhi, dlo], axis=1)
    dc2 = jnp.concatenate([dc, dc], axis=0)
    qc = jnp.concatenate([qhi, qlo], axis=1)
    qc2 = jnp.concatenate([qc, qc], axis=0)
    oacc[...] = jnp.zeros_like(oacc)
    oacc2[...] = jnp.zeros_like(oacc2)

    def grad_chunk(blk, sub):
        start = blk * BLK + sub * CH
        rows = pl.ds(pl.multiple_of(start, CH), CH)
        v = vc[rows, :]
        dp = nt(jnp.concatenate([v, v], axis=1), dcat)
        ds = s_sc[rows, :] * (dp - rd)
        hi, lo = split(ds)
        k = kt[:, rows]
        oacc[...] += nn(k, hi)
        oacc2[...] += nn(k[0:W], lo)
        dv = nn(jnp.concatenate([phi[rows, :], plo[rows, :]], axis=1), dc2)
        dk = nn(jnp.concatenate([hi, lo], axis=1), qc2)
        dv = dv[:, 0:W] + dv[:, W:2 * W]
        dk = (dk[:, 0:W] + dk[:, W:2 * W]) * LN2
        for u in range(CH // T):
            z = sub * (CH // T) + u
            piece = slice(u * T, (u + 1) * T)
            ref, idx = (dkvs_ref, (z, blk)) if blk < 2 else (dkvo_ref, (z,))
            for col, d in ((kcol, dk), (vcol, dv)):
                at = idx + (slice(None), col)

                @pl.when(qh == 0)
                def _(ref=ref, at=at, d=d, piece=piece):
                    ref[at] = d[piece]

                @pl.when(qh > 0)
                def _(ref=ref, at=at, d=d, piece=piece):
                    ref[at] += d[piece]

    for blk in range(3):
        @pl.loop(0, per)
        def _(sub, blk=blk):
            grad_chunk(blk, sub)
    dq_ref[...] = (oacc[0:W, :] + oacc[W:2 * W, :] + oacc2[...]).T * SCALE


def attention(info, q, do, kvs, kvo):
    heads = pl.BlockSpec((T, W), lambda g, h, *_: (0, g * 4 + h))
    whole = lambda a: pl.BlockSpec(a.shape, lambda g, h, *_: (0,) * a.ndim)
    return pl.pallas_call(
        attn_kernel,
        out_shape=(
            jax.ShapeDtypeStruct(q.shape, F32),
            jax.ShapeDtypeStruct(q.shape, F32),
            jax.ShapeDtypeStruct(kvs.shape, F32),
            jax.ShapeDtypeStruct(kvo.shape, F32),
        ),
        grid_spec=pltpu.PrefetchScalarGridSpec(
            num_scalar_prefetch=1,
            grid=(2, 4),
            in_specs=[heads, heads, whole(kvs), whole(kvo)],
            out_specs=(heads, heads, whole(kvs), whole(kvo)),
            scratch_shapes=[
                pltpu.VMEM((NK, 2 * W), BF),
                pltpu.VMEM((NK, 2 * W), BF),
                pltpu.VMEM((2 * W, NK), BF),
                pltpu.VMEM((2 * W, NK), BF),
                pltpu.VMEM((NK, T), F32),
                pltpu.VMEM((NK, T), BF),
                pltpu.VMEM((NK, T), BF),
                pltpu.VMEM((2 * W, T), F32),
                pltpu.VMEM((W, T), F32),
            ],
        ),
        compiler_params=pltpu.CompilerParams(
            dimension_semantics=("arbitrary", "arbitrary"), vmem_limit_bytes=60 << 20),
        cost_estimate=pl.CostEstimate(flops=5 * 2 * 2048 * NK * W * 3, transcendentals=2048 * NK, bytes_accessed=20 << 20),
    )(info, q, do, kvs, kvo)


GRID = ("y", "x")


def shards(queries, keys, values, cotangent, selected):
    core = lax.axis_index("head")
    block = lax.axis_index("y") * 4 + lax.axis_index("x")
    chosen = lax.dynamic_slice_in_dim(selected, block, 1, 0)[0, 1:]
    info = jnp.concatenate(
        [jnp.stack([block, lax.axis_index("z")]), (chosen >= 0).astype(jnp.int32)]
    )
    chosen = jnp.maximum(chosen, 0)
    swap = [(0, 1), (1, 0)]

    def columns(h):
        return jnp.concatenate(
            [lax.dynamic_slice_in_dim(a, h * 2 * W, 2 * W, 1) for a in (keys, values)], 1
        )

    mine, theirs = columns(core), lax.ppermute(columns(1 - core), "head", swap)
    kv = jnp.where(
        core == 0, jnp.concatenate([mine, theirs], 0), jnp.concatenate([theirs, mine], 0)
    )
    own = lax.all_gather(kv, "z", axis=0)
    every = lax.all_gather(kv, GRID, axis=0)
    quarter = jnp.stack(
        [lax.dynamic_index_in_dim(every, chosen[j], 0, keepdims=False) for j in range(2)]
    )
    picked = lax.all_gather(quarter, "z", axis=0)
    attended, grad_queries, grad_picked, grad_own = attention(
        info, queries, cotangent, picked, own
    )
    grad_picked = lax.psum_scatter(grad_picked, "z", scatter_dimension=0)
    grad_own = lax.psum_scatter(grad_own, "z", scatter_dimension=0)
    at = jnp.arange(16, dtype=jnp.int32)[:, None, None]
    spread = sum(jnp.where(at == chosen[j], grad_picked[j][None], 0.0) for j in range(2))
    grad_kv = lax.psum_scatter(spread, GRID, scatter_dimension=0) + grad_own
    half = T // 2
    keep = lax.dynamic_slice_in_dim(grad_kv, core * half, half, 0)
    back = lax.ppermute(
        lax.dynamic_slice_in_dim(grad_kv, (1 - core) * half, half, 0), "head", swap
    )

    def joined(cols):
        a, b = keep[:, cols], back[:, cols]
        return jnp.where(core == 0, jnp.concatenate([a, b], 1), jnp.concatenate([b, a], 1))

    return attended, grad_queries, joined(slice(0, 2 * W)), joined(slice(2 * W, 4 * W))


def solution(mesh):
    grid = Mesh(mesh.devices.reshape(4, 4, 4, 2), ("y", "x", "z", "head"))
    tokens = ("y", "x", "z")
    wide, narrow = P(tokens, "head"), P(tokens + ("head",), None)
    return jax.shard_map(
        shards,
        mesh=grid,
        in_specs=(wide, narrow, narrow, wide, P()),
        out_specs=(wide, wide, narrow, narrow),
        check_vma=False,
    )
```

```python
import math

import jax
import jax.numpy as jnp
from jax import lax
from jax.experimental import pallas as pl
from jax.experimental.pallas import tpu as pltpu
from jax.sharding import Mesh, PartitionSpec as P

W = 128
T = 256
SEL = 8 * T
NK = 12 * T
CH = 512
SCALE = 1.0 / math.sqrt(W)
LOG2E = math.log2(math.e)
LN2 = math.log(2.0)
BF = jnp.bfloat16
F32 = jnp.float32


def split(x):
    hi = x.astype(BF)
    return hi, (x - hi.astype(F32)).astype(BF)


def nn(a, b):
    return lax.dot_general(a, b, (((1,), (0,)), ((), ())), preferred_element_type=F32)


def nt(a, b):
    return lax.dot_general(a, b, (((1,), (1,)), ((), ())), preferred_element_type=F32)


def attn_kernel(info, ql_ref, qr_ref, dl_ref, dr_ref, s0, s1, s2, s3, own_ref,
                ol_ref, or_ref, gl_ref, gr_ref, g0, g1, g2, g3, h0, h1, h2, h3,
                kc, vc, kt, vt, s_sc, phi, plo, oacc, oacc2, dk_acc, dv_acc):
    u = pl.program_id(0)
    qh = pl.program_id(1)
    z = info[0]
    head = info[1]
    quarter = jnp.where(u == 0, z, 3 - z)

    @pl.when((u == 0) & (qh == 0))
    def _():
        pieces = []
        for j in range(2):
            for x, ref in enumerate((s0, s1, s2, s3)):
                pieces.append((ref.at[0, j], ref.at[1, j], (j * 4 + x) * T))
        for c in range(4):
            cols = [pl.ds(pl.multiple_of(k + head * W, W), W) for k in (0, 2 * W)]
            pieces.append((own_ref.at[c, :, cols[0]], own_ref.at[c, :, cols[1]], SEL + c * T))
        for kref, vref, row in pieces:
            for ref, cat, tr in ((kref, kc, kt), (vref, vc, vt)):
                x = ref[...]
                hi, lo = split(x)
                cat[row:row + T, 0:W] = hi
                cat[row:row + T, W:2 * W] = lo
                hit, lot = split(x.T)
                tr[0:W, row:row + T] = hit
                tr[W:2 * W, row:row + T] = lot
        dk_acc[...] = jnp.zeros_like(dk_acc)
        dv_acc[...] = jnp.zeros_like(dv_acc)

    q = jnp.where(u == 0, ql_ref[...], qr_ref[...])
    do = jnp.where(u == 0, dl_ref[...], dr_ref[...])
    qhi, qlo = split(q * (SCALE * LOG2E))
    qcat = jnp.concatenate([qhi, qhi, qlo, qlo], axis=1)

    def sel_rows(c):
        return pl.ds(pl.multiple_of(c * CH, CH), CH)

    def own_rows(c):
        return pl.ds(pl.multiple_of(SEL + c * T, T), T)

    def scores(rows):
        k = kc[rows, :]
        return nt(jnp.concatenate([k, k], axis=1), qcat)

    def sel_scores(c, m):
        rows = sel_rows(c)
        s = jnp.where(info[2 + c // 2] > 0, scores(rows), -jnp.inf)
        s_sc[rows, :] = s
        return jnp.maximum(m, jnp.max(s, axis=0, keepdims=True))

    def own_scores(c, m):
        rows = own_rows(c)
        ahead = lax.broadcasted_iota(jnp.int32, (T, T), 0) - lax.broadcasted_iota(
            jnp.int32, (T, T), 1)
        s = jnp.where(ahead <= (quarter - c) * T, scores(rows), -jnp.inf)
        s_sc[rows, :] = s
        return jnp.maximum(m, jnp.max(s, axis=0, keepdims=True))

    m = jnp.full((1, T), -jnp.inf, F32)
    m = lax.fori_loop(0, SEL // CH, sel_scores, m)
    m = lax.fori_loop(0, quarter + 1, own_scores, m)

    oacc[...] = jnp.zeros_like(oacc)
    oacc2[...] = jnp.zeros_like(oacc2)

    def out(rows, l):
        p = jnp.exp2(s_sc[rows, :] - m)
        s_sc[rows, :] = p
        hi, lo = split(p)
        phi[rows, :] = hi
        plo[rows, :] = lo
        v = vt[:, rows]
        oacc[...] += nn(v, hi)
        oacc2[...] += nn(v[0:W], lo)
        return l + jnp.sum(p, axis=0, keepdims=True)

    l = jnp.zeros((1, T), F32)
    l = lax.fori_loop(0, SEL // CH, lambda c, l: out(sel_rows(c), l), l)
    l = lax.fori_loop(0, quarter + 1, lambda c, l: out(own_rows(c), l), l)
    inv = 1.0 / l
    ot = (oacc[0:W, :] + oacc[W:2 * W, :] + oacc2[...]) * inv
    dot = do.T * inv
    rd = jnp.sum(dot * ot, axis=0, keepdims=True)
    dhi, dlo = split(dot.T)
    dcat = jnp.concatenate([dhi, dhi, dlo, dlo], axis=1)
    dc = jnp.concatenate([dhi, dlo], axis=1)
    dc2 = jnp.concatenate([dc, dc], axis=0)
    qc = jnp.concatenate([qhi, qlo], axis=1)
    qc2 = jnp.concatenate([qc, qc], axis=0)
    oacc[...] = jnp.zeros_like(oacc)
    oacc2[...] = jnp.zeros_like(oacc2)

    def grads(rows):
        v = vc[rows, :]
        dp = nt(jnp.concatenate([v, v], axis=1), dcat)
        ds = s_sc[rows, :] * (dp - rd)
        hi, lo = split(ds)
        k = kt[:, rows]
        oacc[...] += nn(k, hi)
        oacc2[...] += nn(k[0:W], lo)
        dv = nn(jnp.concatenate([phi[rows, :], plo[rows, :]], axis=1), dc2)
        dk = nn(jnp.concatenate([hi, lo], axis=1), qc2)
        dv_acc[rows, :] += dv[:, 0:W] + dv[:, W:2 * W]
        dk_acc[rows, :] += dk[:, 0:W] + dk[:, W:2 * W]

    @pl.loop(0, SEL // CH)
    def _(c):
        grads(sel_rows(c))

    @pl.loop(0, quarter + 1)
    def _(c):
        grads(own_rows(c))

    dq = (oacc[0:W, :] + oacc[W:2 * W, :] + oacc2[...]).T * SCALE
    o = ot.T

    @pl.when(u == 0)
    def _():
        ol_ref[...] = o
        gl_ref[...] = dq

    @pl.when(u == 1)
    def _():
        or_ref[...] = o
        gr_ref[...] = dq

    @pl.when((u == 1) & (qh == 3))
    def _():
        for acc, k, mul in ((dk_acc, 0, LN2), (dv_acc, 1, 1.0)):
            for x, (ref, own) in enumerate(((g0, h0), (g1, h1), (g2, h2), (g3, h3))):
                for j in range(2):
                    row = (j * 4 + x) * T
                    ref[k, j] = acc[row:row + T, :] * mul
                own[k] = acc[own_rows(z ^ x), :] * mul


def attention(info, q, q_far, do, do_far, pieces, own):
    near = pl.BlockSpec((T, W), lambda u, h, i: (0, i[1] * 4 + h))
    far = pl.BlockSpec((T, W), lambda u, h, i: (0, h))
    first = pl.BlockSpec((T, W), lambda u, h, i: (0, jnp.where(u == 0, h, 3)))
    second = pl.BlockSpec((T, W), lambda u, h, i: (0, jnp.where(u == 0, 0, h)))
    whole = lambda shape: pl.BlockSpec(shape, lambda u, h, i: (0,) * len(shape))
    half = jax.ShapeDtypeStruct((T, 4 * W), F32)
    picked = (2, 2, T, W)
    grads = [jax.ShapeDtypeStruct(picked, F32)] * 4 + [jax.ShapeDtypeStruct((2, T, W), F32)] * 4
    return pl.pallas_call(
        attn_kernel,
        out_shape=[half] * 4 + grads,
        grid_spec=pltpu.PrefetchScalarGridSpec(
            num_scalar_prefetch=1,
            grid=(2, 4),
            in_specs=[near, far, near, far] + [whole(picked)] * 4 + [whole(own.shape)],
            out_specs=[first, second, first, second] + [whole(g.shape) for g in grads],
            scratch_shapes=[
                pltpu.VMEM((NK, 2 * W), BF),
                pltpu.VMEM((NK, 2 * W), BF),
                pltpu.VMEM((2 * W, NK), BF),
                pltpu.VMEM((2 * W, NK), BF),
                pltpu.VMEM((NK, T), F32),
                pltpu.VMEM((NK, T), BF),
                pltpu.VMEM((NK, T), BF),
                pltpu.VMEM((2 * W, T), F32),
                pltpu.VMEM((W, T), F32),
                pltpu.VMEM((NK, W), F32),
                pltpu.VMEM((NK, W), F32),
            ],
        ),
        compiler_params=pltpu.CompilerParams(
            dimension_semantics=("arbitrary", "arbitrary"), vmem_limit_bytes=40 << 20),
        cost_estimate=pl.CostEstimate(
            flops=30 * 2048 * NK * W, transcendentals=2048 * NK, bytes_accessed=20 << 20),
    )(info, q, q_far, do, do_far, *pieces, own)


def ring(axis, array):
    return [array] + [
        lax.ppermute(array, axis, [(i, (i + step) % 4) for i in range(4)]) for step in (1, 2, 3)
    ]


def mirror(array, flip):
    return lax.ppermute(array, "z", [(i, i ^ flip) for i in range(4)])


def choose(index, arrays):
    out = arrays[0]
    for i in range(1, len(arrays)):
        out = jnp.where(index == i, arrays[i], out)
    return out


def route(array, first, second, rows, columns):
    along = ring(first, array)
    here, there = lax.axis_index(first), lax.axis_index(second)

    def to(step):
        target = (there + step) % 4
        return jnp.stack(
            [choose((here - rows[target, j]) % 4, along) for j in range(2)]
        )

    arrived = [to(0)] + [
        lax.ppermute(to(step), second, [(i, (i + step) % 4) for i in range(4)])
        for step in (1, 2, 3)
    ]
    return [choose((there - columns[there, j]) % 4, [a[j] for a in arrived]) for j in range(2)]


def unroute(array, first, second, rows, columns):
    here, there = lax.axis_index(first), lax.axis_index(second)
    arrived = ring(second, array)
    parts = []
    for off in range(4):
        total = 0.0
        for step in range(4):
            source = (there - step) % 4
            for j in range(2):
                hit = (columns[source, j] == there) & ((here - rows[source, j]) % 4 == off)
                total = total + jnp.where(hit, arrived[step][j], 0.0)
        parts.append(total)
    out = parts[0]
    for off in range(1, 4):
        out = out + lax.ppermute(parts[off], first, [(i, (i - off) % 4) for i in range(4)])
    return out


def shards(queries, keys, values, cotangent, selected):
    core, z = lax.axis_index("head"), lax.axis_index("z")
    y, x = lax.axis_index("y"), lax.axis_index("x")
    head = z // 2
    table = selected[:, 1:]
    mine = lax.dynamic_index_in_dim(table, y * 4 + x, 0, keepdims=False)
    info = jnp.concatenate([jnp.stack([z, head]), (mine >= 0).astype(jnp.int32)])
    table = jnp.maximum(table, 0).reshape(4, 4, 2)
    by_row = lax.dynamic_index_in_dim(table, y, 0, keepdims=False)
    by_column = lax.dynamic_index_in_dim(table, x, 1, keepdims=False)
    swap = [(0, 1), (1, 0)]

    far = 1 - head
    q_far, do_far = (
        mirror(lax.dynamic_slice_in_dim(a, far * 4 * W, 4 * W, 1), 3)
        for a in (queries, cotangent)
    )

    def columns(h):
        return jnp.concatenate(
            [lax.dynamic_slice_in_dim(a, h * 2 * W, 2 * W, 1) for a in (keys, values)], 1
        )

    near, other = columns(core), lax.ppermute(columns(1 - core), "head", swap)
    kv = jnp.where(
        core == 0, jnp.concatenate([near, other], 0), jnp.concatenate([other, near], 0)
    )
    own = lax.all_gather(kv, "z", axis=0)
    k, v = (jnp.stack([kv[:, a:a + W], kv[:, a + W:a + 2 * W]]) for a in (0, 2 * W))
    k_args = ("y", "x", by_row // 4, by_row % 4)
    v_args = ("x", "y", by_column % 4, by_column // 4)
    got_k = route(k, *k_args)
    got_v = route(v, *v_args)

    def picked(h):
        return jnp.stack(
            [jnp.stack([lax.dynamic_index_in_dim(a, h, 0, keepdims=False) for a in got])
             for got in (got_k, got_v)]
        )

    same, cross = picked(head), picked(far)
    p1 = mirror(same, 1)
    p3 = mirror(cross, 3)
    p2 = mirror(p3, 1)
    out = attention(info, queries, q_far, cotangent, do_far, (same, p1, p2, p3), own)
    o_near, o_far, dq_near, dq_far = out[:4]
    o_far, dq_far = mirror(o_far, 3), mirror(dq_far, 3)

    def sides(a, b):
        return jnp.where(head == 0, jnp.concatenate([a, b], 1), jnp.concatenate([b, a], 1))

    def reduced(g):
        passed = mirror(g[3] + mirror(g[2], 1), 3)
        kept = g[0] + mirror(g[1], 1)
        return kept, passed

    def heads(kept, passed):
        return jnp.where(head == 0, jnp.stack([kept, passed]), jnp.stack([passed, kept]))

    kept, passed = reduced(out[4:8])
    grad_k = unroute(jnp.stack([heads(kept[0, j], passed[0, j]) for j in range(2)]), *k_args)
    grad_v = unroute(jnp.stack([heads(kept[1, j], passed[1, j]) for j in range(2)]), *v_args)
    kept, passed = reduced(out[8:12])
    grad_k = grad_k + heads(kept[0], passed[0])
    grad_v = grad_v + heads(kept[1], passed[1])
    grad_kv = jnp.concatenate([grad_k[0], grad_k[1], grad_v[0], grad_v[1]], 1)
    half = T // 2
    keep = lax.dynamic_slice_in_dim(grad_kv, core * half, half, 0)
    back = lax.ppermute(
        lax.dynamic_slice_in_dim(grad_kv, (1 - core) * half, half, 0), "head", swap
    )

    def joined(cols):
        a, b = keep[:, cols], back[:, cols]
        return jnp.where(core == 0, jnp.concatenate([a, b], 1), jnp.concatenate([b, a], 1))

    return (
        sides(o_near, o_far),
        sides(dq_near, dq_far),
        joined(slice(0, 2 * W)),
        joined(slice(2 * W, 4 * W)),
    )


def solution(mesh):
    grid = Mesh(mesh.devices.reshape(4, 4, 4, 2), ("y", "x", "z", "head"))
    tokens = ("y", "x", "z")
    wide, narrow = P(tokens, "head"), P(tokens + ("head",), None)
    return jax.shard_map(
        shards,
        mesh=grid,
        in_specs=(wide, narrow, narrow, wide, P()),
        out_specs=(wide, wide, narrow, narrow),
        check_vma=False,
    )
```

```python
import math

import jax
import jax.numpy as jnp
from jax import lax
from jax.experimental import pallas as pl
from jax.experimental.pallas import tpu as pltpu
from jax.sharding import Mesh, PartitionSpec as P

W = 128
T = 256

SCALE = 1.0 / math.sqrt(W)
LOG2E = math.log2(math.e)
LN2 = math.log(2.0)
BF = jnp.bfloat16
F32 = jnp.float32
BLK = 4 * T
HP = 2
STEPS = 4 // HP
R = HP * T

def split(x):
    hi = x.astype(BF)
    return hi, (x - hi.astype(F32)).astype(BF)

def twice(x, axis):
    return jnp.concatenate([x, x], axis=axis)

def mm(a, b):
    return lax.dot_general(a, b, (((1,), (0,)), ((), ())), preferred_element_type=F32)

def turned(x):
    return jnp.concatenate([x[:, i * W:(i + 1) * W].T for i in range(HP)], axis=1)

def upright(x):
    return jnp.concatenate([x[:, i * T:(i + 1) * T].T for i in range(HP)], axis=1)

def stacked(x):
    return jnp.concatenate([x[:, i * W:(i + 1) * W] for i in range(HP)], axis=0)

def left(x):
    hi, lo = split(x)
    return jnp.concatenate([hi, hi, lo, lo], axis=0)

def right(x):
    hi, lo = split(x)
    return twice(jnp.concatenate([hi, lo], axis=1), 0)

def fill(ref, rows, cat, tr):
    x = ref[...]
    hi, lo = split(x)
    if cat is not None:
        cat[rows, 0:W] = hi
        cat[rows, W:2 * W] = lo
    if tr is not None:
        hit, lot = split(x.T)
        tr[0:W, rows] = hit
        tr[W:2 * W, rows] = lot

def values_sum(tr, hi, lo):
    a = mm(tr, hi)
    return a[0:W] + a[W:2 * W] + mm(tr[0:W], lo)

def halves(x):
    return x[:, 0:W] + x[:, W:2 * W]

def own_refs(own_ref, head, c):
    return [own_ref.at[c, i, head] for i in range(2)]

def near_far(u, near, far):
    return jnp.where(u == 0, near[...], far[...])

def own_forward(info, ql_ref, qr_ref, own_ref, p_ref, m_ref, l_ref, ot_ref, kc, vt):
    u = pl.program_id(0)

    @pl.when((u == 0) & (pl.program_id(1) == 0))
    def _():
        for c in range(4):
            k, v = own_refs(own_ref, info[1], c)
            fill(k, slice(c * T, (c + 1) * T), kc, None)
            fill(v, slice(c * T, (c + 1) * T), None, vt)

    quarter = jnp.where(u == 0, info[0], 3 - info[0])
    q = left(turned(near_far(u, ql_ref, qr_ref)) * (SCALE * LOG2E))
    s = mm(twice(kc[...], 1), q)
    token = lax.broadcasted_iota(jnp.int32, (BLK, R), 1) & (T - 1)
    ahead = lax.broadcasted_iota(jnp.int32, (BLK, R), 0) - token
    s = jnp.where(ahead <= quarter * T, s, -jnp.inf)
    m = jnp.max(s, axis=0, keepdims=True)
    p = jnp.exp2(s - m)
    p_ref[0] = p
    m_ref[0] = m
    l_ref[0] = jnp.sum(p, axis=0, keepdims=True)
    hi, lo = split(p)
    ot_ref[0] = values_sum(vt[...], hi, lo)

def picked(info, ql_ref, qr_ref, dl_ref, dr_ref, s00, s01, s02, s03, s10, s11, s12, s13,
           m0_ref, l0_ref, ot0_ref, ol_ref, or_ref, dq_ref, c_ref, rd_ref,
           g00, g01, g02, g03, g10, g11, g12, g13,
           kc, vc, kt, vt, s_sc, phi, plo, dk_acc, dv_acc):
    u, step = pl.program_id(0), pl.program_id(1)
    pieces = ((s00, s01, s02, s03), (s10, s11, s12, s13))

    @pl.when((u == 0) & (step == 0))
    def _():
        for j in range(2):
            for x in range(4):
                rows = slice((j * 4 + x) * T, (j * 4 + x + 1) * T)
                fill(pieces[j][x].at[0], rows, kc, kt)
                fill(pieces[j][x].at[1], rows, vc, vt)
        dk_acc[...] = jnp.zeros_like(dk_acc)
        dv_acc[...] = jnp.zeros_like(dv_acc)

    q = near_far(u, ql_ref, qr_ref) * (SCALE * LOG2E)
    do = near_far(u, dl_ref, dr_ref)
    qt = left(turned(q))
    m0 = m0_ref[0]
    m = m0
    for j in range(2):
        rows = slice(j * BLK, (j + 1) * BLK)
        s = mm(twice(kc[rows, :], 1), qt)
        s = jnp.where(info[2 + j] > 0, s, -jnp.inf)
        s_sc[rows, :] = s
        m = jnp.maximum(m, jnp.max(s, axis=0, keepdims=True))
    shrink = jnp.exp2(m0 - m)
    l = l0_ref[0] * shrink
    ot = ot0_ref[0] * shrink
    for j in range(2):
        rows = slice(j * BLK, (j + 1) * BLK)
        p = jnp.exp2(s_sc[rows, :] - m)
        s_sc[rows, :] = p
        hi, lo = split(p)
        phi[rows, :] = hi
        plo[rows, :] = lo
        l = l + jnp.sum(p, axis=0, keepdims=True)
        ot = ot + values_sum(vt[:, rows], hi, lo)
    inv = 1.0 / l
    ot = ot * inv
    dot = turned(do) * inv
    rd = jnp.sum(dot * ot, axis=0, keepdims=True)
    c_ref[0] = inv * shrink
    rd_ref[0] = rd * shrink
    o = upright(ot)

    @pl.when(u == 0)
    def _():
        ol_ref[...] = o

    @pl.when(u == 1)
    def _():
        or_ref[...] = o

    dt = left(dot)
    d2 = right(stacked(upright(dot)))
    q2 = right(stacked(q))
    dq = jnp.zeros((W, R), F32)
    for j in range(2):
        rows = slice(j * BLK, (j + 1) * BLK)
        dp = mm(twice(vc[rows, :], 1), dt)
        hi, lo = split(s_sc[rows, :] * (dp - rd))
        dq = dq + values_sum(kt[:, rows], hi, lo)
        dv_acc[rows, :] += halves(mm(jnp.concatenate([phi[rows, :], plo[rows, :]], axis=1), d2))
        dk_acc[rows, :] += halves(mm(jnp.concatenate([hi, lo], axis=1), q2))
    dq_ref[0] = dq

    @pl.when((u == 1) & (step == STEPS - 1))
    def _():
        for j, out in enumerate(((g00, g01, g02, g03), (g10, g11, g12, g13))):
            for x in range(4):
                rows = slice((j * 4 + x) * T, (j * 4 + x + 1) * T)
                out[x][0] = dk_acc[rows, :] * LN2
                out[x][1] = dv_acc[rows, :]

def own_backward(info, ql_ref, qr_ref, dl_ref, dr_ref, own_ref, p_ref, c_ref, rd_ref, dq_ref,
                 gl_ref, gr_ref, h0, h1, h2, h3, vc, kt, dk_acc, dv_acc):
    u, step = pl.program_id(0), pl.program_id(1)

    @pl.when((u == 0) & (step == 0))
    def _():
        for c in range(4):
            k, v = own_refs(own_ref, info[1], c)
            fill(k, slice(c * T, (c + 1) * T), None, kt)
            fill(v, slice(c * T, (c + 1) * T), vc, None)
        dk_acc[...] = jnp.zeros_like(dk_acc)
        dv_acc[...] = jnp.zeros_like(dv_acc)

    q = near_far(u, ql_ref, qr_ref) * (SCALE * LOG2E)
    dot = turned(near_far(u, dl_ref, dr_ref)) * c_ref[0]
    p = p_ref[0]
    hi, lo = split(p)
    dv_acc[...] += halves(mm(jnp.concatenate([hi, lo], axis=1), right(stacked(upright(dot)))))
    dp = mm(twice(vc[...], 1), left(dot))
    hi, lo = split(p * (dp - rd_ref[0]))
    dk_acc[...] += halves(mm(jnp.concatenate([hi, lo], axis=1), right(stacked(q))))
    dq = upright(dq_ref[0] + values_sum(kt[...], hi, lo)) * SCALE

    @pl.when(u == 0)
    def _():
        gl_ref[...] = dq

    @pl.when(u == 1)
    def _():
        gr_ref[...] = dq

    @pl.when((u == 1) & (step == STEPS - 1))
    def _():
        for x, out in enumerate((h0, h1, h2, h3)):
            rows = pl.ds(pl.multiple_of((info[0] ^ x) * T, T), T)
            out[0] = dk_acc[rows, :] * LN2
            out[1] = dv_acc[rows, :]

def tile(shape):
    return pl.BlockSpec((1,) + shape[1:], lambda u, h, i: (u * STEPS + h, 0, 0))

def whole(shape):
    return pl.BlockSpec(shape, lambda u, h, i: (0,) * len(shape))

NEAR = pl.BlockSpec((T, HP * W), lambda u, h, i: (0, i[1] * STEPS + h))
FAR = pl.BlockSpec((T, HP * W), lambda u, h, i: (0, h))
FIRST = pl.BlockSpec((T, HP * W), lambda u, h, i: (0, jnp.where(u == 0, h, STEPS - 1)))
SECOND = pl.BlockSpec((T, HP * W), lambda u, h, i: (0, jnp.where(u == 0, 0, h)))
PROBS, ROW, TURNED = (2 * STEPS, BLK, R), (2 * STEPS, 1, R), (2 * STEPS, W, R)
HALF, PIECE = (T, 4 * W), (2, T, W)

def kernel(body, ins, outs, out_shapes, scratch, flops, limit):
    return pl.pallas_call(
        body,
        out_shape=[jax.ShapeDtypeStruct(s, F32) for s in out_shapes],
        grid_spec=pltpu.PrefetchScalarGridSpec(
            num_scalar_prefetch=1,
            grid=(2, STEPS),
            in_specs=ins,
            out_specs=outs,
            scratch_shapes=[pltpu.VMEM(s, d) for s, d in scratch],
        ),
        compiler_params=pltpu.CompilerParams(
            dimension_semantics=("arbitrary", "arbitrary"), vmem_limit_bytes=limit << 20),
        cost_estimate=pl.CostEstimate(
            flops=flops, transcendentals=0, bytes_accessed=16 << 20),
        name=body.__name__,
    )

UNIT = 2 * 2048 * BLK * W * 4

def call_own_forward(info, q, q_far, own):
    return kernel(
        own_forward,
        [NEAR, FAR, whole(own.shape)],
        [tile(PROBS), tile(ROW), tile(ROW), tile(TURNED)],
        [PROBS, ROW, ROW, TURNED],
        [((BLK, 2 * W), BF), ((2 * W, BLK), BF)],
        2 * UNIT, 30,
    )(info, q, q_far, own)

def call_picked(info, q, q_far, do, do_far, pieces, m, l, ot):
    return kernel(
        picked,
        [NEAR, FAR, NEAR, FAR] + [whole(PIECE)] * 8 + [tile(ROW), tile(ROW), tile(TURNED)],
        [FIRST, SECOND, tile(TURNED), tile(ROW), tile(ROW)] + [whole(PIECE)] * 8,
        [HALF, HALF, TURNED, ROW, ROW] + [PIECE] * 8,
        [((2 * BLK, 2 * W), BF), ((2 * BLK, 2 * W), BF), ((2 * W, 2 * BLK), BF), ((2 * W, 2 * BLK), BF),
         ((2 * BLK, R), F32), ((2 * BLK, R), BF), ((2 * BLK, R), BF),
         ((2 * BLK, W), F32), ((2 * BLK, W), F32)],
        10 * UNIT, 52,
    )(info, q, q_far, do, do_far, *pieces, m, l, ot)

def call_own_backward(info, q, q_far, do, do_far, own, p, c, rd, dq):
    return kernel(
        own_backward,
        [NEAR, FAR, NEAR, FAR, whole(own.shape), tile(PROBS), tile(ROW), tile(ROW), tile(TURNED)],
        [FIRST, SECOND] + [whole(PIECE)] * 4,
        [HALF, HALF] + [PIECE] * 4,
        [((BLK, 2 * W), BF), ((2 * W, BLK), BF), ((BLK, W), F32), ((BLK, W), F32)],
        3 * UNIT, 40,
    )(info, q, q_far, do, do_far, own, p, c, rd, dq)

HEADS = (2, T, W)

def glue(body, args, outs, limit=24):
    return pl.pallas_call(
        body,
        out_shape=[jax.ShapeDtypeStruct(s, F32) for s in outs],
        in_specs=[pl.BlockSpec(memory_space=pltpu.SMEM)]
        + [pl.BlockSpec(memory_space=pltpu.VMEM)] * (len(args) - 1),
        out_specs=[pl.BlockSpec(memory_space=pltpu.VMEM)] * len(outs),
        compiler_params=pltpu.CompilerParams(vmem_limit_bytes=limit << 20),
        cost_estimate=pl.CostEstimate(
            flops=0, transcendentals=0, bytes_accessed=(len(args) + len(outs)) * HEADS[0] * T * W * 4),
        name=body.__name__.strip("_"),
    )(*args)

def shift(array, axis, step):
    if step == 0:
        return array
    return lax.ppermute(array, axis, [(i, (i + step) % 4) for i in range(4)])

def mirror(array, flip):
    return lax.ppermute(array, "z", [(i, i ^ flip) for i in range(4)])

def chosen(table, y, x, j):
    block = jnp.maximum(table[y * 4 + x, 1 + j], 0)
    return block // 4, block % 4

def assemble(spot, keys, values, other_keys, other_values, k_ref, v_ref, kv_ref):
    core = spot[0]
    for h in range(2):
        cols = pl.ds(pl.multiple_of((core * 2 + h) * W, W), W)
        for i, (mine, other, out) in enumerate(
                ((keys, other_keys, k_ref), (values, other_values, v_ref))):
            for ref, half in ((mine, core), (other, 1 - core)):
                rows = pl.ds(pl.multiple_of(half * (T // 2), T // 2), T // 2)
                a = ref[:, cols]
                out[h, rows, :] = a
                kv_ref[i, h, rows, :] = a

def pick(j, table, *refs):
    y, x = lax.axis_index("y"), lax.axis_index("x")
    k_in, v_in, k_out, v_out = (refs[i:i + 4] for i in range(0, 16, 4))
    for step in range(4):
        row, _ = chosen(table, y, (x + step) % 4, j)
        _, column = chosen(table, (y + step) % 4, x, j)
        for off, arrays, out in (((y - row) % 4, k_in, k_out), ((x - column) % 4, v_in, v_out)):
            for i in range(4):
                @pl.when(off == i)
                def _(source=arrays[i], out=out[step]):
                    out[...] = source[...]

def pick0(*refs):
    pick(0, *refs)

def pick1(*refs):
    pick(1, *refs)

def join(j, table, *refs):
    y, x = lax.axis_index("y"), lax.axis_index("x")
    head = lax.axis_index("z") // 2
    row, column = chosen(table, y, x, j)
    k_in, v_in, (same, cross) = refs[0:4], refs[4:8], refs[8:10]
    for i in range(4):
        for n, off, source in ((0, (x - column) % 4, k_in[i]), (1, (y - row) % 4, v_in[i])):
            @pl.when(off == i)
            def _(n=n, source=source):
                same[n] = source[head]
                cross[n] = source[1 - head]

def join0(*refs):
    join(0, *refs)

def join1(*refs):
    join(1, *refs)

def spread(spot, kept, added, passed, k_out, v_out):
    head = spot[1]
    for n, out in ((0, k_out), (1, v_out)):
        out[head] = kept[n] + added[n]
        out[1 - head] = passed[n]

def collect(j, table, *refs):
    y, x = lax.axis_index("y"), lax.axis_index("x")
    if j == 0:
        k_in, v_in, k_out, v_out = (refs[i:i + 4] for i in range(0, 16, 4))
        for ref in k_out + v_out:
            ref[...] = jnp.zeros_like(ref)
    else:
        k_in, v_in, k_old, v_old, k_out, v_out = (refs[i:i + 4] for i in range(0, 24, 4))
        for ref, old in zip(k_out + v_out, k_old + v_old):
            ref[...] = old[...]
    for step in range(4):
        row, column = chosen(table, y, (x - step) % 4, j)
        row2, column2 = chosen(table, (y - step) % 4, x, j)
        for hit, off, source, out in (
                (column == x, (y - row) % 4, k_in[step], k_out),
                (row2 == y, (x - column2) % 4, v_in[step], v_out)):
            for i in range(4):
                @pl.when(hit & (off == i))
                def _(source=source, ref=out[i]):
                    ref[...] += source[...]

def collect0(*refs):
    collect(0, *refs)

def collect1(*refs):
    collect(1, *refs)

def shards(queries, keys, values, cotangent, selected):
    core, z = lax.axis_index("head"), lax.axis_index("z")
    y, x = lax.axis_index("y"), lax.axis_index("x")
    head = z // 2
    mine = lax.dynamic_slice(selected, (y * 4 + x, 1), (1, 2))[0]
    info = jnp.concatenate([jnp.stack([z, head]), (mine >= 0).astype(jnp.int32)])
    spot = jnp.stack([core, head])
    swap = [(0, 1), (1, 0)]

    far = 1 - head
    q_far, do_far = (
        mirror(lax.dynamic_slice_in_dim(a, far * 4 * W, 4 * W, 1), 3)
        for a in (queries, cotangent)
    )
    other = [lax.ppermute(a, "head", swap) for a in (keys, values)]
    k, v, kv = glue(assemble, (spot, keys, values, *other), (HEADS, HEADS, (2,) + HEADS))
    own = lax.all_gather(kv, "z", axis=0)

    k_along = [shift(k, "y", s) for s in range(4)]
    v_along = [shift(v, "x", s) for s in range(4)]
    pieces = []
    for pick_j, join_j in ((pick0, join0), (pick1, join1)):
        sent = glue(pick_j, (selected, *k_along, *v_along), (HEADS,) * 8)
        k_got = [shift(sent[s], "x", s) for s in range(4)]
        v_got = [shift(sent[4 + s], "y", s) for s in range(4)]
        same, cross = glue(join_j, (selected, *k_got, *v_got), (HEADS, HEADS))
        p1 = mirror(same, 1)
        p3 = mirror(cross, 3)
        pieces += [same, p1, mirror(p3, 1), p3]

    p, m, l, ot = call_own_forward(info, queries, q_far, own)
    out = call_picked(info, queries, q_far, cotangent, do_far, pieces, m, l, ot)
    o_near, o_far, dq, c, rd = out[:5]
    last = call_own_backward(info, queries, q_far, cotangent, do_far, own, p, c, rd, dq)

    def reduced(g):
        passed = mirror(g[3] + mirror(g[2], 1), 3)
        return glue(spread, (spot, g[0], mirror(g[1], 1), passed), (HEADS, HEADS))

    sums = ()
    for j, collect_j in enumerate((collect0, collect1)):
        k_part, v_part = reduced(out[5 + 4 * j:9 + 4 * j])
        arrived = [shift(k_part, "x", s) for s in range(4)]
        arrived += [shift(v_part, "y", s) for s in range(4)]
        sums = glue(collect_j, (selected, *arrived, *sums), (HEADS,) * 8)
    own_k, own_v = reduced(last[2:6])
    grad_k = own_k + sum(shift(sums[s], "y", (4 - s) % 4) for s in range(4))
    grad_v = own_v + sum(shift(sums[4 + s], "x", (4 - s) % 4) for s in range(4))

    half = T // 2

    def home(a):
        keep = lax.dynamic_slice_in_dim(a, core * half, half, 1)
        back = lax.ppermute(lax.dynamic_slice_in_dim(a, (1 - core) * half, half, 1), "head", swap)
        low, high = jnp.where(core == 0, keep, back), jnp.where(core == 0, back, keep)
        return jnp.concatenate([low[0], low[1], high[0], high[1]], 1)

    def sides(a, b):
        return jnp.where(head == 0, jnp.concatenate([a, b], 1), jnp.concatenate([b, a], 1))

    return (
        sides(o_near, mirror(o_far, 3)),
        sides(last[0], mirror(last[1], 3)),
        home(grad_k),
        home(grad_v),
    )

def solution(mesh):
    grid = Mesh(mesh.devices.reshape(4, 4, 4, 2), ("y", "x", "z", "head"))
    tokens = ("y", "x", "z")
    wide, narrow = P(tokens, "head"), P(tokens + ("head",), None)
    return jax.shard_map(
        shards,
        mesh=grid,
        in_specs=(wide, narrow, narrow, wide, P()),
        out_specs=(wide, wide, narrow, narrow),
        check_vma=False,
    )
```

```python
import math

import jax
import jax.numpy as jnp
from jax import lax
from jax.experimental import pallas as pl
from jax.experimental.pallas import tpu as pltpu
from jax.sharding import Mesh, PartitionSpec as P

W = 128
T = 256

SCALE = 1.0 / math.sqrt(W)
LOG2E = math.log2(math.e)
LN2 = math.log(2.0)
BF = jnp.bfloat16
F32 = jnp.float32
BLK = 4 * T
HP = 2
STEPS = 4 // HP
R = HP * T

def split(x):
    hi = x.astype(BF)
    return hi, (x - hi.astype(F32)).astype(BF)

def twice(x, axis):
    return jnp.concatenate([x, x], axis=axis)

def mm(a, b):
    return lax.dot_general(a, b, (((1,), (0,)), ((), ())), preferred_element_type=F32)

def turned(x):
    return jnp.concatenate([x[:, i * W:(i + 1) * W].T for i in range(HP)], axis=1)

def upright(x):
    return jnp.concatenate([x[:, i * T:(i + 1) * T].T for i in range(HP)], axis=1)

def stacked(x):
    return jnp.concatenate([x[:, i * W:(i + 1) * W] for i in range(HP)], axis=0)

def left(x):
    hi, lo = split(x)
    return jnp.concatenate([hi, hi, lo, lo], axis=0)

def right(x):
    hi, lo = split(x)
    return twice(jnp.concatenate([hi, lo], axis=1), 0)

def fill(ref, rows, cat, tr):
    x = ref[...]
    hi, lo = split(x)
    if cat is not None:
        cat[rows, 0:W] = hi
        cat[rows, W:2 * W] = lo
    if tr is not None:
        hit, lot = split(x.T)
        tr[0:W, rows] = hit
        tr[W:2 * W, rows] = lot

def values_sum(tr, hi, lo):
    a = mm(tr, hi)
    return a[0:W] + a[W:2 * W] + mm(tr[0:W], lo)

def halves(x):
    return x[:, 0:W] + x[:, W:2 * W]

def own_refs(own_ref, head, c):
    return [own_ref.at[c, i, head] for i in range(2)]

def near_far(u, near, far):
    return jnp.where(u == 0, near[...], far[...])

def own_forward(info, ql_ref, qr_ref, own_ref, p_ref, m_ref, l_ref, ot_ref, kc, vt):
    u = pl.program_id(0)

    @pl.when((u == 0) & (pl.program_id(1) == 0))
    def _():
        for c in range(4):
            k, v = own_refs(own_ref, info[1], c)
            fill(k, slice(c * T, (c + 1) * T), kc, None)
            fill(v, slice(c * T, (c + 1) * T), None, vt)

    quarter = jnp.where(u == 0, info[0], 3 - info[0])
    q = left(turned(near_far(u, ql_ref, qr_ref)) * (SCALE * LOG2E))
    s = mm(twice(kc[...], 1), q)
    token = lax.broadcasted_iota(jnp.int32, (BLK, R), 1) & (T - 1)
    ahead = lax.broadcasted_iota(jnp.int32, (BLK, R), 0) - token
    s = jnp.where(ahead <= quarter * T, s, -jnp.inf)
    m = jnp.max(s, axis=0, keepdims=True)
    p = jnp.exp2(s - m)
    p_ref[0] = p
    m_ref[0] = m
    l_ref[0] = jnp.sum(p, axis=0, keepdims=True)
    hi, lo = split(p)
    ot_ref[0] = values_sum(vt[...], hi, lo)

def picked(info, ql_ref, qr_ref, dl_ref, dr_ref, s0, s1, s2, s3,
           m0_ref, l0_ref, ot0_ref, ol_ref, or_ref, dq_ref, c_ref, rd_ref, g0, g1, g2, g3,
           kc, vc, kt, vt, s_sc, phi, plo, dk_acc, dv_acc):
    u, step = pl.program_id(0), pl.program_id(1)

    @pl.when((u == 0) & (step == 0))
    def _():
        for j in range(2):
            for x in range(4):
                rows = slice((j * 4 + x) * T, (j * 4 + x + 1) * T)
                piece = (s0, s1, s2, s3)[x]
                fill(piece.at[j, 0], rows, kc, kt)
                fill(piece.at[j, 1], rows, vc, vt)
        dk_acc[...] = jnp.zeros_like(dk_acc)
        dv_acc[...] = jnp.zeros_like(dv_acc)

    q = near_far(u, ql_ref, qr_ref) * (SCALE * LOG2E)
    do = near_far(u, dl_ref, dr_ref)
    qt = left(turned(q))
    m0 = m0_ref[0]
    m = m0
    for j in range(2):
        rows = slice(j * BLK, (j + 1) * BLK)
        s = mm(twice(kc[rows, :], 1), qt)
        s = jnp.where(info[2 + j] > 0, s, -jnp.inf)
        s_sc[rows, :] = s
        m = jnp.maximum(m, jnp.max(s, axis=0, keepdims=True))
    shrink = jnp.exp2(m0 - m)
    l = l0_ref[0] * shrink
    ot = ot0_ref[0] * shrink
    for j in range(2):
        rows = slice(j * BLK, (j + 1) * BLK)
        p = jnp.exp2(s_sc[rows, :] - m)
        s_sc[rows, :] = p
        hi, lo = split(p)
        phi[rows, :] = hi
        plo[rows, :] = lo
        l = l + jnp.sum(p, axis=0, keepdims=True)
        ot = ot + values_sum(vt[:, rows], hi, lo)
    inv = 1.0 / l
    ot = ot * inv
    dot = turned(do) * inv
    rd = jnp.sum(dot * ot, axis=0, keepdims=True)
    c_ref[0] = inv * shrink
    rd_ref[0] = rd * shrink
    o = upright(ot)

    @pl.when(u == 0)
    def _():
        ol_ref[...] = o

    @pl.when(u == 1)
    def _():
        or_ref[...] = o

    dt = left(dot)
    d2 = right(stacked(upright(dot)))
    q2 = right(stacked(q))
    dq = jnp.zeros((W, R), F32)
    for j in range(2):
        rows = slice(j * BLK, (j + 1) * BLK)
        dp = mm(twice(vc[rows, :], 1), dt)
        hi, lo = split(s_sc[rows, :] * (dp - rd))
        dq = dq + values_sum(kt[:, rows], hi, lo)
        dv_acc[rows, :] += halves(mm(jnp.concatenate([phi[rows, :], plo[rows, :]], axis=1), d2))
        dk_acc[rows, :] += halves(mm(jnp.concatenate([hi, lo], axis=1), q2))
    dq_ref[0] = dq

    @pl.when((u == 1) & (step == STEPS - 1))
    def _():
        for j in range(2):
            for x, out in enumerate((g0, g1, g2, g3)):
                rows = slice((j * 4 + x) * T, (j * 4 + x + 1) * T)
                out[j, 0] = dk_acc[rows, :] * LN2
                out[j, 1] = dv_acc[rows, :]

def own_backward(info, ql_ref, qr_ref, dl_ref, dr_ref, own_ref, p_ref, c_ref, rd_ref, dq_ref,
                 gl_ref, gr_ref, h0, h1, h2, h3, vc, kt, dk_acc, dv_acc):
    u, step = pl.program_id(0), pl.program_id(1)

    @pl.when((u == 0) & (step == 0))
    def _():
        for c in range(4):
            k, v = own_refs(own_ref, info[1], c)
            fill(k, slice(c * T, (c + 1) * T), None, kt)
            fill(v, slice(c * T, (c + 1) * T), vc, None)
        dk_acc[...] = jnp.zeros_like(dk_acc)
        dv_acc[...] = jnp.zeros_like(dv_acc)

    q = near_far(u, ql_ref, qr_ref) * (SCALE * LOG2E)
    dot = turned(near_far(u, dl_ref, dr_ref)) * c_ref[0]
    p = p_ref[0]
    hi, lo = split(p)
    dv_acc[...] += halves(mm(jnp.concatenate([hi, lo], axis=1), right(stacked(upright(dot)))))
    dp = mm(twice(vc[...], 1), left(dot))
    hi, lo = split(p * (dp - rd_ref[0]))
    dk_acc[...] += halves(mm(jnp.concatenate([hi, lo], axis=1), right(stacked(q))))
    dq = upright(dq_ref[0] + values_sum(kt[...], hi, lo)) * SCALE

    @pl.when(u == 0)
    def _():
        gl_ref[...] = dq

    @pl.when(u == 1)
    def _():
        gr_ref[...] = dq

    @pl.when((u == 1) & (step == STEPS - 1))
    def _():
        for x, out in enumerate((h0, h1, h2, h3)):
            rows = pl.ds(pl.multiple_of((info[0] ^ x) * T, T), T)
            out[0] = dk_acc[rows, :] * LN2
            out[1] = dv_acc[rows, :]

def tile(shape):
    return pl.BlockSpec((1,) + shape[1:], lambda u, h, i: (u * STEPS + h, 0, 0))

def whole(shape):
    return pl.BlockSpec(shape, lambda u, h, i: (0,) * len(shape))

NEAR = pl.BlockSpec((T, HP * W), lambda u, h, i: (0, i[1] * STEPS + h))
FAR = pl.BlockSpec((T, HP * W), lambda u, h, i: (0, h))
FIRST = pl.BlockSpec((T, HP * W), lambda u, h, i: (0, jnp.where(u == 0, h, STEPS - 1)))
SECOND = pl.BlockSpec((T, HP * W), lambda u, h, i: (0, jnp.where(u == 0, 0, h)))
PROBS, ROW, TURNED = (2 * STEPS, BLK, R), (2 * STEPS, 1, R), (2 * STEPS, W, R)
HALF, PIECE, PAIR = (T, 4 * W), (2, T, W), (2, 2, T, W)

def kernel(body, ins, outs, out_shapes, scratch, flops, limit):
    return pl.pallas_call(
        body,
        out_shape=[pltpu.HBM(s, F32) for s in out_shapes],
        grid_spec=pltpu.PrefetchScalarGridSpec(
            num_scalar_prefetch=1,
            grid=(2, STEPS),
            in_specs=ins,
            out_specs=outs,
            scratch_shapes=[pltpu.VMEM(s, d) for s, d in scratch],
        ),
        compiler_params=pltpu.CompilerParams(
            dimension_semantics=("arbitrary", "arbitrary"), vmem_limit_bytes=limit << 20),
        cost_estimate=pl.CostEstimate(
            flops=flops, transcendentals=0, bytes_accessed=16 << 20),
        name=body.__name__,
    )

UNIT = 2 * 2048 * BLK * W * 4

def call_own_forward(info, q, q_far, own):
    return kernel(
        own_forward,
        [NEAR, FAR, whole(own.shape)],
        [tile(PROBS), tile(ROW), tile(ROW), tile(TURNED)],
        [PROBS, ROW, ROW, TURNED],
        [((BLK, 2 * W), BF), ((2 * W, BLK), BF)],
        2 * UNIT, 30,
    )(info, q, q_far, own)

def call_picked(info, q, q_far, do, do_far, pieces, m, l, ot):
    return kernel(
        picked,
        [NEAR, FAR, NEAR, FAR] + [whole(PAIR)] * 4 + [tile(ROW), tile(ROW), tile(TURNED)],
        [FIRST, SECOND, tile(TURNED), tile(ROW), tile(ROW)] + [whole(PAIR)] * 4,
        [HALF, HALF, TURNED, ROW, ROW] + [PAIR] * 4,
        [((2 * BLK, 2 * W), BF), ((2 * BLK, 2 * W), BF), ((2 * W, 2 * BLK), BF), ((2 * W, 2 * BLK), BF),
         ((2 * BLK, R), F32), ((2 * BLK, R), BF), ((2 * BLK, R), BF),
         ((2 * BLK, W), F32), ((2 * BLK, W), F32)],
        10 * UNIT, 52,
    )(info, q, q_far, do, do_far, *pieces, m, l, ot)

def call_own_backward(info, q, q_far, do, do_far, own, p, c, rd, dq):
    return kernel(
        own_backward,
        [NEAR, FAR, NEAR, FAR, whole(own.shape), tile(PROBS), tile(ROW), tile(ROW), tile(TURNED)],
        [FIRST, SECOND] + [whole(PIECE)] * 4,
        [HALF, HALF] + [PIECE] * 4,
        [((BLK, 2 * W), BF), ((2 * W, BLK), BF), ((BLK, W), F32), ((BLK, W), F32)],
        3 * UNIT, 40,
    )(info, q, q_far, do, do_far, own, p, c, rd, dq)

HEADS = (2, T, W)

def glue(body, args, outs, copies):
    spec = lambda shape: pl.BlockSpec(shape, lambda i: (0,) * len(shape))
    if copies:
        spec = lambda shape: pl.BlockSpec(memory_space=pl.ANY)
    arrays = args[1:]
    return pl.pallas_call(
        body,
        out_shape=[pltpu.HBM(s, F32) for s in outs],
        grid=(1,),
        in_specs=[pl.BlockSpec(memory_space=pltpu.SMEM)] + [spec(a.shape) for a in arrays],
        out_specs=[spec(s) for s in outs],
        scratch_shapes=[pltpu.SemaphoreType.DMA((copies,))] if copies else [],
        compiler_params=pltpu.CompilerParams(
            dimension_semantics=("arbitrary",), vmem_limit_bytes=(4 if copies else 20) << 20),
        cost_estimate=pl.CostEstimate(
            flops=0, transcendentals=0,
            bytes_accessed=4 * sum(math.prod(s) for s in [a.shape for a in arrays] + list(outs))),
        name=body.__name__,
    )(args[0], *arrays)

def finish(pairs, sems):
    for n, (source, target) in enumerate(pairs):
        pltpu.make_async_copy(source, target, sems.at[n]).wait()

def shift(array, axis, step):
    if step == 0:
        return array
    return lax.ppermute(array, axis, [(i, (i + step) % 4) for i in range(4)])

def mirror(array, flip):
    return lax.ppermute(array, "z", [(i, i ^ flip) for i in range(4)])

def chosen(table, y, x, j):
    block = jnp.maximum(table[y * 4 + x, 1 + j], 0)
    return block // 4, block % 4

def assemble(spot, keys, values, other_keys, other_values, k_ref, v_ref, kv_ref, sems):
    core = spot[0]
    pairs = []
    for h in range(2):
        cols = pl.ds(pl.multiple_of((core * 2 + h) * W, W), W)
        for i, (mine, other, out) in enumerate(
                ((keys, other_keys, k_ref), (values, other_values, v_ref))):
            for ref, half in ((mine, core), (other, 1 - core)):
                rows = pl.ds(pl.multiple_of(half * (T // 2), T // 2), T // 2)
                pairs += [(ref.at[:, cols], out.at[h, rows, :]),
                          (ref.at[:, cols], kv_ref.at[i, h, rows, :])]
    for n, (source, target) in enumerate(pairs):
        pltpu.make_async_copy(source, target, sems.at[n]).start()
    finish(pairs, sems)

def pick(table, *refs):
    y, x = lax.axis_index("y"), lax.axis_index("x")
    k_in, v_in, k_out, v_out, sems = refs[0:4], refs[4:8], refs[8:11], refs[11:14], refs[14]
    pairs = []
    for step in (1, 2, 3):
        for j in range(2):
            row, _ = chosen(table, y, (x + step) % 4, j)
            _, column = chosen(table, (y + step) % 4, x, j)
            for off, arrays, out in (((y - row) % 4, k_in, k_out), ((x - column) % 4, v_in, v_out)):
                target = out[step - 1].at[j]
                for i in range(4):
                    @pl.when(off == i)
                    def _(source=arrays[i], target=target, n=len(pairs)):
                        pltpu.make_async_copy(source, target, sems.at[n]).start()
                pairs.append((arrays[0], target))
    finish(pairs, sems)

def join(table, *refs):
    y, x = lax.axis_index("y"), lax.axis_index("x")
    head = lax.axis_index("z") // 2
    k_along, v_along, k_in, v_in = refs[0:4], refs[4:8], refs[8:11], refs[11:14]
    same, cross, sems = refs[14:]
    pairs = []
    for j in range(2):
        row, column = chosen(table, y, x, j)
        for n, near, off, along, got in (
                (0, (y - row) % 4, (x - column) % 4, k_along, k_in),
                (1, (x - column) % 4, (y - row) % 4, v_along, v_in)):
            for h, out in ((head, same), (1 - head, cross)):
                target = out.at[j, n]
                for i in range(4):
                    @pl.when((off == 0) & (near == i))
                    def _(source=along[i].at[h], target=target, at=len(pairs)):
                        pltpu.make_async_copy(source, target, sems.at[at]).start()
                for i in range(3):
                    @pl.when(off == i + 1)
                    def _(source=got[i].at[j, h], target=target, at=len(pairs)):
                        pltpu.make_async_copy(source, target, sems.at[at]).start()
                pairs.append((along[0].at[h], target))
    finish(pairs, sems)

def spread(spot, mine, added, passed, passed2, k_out, v_out):
    head = spot[1]
    for j in range(mine.shape[0]):
        for n, out in ((0, k_out), (1, v_out)):
            out[j, head] = mine[j, n] + added[j, n]
            out[j, 1 - head] = passed[j, n] + passed2[j, n]

def collect(table, *refs):
    y, x = lax.axis_index("y"), lax.axis_index("x")
    k_in, v_in, k_out, v_out = (refs[i:i + 4] for i in range(0, 16, 4))
    for ref in k_out + v_out:
        ref[...] = jnp.zeros_like(ref)
    for step in range(4):
        for j in range(2):
            row, column = chosen(table, y, (x - step) % 4, j)
            row2, column2 = chosen(table, (y - step) % 4, x, j)
            for hit, off, source, out in (
                    (column == x, (y - row) % 4, k_in[step], k_out),
                    (row2 == y, (x - column2) % 4, v_in[step], v_out)):
                for i in range(4):
                    @pl.when(hit & (off == i))
                    def _(source=source, ref=out[i], j=j):
                        ref[...] += source[j]

def shards(queries, keys, values, cotangent, selected):
    core, z = lax.axis_index("head"), lax.axis_index("z")
    y, x = lax.axis_index("y"), lax.axis_index("x")
    head = z // 2
    mine = lax.dynamic_slice(selected, (y * 4 + x, 1), (1, 2))[0]
    info = jnp.concatenate([jnp.stack([z, head]), (mine >= 0).astype(jnp.int32)])
    spot = jnp.stack([core, head])
    swap = [(0, 1), (1, 0)]

    far = 1 - head
    q_far, do_far = (
        mirror(lax.dynamic_slice_in_dim(a, far * 4 * W, 4 * W, 1), 3)
        for a in (queries, cotangent)
    )
    other = [lax.ppermute(a, "head", swap) for a in (keys, values)]
    k, v, kv = glue(assemble, (spot, keys, values, *other), (HEADS, HEADS, (2,) + HEADS), 16)
    own = lax.all_gather(kv, "z", axis=0)

    k_along = [shift(k, "y", s) for s in range(4)]
    v_along = [shift(v, "x", s) for s in range(4)]
    sent = glue(pick, (selected, *k_along, *v_along), (PAIR,) * 6, 12)
    k_got = [shift(sent[s], "x", s + 1) for s in range(3)]
    v_got = [shift(sent[s + 3], "y", s + 1) for s in range(3)]
    same, cross = glue(join, (selected, *k_along, *v_along, *k_got, *v_got), (PAIR, PAIR), 8)
    pieces = [same, mirror(same, 1), mirror(cross, 2), mirror(cross, 3)]

    p, m, l, ot = call_own_forward(info, queries, q_far, own)
    out = call_picked(info, queries, q_far, cotangent, do_far, pieces, m, l, ot)
    o_near, o_far, dq, c, rd = out[:5]
    last = call_own_backward(info, queries, q_far, cotangent, do_far, own, p, c, rd, dq)

    def reduced(g):
        arrived = [g[0]] + [mirror(g[flip], flip) for flip in (1, 2, 3)]
        return glue(spread, (spot, *arrived), (g[0].shape,) * 2, 0)

    k_part, v_part = reduced(out[5:9])
    arrived = [shift(k_part, "x", s) for s in range(4)] + [shift(v_part, "y", s) for s in range(4)]
    sums = glue(collect, (selected, *arrived), (HEADS,) * 8, 0)
    own_k, own_v = reduced([a[None] for a in last[2:6]])
    grad_k = own_k[0] + sum(shift(sums[s], "y", (4 - s) % 4) for s in range(4))
    grad_v = own_v[0] + sum(shift(sums[4 + s], "x", (4 - s) % 4) for s in range(4))

    half = T // 2

    def home(a):
        keep = lax.dynamic_slice_in_dim(a, core * half, half, 1)
        back = lax.ppermute(lax.dynamic_slice_in_dim(a, (1 - core) * half, half, 1), "head", swap)
        low, high = jnp.where(core == 0, keep, back), jnp.where(core == 0, back, keep)
        return jnp.concatenate([low[0], low[1], high[0], high[1]], 1)

    def sides(a, b):
        return jnp.where(head == 0, jnp.concatenate([a, b], 1), jnp.concatenate([b, a], 1))

    return (
        sides(o_near, mirror(o_far, 3)),
        sides(last[0], mirror(last[1], 3)),
        home(grad_k),
        home(grad_v),
    )

def solution(mesh):
    grid = Mesh(mesh.devices.reshape(4, 4, 4, 2), ("y", "x", "z", "head"))
    tokens = ("y", "x", "z")
    wide, narrow = P(tokens, "head"), P(tokens + ("head",), None)
    return jax.shard_map(
        shards,
        mesh=grid,
        in_specs=(wide, narrow, narrow, wide, P()),
        out_specs=(wide, wide, narrow, narrow),
        check_vma=False,
    )
```

```python
import math

import jax
import jax.numpy as jnp
from jax import lax
from jax.experimental import pallas as pl
from jax.experimental.pallas import tpu as pltpu
from jax.sharding import Mesh, PartitionSpec as P

W = 128
T = 256

SCALE = 1.0 / math.sqrt(W)
LOG2E = math.log2(math.e)
LN2 = math.log(2.0)
BF = jnp.bfloat16
F32 = jnp.float32
BLK = 4 * T
HP = 2
STEPS = 4 // HP
R = HP * T

def split(x):
    hi = x.astype(BF)
    return hi, (x - hi.astype(F32)).astype(BF)

def twice(x, axis):
    return jnp.concatenate([x, x], axis=axis)

def mm(a, b):
    return lax.dot_general(a, b, (((1,), (0,)), ((), ())), preferred_element_type=F32)

def turned(x):
    return jnp.concatenate([x[:, i * W:(i + 1) * W].T for i in range(HP)], axis=1)

def upright(x):
    return jnp.concatenate([x[:, i * T:(i + 1) * T].T for i in range(HP)], axis=1)

def stacked(x):
    return jnp.concatenate([x[:, i * W:(i + 1) * W] for i in range(HP)], axis=0)

def left(x):
    hi, lo = split(x)
    return jnp.concatenate([hi, hi, lo, lo], axis=0)

def right(x):
    hi, lo = split(x)
    return twice(jnp.concatenate([hi, lo], axis=1), 0)

def fill(ref, rows, cat, tr):
    x = ref[...]
    hi, lo = split(x)
    if cat is not None:
        cat[rows, 0:W] = hi
        cat[rows, W:2 * W] = lo
    if tr is not None:
        hit, lot = split(x.T)
        tr[0:W, rows] = hit
        tr[W:2 * W, rows] = lot

def values_sum(tr, hi, lo):
    a = mm(tr, hi)
    return a[0:W] + a[W:2 * W] + mm(tr[0:W], lo)

def halves(x):
    return x[:, 0:W] + x[:, W:2 * W]

def own_refs(own_ref, head, c):
    return [own_ref.at[c, i, head] for i in range(2)]

def near_far(u, near, far):
    return jnp.where(u == 0, near[...], far[...])

def own_forward(info, ql_ref, qr_ref, own_ref, p_ref, m_ref, l_ref, ot_ref, kc, vt):
    u = pl.program_id(0)

    @pl.when((u == 0) & (pl.program_id(1) == 0))
    def _():
        for c in range(4):
            k, v = own_refs(own_ref, info[1], c)
            fill(k, slice(c * T, (c + 1) * T), kc, None)
            fill(v, slice(c * T, (c + 1) * T), None, vt)

    quarter = jnp.where(u == 0, info[0], 3 - info[0])
    q = left(turned(near_far(u, ql_ref, qr_ref)) * (SCALE * LOG2E))
    s = mm(twice(kc[...], 1), q)
    token = lax.broadcasted_iota(jnp.int32, (BLK, R), 1) & (T - 1)
    ahead = lax.broadcasted_iota(jnp.int32, (BLK, R), 0) - token
    s = jnp.where(ahead <= quarter * T, s, -jnp.inf)
    m = jnp.max(s, axis=0, keepdims=True)
    p = jnp.exp2(s - m)
    p_ref[0] = p
    m_ref[0] = m
    l_ref[0] = jnp.sum(p, axis=0, keepdims=True)
    hi, lo = split(p)
    ot_ref[0] = values_sum(vt[...], hi, lo)

def picked(info, ql_ref, qr_ref, dl_ref, dr_ref, s0, s1, s2, s3,
           m0_ref, l0_ref, ot0_ref, ol_ref, or_ref, dq_ref, c_ref, rd_ref, g0, g1, g2, g3,
           kc, vc, kt, vt, s_sc, phi, plo, dk_acc, dv_acc):
    u, step = pl.program_id(0), pl.program_id(1)

    @pl.when((u == 0) & (step == 0))
    def _():
        for j in range(2):
            for x in range(4):
                rows = slice((j * 4 + x) * T, (j * 4 + x + 1) * T)
                piece = (s0, s1, s2, s3)[x]
                fill(piece.at[j, 0], rows, kc, kt)
                fill(piece.at[j, 1], rows, vc, vt)
        dk_acc[...] = jnp.zeros_like(dk_acc)
        dv_acc[...] = jnp.zeros_like(dv_acc)

    q = near_far(u, ql_ref, qr_ref) * (SCALE * LOG2E)
    do = near_far(u, dl_ref, dr_ref)
    qt = left(turned(q))
    m0 = m0_ref[0]
    m = m0
    for j in range(2):
        rows = slice(j * BLK, (j + 1) * BLK)
        s = mm(twice(kc[rows, :], 1), qt)
        s = jnp.where(info[2 + j] > 0, s, -jnp.inf)
        s_sc[rows, :] = s
        m = jnp.maximum(m, jnp.max(s, axis=0, keepdims=True))
    shrink = jnp.exp2(m0 - m)
    l = l0_ref[0] * shrink
    ot = ot0_ref[0] * shrink
    for j in range(2):
        rows = slice(j * BLK, (j + 1) * BLK)
        p = jnp.exp2(s_sc[rows, :] - m)
        s_sc[rows, :] = p
        hi, lo = split(p)
        phi[rows, :] = hi
        plo[rows, :] = lo
        l = l + jnp.sum(p, axis=0, keepdims=True)
        ot = ot + values_sum(vt[:, rows], hi, lo)
    inv = 1.0 / l
    ot = ot * inv
    dot = turned(do) * inv
    rd = jnp.sum(dot * ot, axis=0, keepdims=True)
    c_ref[0] = inv * shrink
    rd_ref[0] = rd * shrink
    o = upright(ot)

    @pl.when(u == 0)
    def _():
        ol_ref[...] = o

    @pl.when(u == 1)
    def _():
        or_ref[...] = o

    dt = left(dot)
    d2 = right(stacked(upright(dot)))
    q2 = right(stacked(q))
    dq = jnp.zeros((W, R), F32)
    for j in range(2):
        rows = slice(j * BLK, (j + 1) * BLK)
        dp = mm(twice(vc[rows, :], 1), dt)
        hi, lo = split(s_sc[rows, :] * (dp - rd))
        dq = dq + values_sum(kt[:, rows], hi, lo)
        dv_acc[rows, :] += halves(mm(jnp.concatenate([phi[rows, :], plo[rows, :]], axis=1), d2))
        dk_acc[rows, :] += halves(mm(jnp.concatenate([hi, lo], axis=1), q2))
    dq_ref[0] = dq

    @pl.when((u == 1) & (step == STEPS - 1))
    def _():
        for j in range(2):
            for x, out in enumerate((g0, g1, g2, g3)):
                rows = slice((j * 4 + x) * T, (j * 4 + x + 1) * T)
                out[j, 0] = dk_acc[rows, :] * LN2
                out[j, 1] = dv_acc[rows, :]

def own_backward(info, ql_ref, qr_ref, dl_ref, dr_ref, own_ref, p_ref, c_ref, rd_ref, dq_ref,
                 gl_ref, gr_ref, h0, h1, h2, h3, vc, kt, dk_acc, dv_acc):
    u, step = pl.program_id(0), pl.program_id(1)

    @pl.when((u == 0) & (step == 0))
    def _():
        for c in range(4):
            k, v = own_refs(own_ref, info[1], c)
            fill(k, slice(c * T, (c + 1) * T), None, kt)
            fill(v, slice(c * T, (c + 1) * T), vc, None)
        dk_acc[...] = jnp.zeros_like(dk_acc)
        dv_acc[...] = jnp.zeros_like(dv_acc)

    q = near_far(u, ql_ref, qr_ref) * (SCALE * LOG2E)
    dot = turned(near_far(u, dl_ref, dr_ref)) * c_ref[0]
    p = p_ref[0]
    hi, lo = split(p)
    dv_acc[...] += halves(mm(jnp.concatenate([hi, lo], axis=1), right(stacked(upright(dot)))))
    dp = mm(twice(vc[...], 1), left(dot))
    hi, lo = split(p * (dp - rd_ref[0]))
    dk_acc[...] += halves(mm(jnp.concatenate([hi, lo], axis=1), right(stacked(q))))
    dq = upright(dq_ref[0] + values_sum(kt[...], hi, lo)) * SCALE

    @pl.when(u == 0)
    def _():
        gl_ref[...] = dq

    @pl.when(u == 1)
    def _():
        gr_ref[...] = dq

    @pl.when((u == 1) & (step == STEPS - 1))
    def _():
        for x, out in enumerate((h0, h1, h2, h3)):
            rows = pl.ds(pl.multiple_of((info[0] ^ x) * T, T), T)
            out[0] = dk_acc[rows, :] * LN2
            out[1] = dv_acc[rows, :]

def tile(shape):
    return pl.BlockSpec((1,) + shape[1:], lambda u, h, i: (u * STEPS + h, 0, 0))

def whole(shape):
    return pl.BlockSpec(shape, lambda u, h, i: (0,) * len(shape))

NEAR = pl.BlockSpec((T, HP * W), lambda u, h, i: (0, i[1] * STEPS + h))
FAR = pl.BlockSpec((T, HP * W), lambda u, h, i: (0, h))
FIRST = pl.BlockSpec((T, HP * W), lambda u, h, i: (0, jnp.where(u == 0, h, STEPS - 1)))
SECOND = pl.BlockSpec((T, HP * W), lambda u, h, i: (0, jnp.where(u == 0, 0, h)))
PROBS, ROW, TURNED = (2 * STEPS, BLK, R), (2 * STEPS, 1, R), (2 * STEPS, W, R)
HALF, PIECE, PAIR = (T, 4 * W), (2, T, W), (2, 2, T, W)

def kernel(body, ins, outs, out_shapes, scratch, flops, limit):
    return pl.pallas_call(
        body,
        out_shape=[pltpu.HBM(s, F32) for s in out_shapes],
        grid_spec=pltpu.PrefetchScalarGridSpec(
            num_scalar_prefetch=1,
            grid=(2, STEPS),
            in_specs=ins,
            out_specs=outs,
            scratch_shapes=[pltpu.VMEM(s, d) for s, d in scratch],
        ),
        compiler_params=pltpu.CompilerParams(
            dimension_semantics=("arbitrary", "arbitrary"), vmem_limit_bytes=limit << 20),
        cost_estimate=pl.CostEstimate(
            flops=flops, transcendentals=0, bytes_accessed=16 << 20),
        name=body.__name__,
    )

UNIT = 2 * 2048 * BLK * W * 4

def call_own_forward(info, q, q_far, own):
    return kernel(
        own_forward,
        [NEAR, FAR, whole(own.shape)],
        [tile(PROBS), tile(ROW), tile(ROW), tile(TURNED)],
        [PROBS, ROW, ROW, TURNED],
        [((BLK, 2 * W), BF), ((2 * W, BLK), BF)],
        2 * UNIT, 30,
    )(info, q, q_far, own)

def call_picked(info, q, q_far, do, do_far, pieces, m, l, ot):
    return kernel(
        picked,
        [NEAR, FAR, NEAR, FAR] + [whole(PAIR)] * 4 + [tile(ROW), tile(ROW), tile(TURNED)],
        [FIRST, SECOND, tile(TURNED), tile(ROW), tile(ROW)] + [whole(PAIR)] * 4,
        [HALF, HALF, TURNED, ROW, ROW] + [PAIR] * 4,
        [((2 * BLK, 2 * W), BF), ((2 * BLK, 2 * W), BF), ((2 * W, 2 * BLK), BF), ((2 * W, 2 * BLK), BF),
         ((2 * BLK, R), F32), ((2 * BLK, R), BF), ((2 * BLK, R), BF),
         ((2 * BLK, W), F32), ((2 * BLK, W), F32)],
        10 * UNIT, 52,
    )(info, q, q_far, do, do_far, *pieces, m, l, ot)

def call_own_backward(info, q, q_far, do, do_far, own, p, c, rd, dq):
    return kernel(
        own_backward,
        [NEAR, FAR, NEAR, FAR, whole(own.shape), tile(PROBS), tile(ROW), tile(ROW), tile(TURNED)],
        [FIRST, SECOND] + [whole(PIECE)] * 4,
        [HALF, HALF] + [PIECE] * 4,
        [((BLK, 2 * W), BF), ((2 * W, BLK), BF), ((BLK, W), F32), ((BLK, W), F32)],
        3 * UNIT, 40,
    )(info, q, q_far, do, do_far, own, p, c, rd, dq)

HEADS = (2, T, W)

def glue(body, args, outs, copies, hbm=False):
    spec = lambda shape: pl.BlockSpec(shape, lambda i: (0,) * len(shape))
    if copies:
        spec = lambda shape: pl.BlockSpec(memory_space=pl.ANY)
    arrays = args[1:]
    return pl.pallas_call(
        body,
        out_shape=[(pltpu.HBM if hbm else jax.ShapeDtypeStruct)(s, F32) for s in outs],
        grid=(1,),
        in_specs=[pl.BlockSpec(memory_space=pltpu.SMEM)] + [spec(a.shape) for a in arrays],
        out_specs=[spec(s) for s in outs],
        scratch_shapes=[pltpu.SemaphoreType.DMA((copies,))] if copies else [],
        compiler_params=pltpu.CompilerParams(
            dimension_semantics=("arbitrary",), vmem_limit_bytes=(4 if copies else 20) << 20),
        cost_estimate=pl.CostEstimate(
            flops=0, transcendentals=0,
            bytes_accessed=4 * sum(math.prod(s) for s in [a.shape for a in arrays] + list(outs))),
        name=body.__name__,
    )(args[0], *arrays)

def finish(pairs, sems):
    for n, (source, target) in enumerate(pairs):
        pltpu.make_async_copy(source, target, sems.at[n]).wait()

def shift(array, axis, step):
    if step == 0:
        return array
    return lax.ppermute(array, axis, [(i, (i + step) % 4) for i in range(4)])

def after(array, *others):
    return lax.optimization_barrier((array, *others))[0]

def ring(array, axis, late):
    one = shift(array, axis, 1)
    two = shift(after(array, one) if late else array, axis, 2)
    return [array, one, two, shift(array, axis, 3)]

def mirror(array, flip):
    return lax.ppermute(array, "z", [(i, i ^ flip) for i in range(4)])

def chosen(table, y, x, j):
    block = jnp.maximum(table[y * 4 + x, 1 + j], 0)
    return block // 4, block % 4

def assemble(spot, keys, values, other_keys, other_values, k_ref, v_ref, kv_ref, sems):
    core = spot[0]
    pairs = []
    for h in range(2):
        cols = pl.ds(pl.multiple_of((core * 2 + h) * W, W), W)
        for i, (mine, other, out) in enumerate(
                ((keys, other_keys, k_ref), (values, other_values, v_ref))):
            for ref, half in ((mine, core), (other, 1 - core)):
                rows = pl.ds(pl.multiple_of(half * (T // 2), T // 2), T // 2)
                pairs += [(ref.at[:, cols], out.at[h, rows, :]),
                          (ref.at[:, cols], kv_ref.at[i, h, rows, :])]
    for n, (source, target) in enumerate(pairs):
        pltpu.make_async_copy(source, target, sems.at[n]).start()
    finish(pairs, sems)

def pick(table, *refs):
    y, x = lax.axis_index("y"), lax.axis_index("x")
    k_in, v_in, k_out, v_out, sems = refs[0:4], refs[4:8], refs[8:11], refs[11:14], refs[14]
    pairs = []
    for step in (1, 2, 3):
        for j in range(2):
            row, _ = chosen(table, y, (x + step) % 4, j)
            _, column = chosen(table, (y + step) % 4, x, j)
            for off, arrays, out in (((y - row) % 4, k_in, k_out), ((x - column) % 4, v_in, v_out)):
                target = out[step - 1].at[j]
                for i in range(4):
                    @pl.when(off == i)
                    def _(source=arrays[i], target=target, n=len(pairs)):
                        pltpu.make_async_copy(source, target, sems.at[n]).start()
                pairs.append((arrays[0], target))
    finish(pairs, sems)

def join(table, *refs):
    y, x = lax.axis_index("y"), lax.axis_index("x")
    head = lax.axis_index("z") // 2
    k_along, v_along, k_in, v_in = refs[0:4], refs[4:8], refs[8:11], refs[11:14]
    same, cross, sems = refs[14:]
    pairs = []
    for j in range(2):
        row, column = chosen(table, y, x, j)
        for n, near, off, along, got in (
                (0, (y - row) % 4, (x - column) % 4, k_along, k_in),
                (1, (x - column) % 4, (y - row) % 4, v_along, v_in)):
            for h, out in ((head, same), (1 - head, cross)):
                target = out.at[j, n]
                for i in range(4):
                    @pl.when((off == 0) & (near == i))
                    def _(source=along[i].at[h], target=target, at=len(pairs)):
                        pltpu.make_async_copy(source, target, sems.at[at]).start()
                for i in range(3):
                    @pl.when(off == i + 1)
                    def _(source=got[i].at[j, h], target=target, at=len(pairs)):
                        pltpu.make_async_copy(source, target, sems.at[at]).start()
                pairs.append((along[0].at[h], target))
    finish(pairs, sems)

def spread(spot, mine, added, passed, passed2, k_out, v_out):
    head = spot[1]
    for j in range(mine.shape[0]):
        for n, out in ((0, k_out), (1, v_out)):
            out[j, head] = mine[j, n] + added[j, n]
            out[j, 1 - head] = passed[j, n] + passed2[j, n]

def collect(table, *refs):
    y, x = lax.axis_index("y"), lax.axis_index("x")
    k_in, v_in, k_out, v_out = (refs[i:i + 4] for i in range(0, 16, 4))
    for ref in k_out + v_out:
        ref[...] = jnp.zeros_like(ref)
    for step in range(4):
        for j in range(2):
            row, column = chosen(table, y, (x - step) % 4, j)
            row2, column2 = chosen(table, (y - step) % 4, x, j)
            for hit, off, source, out in (
                    (column == x, (y - row) % 4, k_in[step], k_out),
                    (row2 == y, (x - column2) % 4, v_in[step], v_out)):
                for i in range(4):
                    @pl.when(hit & (off == i))
                    def _(source=source, ref=out[i], j=j):
                        ref[...] += source[j]

def shards(queries, keys, values, cotangent, selected):
    core, z = lax.axis_index("head"), lax.axis_index("z")
    y, x = lax.axis_index("y"), lax.axis_index("x")
    head = z // 2
    mine = lax.dynamic_slice(selected, (y * 4 + x, 1), (1, 2))[0]
    info = jnp.concatenate([jnp.stack([z, head]), (mine >= 0).astype(jnp.int32)])
    spot = jnp.stack([core, head])
    swap = [(0, 1), (1, 0)]

    far = 1 - head
    q_far, do_far = (
        mirror(lax.dynamic_slice_in_dim(a, far * 4 * W, 4 * W, 1), 3)
        for a in (queries, cotangent)
    )
    other = [lax.ppermute(a, "head", swap) for a in (keys, values)]
    k, v, kv = glue(assemble, (spot, keys, values, *other), (HEADS, HEADS, (2,) + HEADS), 16)
    own = lax.all_gather(kv, "z", axis=0)

    k_along = ring(k, "y", False)
    v_along = ring(v, "x", True)
    sent = glue(pick, (selected, *k_along, *v_along), (PAIR,) * 6, 12, hbm=True)
    k_got = [shift(sent[s], "x", s + 1) for s in range(3)]
    v_one = shift(sent[3], "y", 1)
    v_got = [v_one, shift(after(sent[4], v_one), "y", 2), shift(sent[5], "y", 3)]
    same, cross = glue(join, (after(selected, q_far, do_far), *k_along, *v_along, *k_got, *v_got), (PAIR, PAIR), 8)
    pieces = [same, mirror(same, 1), mirror(cross, 2), mirror(cross, 3)]

    p, m, l, ot = call_own_forward(info, queries, q_far, own)
    out = call_picked(info, queries, q_far, cotangent, do_far, pieces, m, l, ot)
    o_near, o_far, dq, c, rd = out[:5]
    last = call_own_backward(info, queries, q_far, cotangent, do_far, own, p, c, rd, dq)

    def reduced(g, *others):
        arrived = [g[0]] + [mirror(g[flip], flip) for flip in (1, 2, 3)]
        arrived[3] = after(arrived[3], *others)
        return glue(spread, (spot, *arrived), (g[0].shape,) * 2, 0)

    k_part, v_part = reduced(out[5:9], last[0])
    arrived = ring(k_part, "x", False) + ring(v_part, "y", True)
    sums = glue(collect, (selected, *arrived), (HEADS,) * 8, 0)
    own_k, own_v = reduced([a[None] for a in last[2:6]])
    grad_k = own_k[0] + sum(shift(sums[s], "y", (4 - s) % 4) for s in range(4))
    v_back = shift(sums[5], "x", 3)
    grad_v = own_v[0] + sums[4] + v_back + shift(after(sums[6], v_back), "x", 2) + shift(sums[7], "x", 1)

    half = T // 2

    def home(a):
        keep = lax.dynamic_slice_in_dim(a, core * half, half, 1)
        back = lax.ppermute(lax.dynamic_slice_in_dim(a, (1 - core) * half, half, 1), "head", swap)
        low, high = jnp.where(core == 0, keep, back), jnp.where(core == 0, back, keep)
        return jnp.concatenate([low[0], low[1], high[0], high[1]], 1)

    def sides(a, b):
        return jnp.where(head == 0, jnp.concatenate([a, b], 1), jnp.concatenate([b, a], 1))

    return (
        sides(o_near, mirror(o_far, 3)),
        sides(last[0], mirror(last[1], 3)),
        home(grad_k),
        home(grad_v),
    )

def solution(mesh):
    grid = Mesh(mesh.devices.reshape(4, 4, 4, 2), ("y", "x", "z", "head"))
    tokens = ("y", "x", "z")
    wide, narrow = P(tokens, "head"), P(tokens + ("head",), None)
    return jax.shard_map(
        shards,
        mesh=grid,
        in_specs=(wide, narrow, narrow, wide, P()),
        out_specs=(wide, wide, narrow, narrow),
        check_vma=False,
    )
```

```python
import math

import jax
import jax.numpy as jnp
from jax import lax
from jax.experimental import pallas as pl
from jax.experimental.pallas import tpu as pltpu
from jax.sharding import Mesh, PartitionSpec as P

W = 128
T = 256

SCALE = 1.0 / math.sqrt(W)
LOG2E = math.log2(math.e)
LN2 = math.log(2.0)
BF = jnp.bfloat16
F32 = jnp.float32
BLK = 4 * T
HP = 2
STEPS = 4 // HP
R = HP * T

def split(x):
    hi = x.astype(BF)
    return hi, (x - hi.astype(F32)).astype(BF)

def twice(x, axis):
    return jnp.concatenate([x, x], axis=axis)

def mm(a, b):
    return lax.dot_general(a, b, (((1,), (0,)), ((), ())), preferred_element_type=F32)

def turned(x):
    return jnp.concatenate([x[:, i * W:(i + 1) * W].T for i in range(HP)], axis=1)

def upright(x):
    return jnp.concatenate([x[:, i * T:(i + 1) * T].T for i in range(HP)], axis=1)

def stacked(x):
    return jnp.concatenate([x[:, i * W:(i + 1) * W] for i in range(HP)], axis=0)

def left(x):
    hi, lo = split(x)
    return jnp.concatenate([hi, hi, lo, lo], axis=0)

def right(x):
    hi, lo = split(x)
    return twice(jnp.concatenate([hi, lo], axis=1), 0)

def fill(x, rows, cat, tr):
    hi, lo = split(x)
    if cat is not None:
        cat[rows, 0:W] = hi
        cat[rows, W:2 * W] = lo
    if tr is not None:
        hit, lot = split(x.T)
        tr[0:W, rows] = hit
        tr[W:2 * W, rows] = lot

def values_sum(tr, hi, lo):
    a = mm(tr, hi)
    return a[0:W] + a[W:2 * W] + mm(tr[0:W], lo)

def halves(x):
    return x[:, 0:W] + x[:, W:2 * W]

def own_quarter(info, mine_ref, other_ref, c):
    core = info[4]
    cols = pl.ds(pl.multiple_of((2 * core + info[1]) * W, W), W)
    a, b = mine_ref[c, :, cols], other_ref[c]
    return jnp.where(core == 0, a, b), jnp.where(core == 0, b, a)

def near_far(u, near, far):
    return jnp.where(u == 0, near[...], far[...])

def own_forward(info, ql_ref, qr_ref, mine_ref, other_ref, p_ref, m_ref, l_ref, ot_ref, kc, vt):
    u = pl.program_id(0)

    @pl.when((u == 0) & (pl.program_id(1) == 0))
    def _():
        for c in range(4):
            k, v = own_quarter(info, mine_ref, other_ref, c)
            fill(k, slice(c * T, (c + 1) * T), kc, None)
            fill(v, slice(c * T, (c + 1) * T), None, vt)

    quarter = jnp.where(u == 0, info[0], 3 - info[0])
    q = left(turned(near_far(u, ql_ref, qr_ref)) * (SCALE * LOG2E))
    s = mm(twice(kc[...], 1), q)
    token = lax.broadcasted_iota(jnp.int32, (BLK, R), 1) & (T - 1)
    ahead = lax.broadcasted_iota(jnp.int32, (BLK, R), 0) - token
    s = jnp.where(ahead <= quarter * T, s, -jnp.inf)
    m = jnp.max(s, axis=0, keepdims=True)
    p = jnp.exp2(s - m)
    p_ref[0] = p
    m_ref[0] = m
    l_ref[0] = jnp.sum(p, axis=0, keepdims=True)
    hi, lo = split(p)
    ot_ref[0] = values_sum(vt[...], hi, lo)

def picked(info, ql_ref, qr_ref, dl_ref, dr_ref, s0, s1, s2, s3,
           m0_ref, l0_ref, ot0_ref, ol_ref, or_ref, dq_ref, c_ref, rd_ref, g0, g1, g2, g3,
           kc, vc, kt, vt, s_sc, phi, plo, dk_acc, dv_acc):
    u, step = pl.program_id(0), pl.program_id(1)

    @pl.when((u == 0) & (step == 0))
    def _():
        for j in range(2):
            for x in range(4):
                rows = slice((j * 4 + x) * T, (j * 4 + x + 1) * T)
                piece = (s0, s1, s2, s3)[x]
                fill(piece[j, info[4]], rows, kc, kt)
                fill(piece[j, 1 - info[4]], rows, vc, vt)
        dk_acc[...] = jnp.zeros_like(dk_acc)
        dv_acc[...] = jnp.zeros_like(dv_acc)

    q = near_far(u, ql_ref, qr_ref) * (SCALE * LOG2E)
    do = near_far(u, dl_ref, dr_ref)
    qt = left(turned(q))
    m0 = m0_ref[0]
    m = m0
    for j in range(2):
        rows = slice(j * BLK, (j + 1) * BLK)
        s = mm(twice(kc[rows, :], 1), qt)
        s = jnp.where(info[2 + j] > 0, s, -jnp.inf)
        s_sc[rows, :] = s
        m = jnp.maximum(m, jnp.max(s, axis=0, keepdims=True))
    shrink = jnp.exp2(m0 - m)
    l = l0_ref[0] * shrink
    ot = ot0_ref[0] * shrink
    for j in range(2):
        rows = slice(j * BLK, (j + 1) * BLK)
        p = jnp.exp2(s_sc[rows, :] - m)
        s_sc[rows, :] = p
        hi, lo = split(p)
        phi[rows, :] = hi
        plo[rows, :] = lo
        l = l + jnp.sum(p, axis=0, keepdims=True)
        ot = ot + values_sum(vt[:, rows], hi, lo)
    inv = 1.0 / l
    ot = ot * inv
    dot = turned(do) * inv
    rd = jnp.sum(dot * ot, axis=0, keepdims=True)
    c_ref[0] = inv * shrink
    rd_ref[0] = rd * shrink
    o = upright(ot)

    @pl.when(u == 0)
    def _():
        ol_ref[...] = o

    @pl.when(u == 1)
    def _():
        or_ref[...] = o

    dt = left(dot)
    d2 = right(stacked(upright(dot)))
    q2 = right(stacked(q))
    dq = jnp.zeros((W, R), F32)
    for j in range(2):
        rows = slice(j * BLK, (j + 1) * BLK)
        dp = mm(twice(vc[rows, :], 1), dt)
        hi, lo = split(s_sc[rows, :] * (dp - rd))
        dq = dq + values_sum(kt[:, rows], hi, lo)
        dv_acc[rows, :] += halves(mm(jnp.concatenate([phi[rows, :], plo[rows, :]], axis=1), d2))
        dk_acc[rows, :] += halves(mm(jnp.concatenate([hi, lo], axis=1), q2))
    dq_ref[0] = dq

    @pl.when((u == 1) & (step == STEPS - 1))
    def _():
        for j in range(2):
            for x, out in enumerate((g0, g1, g2, g3)):
                rows = slice((j * 4 + x) * T, (j * 4 + x + 1) * T)
                out[j, info[4]] = dk_acc[rows, :] * LN2
                out[j, 1 - info[4]] = dv_acc[rows, :]

def own_backward(info, ql_ref, qr_ref, dl_ref, dr_ref, mine_ref, other_ref, p_ref, c_ref, rd_ref, dq_ref,
                 gl_ref, gr_ref, h0, h1, h2, h3, vc, kt, dk_acc, dv_acc):
    u, step = pl.program_id(0), pl.program_id(1)

    @pl.when((u == 0) & (step == 0))
    def _():
        for c in range(4):
            k, v = own_quarter(info, mine_ref, other_ref, c)
            fill(k, slice(c * T, (c + 1) * T), None, kt)
            fill(v, slice(c * T, (c + 1) * T), vc, None)
        dk_acc[...] = jnp.zeros_like(dk_acc)
        dv_acc[...] = jnp.zeros_like(dv_acc)

    q = near_far(u, ql_ref, qr_ref) * (SCALE * LOG2E)
    dot = turned(near_far(u, dl_ref, dr_ref)) * c_ref[0]
    p = p_ref[0]
    hi, lo = split(p)
    dv_acc[...] += halves(mm(jnp.concatenate([hi, lo], axis=1), right(stacked(upright(dot)))))
    dp = mm(twice(vc[...], 1), left(dot))
    hi, lo = split(p * (dp - rd_ref[0]))
    dk_acc[...] += halves(mm(jnp.concatenate([hi, lo], axis=1), right(stacked(q))))
    dq = upright(dq_ref[0] + values_sum(kt[...], hi, lo)) * SCALE

    @pl.when(u == 0)
    def _():
        gl_ref[...] = dq

    @pl.when(u == 1)
    def _():
        gr_ref[...] = dq

    @pl.when((u == 1) & (step == STEPS - 1))
    def _():
        for x, out in enumerate((h0, h1, h2, h3)):
            rows = pl.ds(pl.multiple_of((info[0] ^ x) * T, T), T)
            out[info[4]] = dk_acc[rows, :] * LN2
            out[1 - info[4]] = dv_acc[rows, :]

def tile(shape):
    return pl.BlockSpec((1,) + shape[1:], lambda u, h, i: (u * STEPS + h, 0, 0))

def whole(shape):
    return pl.BlockSpec(shape, lambda u, h, i: (0,) * len(shape))

NEAR = pl.BlockSpec((T, HP * W), lambda u, h, i: (0, i[1] * STEPS + h))
FAR = pl.BlockSpec((T, HP * W), lambda u, h, i: (0, h))
FIRST = pl.BlockSpec((T, HP * W), lambda u, h, i: (0, jnp.where(u == 0, h, STEPS - 1)))
SECOND = pl.BlockSpec((T, HP * W), lambda u, h, i: (0, jnp.where(u == 0, 0, h)))
PROBS, ROW, TURNED = (2 * STEPS, BLK, R), (2 * STEPS, 1, R), (2 * STEPS, W, R)
HALF, PIECE, PAIR = (T, 4 * W), (2, T, W), (2, 2, T, W)

def kernel(body, ins, outs, out_shapes, scratch, flops, limit):
    return pl.pallas_call(
        body,
        out_shape=[pltpu.HBM(s, F32) for s in out_shapes],
        grid_spec=pltpu.PrefetchScalarGridSpec(
            num_scalar_prefetch=1,
            grid=(2, STEPS),
            in_specs=ins,
            out_specs=outs,
            scratch_shapes=[pltpu.VMEM(s, d) for s, d in scratch],
        ),
        compiler_params=pltpu.CompilerParams(
            dimension_semantics=("arbitrary", "arbitrary"), vmem_limit_bytes=limit << 20),
        cost_estimate=pl.CostEstimate(
            flops=flops, transcendentals=0, bytes_accessed=16 << 20),
        name=body.__name__,
    )

UNIT = 2 * 2048 * BLK * W * 4

def call_own_forward(info, q, q_far, mine, other):
    return kernel(
        own_forward,
        [NEAR, FAR, whole(mine.shape), whole(other.shape)],
        [tile(PROBS), tile(ROW), tile(ROW), tile(TURNED)],
        [PROBS, ROW, ROW, TURNED],
        [((BLK, 2 * W), BF), ((2 * W, BLK), BF)],
        2 * UNIT, 30,
    )(info, q, q_far, mine, other)

def call_picked(info, q, q_far, do, do_far, pieces, m, l, ot):
    return kernel(
        picked,
        [NEAR, FAR, NEAR, FAR] + [whole(PAIR)] * 4 + [tile(ROW), tile(ROW), tile(TURNED)],
        [FIRST, SECOND, tile(TURNED), tile(ROW), tile(ROW)] + [whole(PAIR)] * 4,
        [HALF, HALF, TURNED, ROW, ROW] + [PAIR] * 4,
        [((2 * BLK, 2 * W), BF), ((2 * BLK, 2 * W), BF), ((2 * W, 2 * BLK), BF), ((2 * W, 2 * BLK), BF),
         ((2 * BLK, R), F32), ((2 * BLK, R), BF), ((2 * BLK, R), BF),
         ((2 * BLK, W), F32), ((2 * BLK, W), F32)],
        10 * UNIT, 52,
    )(info, q, q_far, do, do_far, *pieces, m, l, ot)

def call_own_backward(info, q, q_far, do, do_far, mine, other, p, c, rd, dq):
    return kernel(
        own_backward,
        [NEAR, FAR, NEAR, FAR, whole(mine.shape), whole(other.shape), tile(PROBS), tile(ROW), tile(ROW), tile(TURNED)],
        [FIRST, SECOND] + [whole(PIECE)] * 4,
        [HALF, HALF] + [PIECE] * 4,
        [((BLK, 2 * W), BF), ((2 * W, BLK), BF), ((BLK, W), F32), ((BLK, W), F32)],
        3 * UNIT, 40,
    )(info, q, q_far, do, do_far, mine, other, p, c, rd, dq)

FULL, HEADS = (T, 4 * W), (4, T, W)
SWAP = [(0, 1), (1, 0)]
PLACE = ("y", "x", "head")

def glue(body, args, outs, copies, hbm=False):
    spec = lambda shape: pl.BlockSpec(shape, lambda i: (0,) * len(shape))
    if copies:
        spec = lambda shape: pl.BlockSpec(memory_space=pl.ANY)
    arrays = args[1:]
    return pl.pallas_call(
        body,
        out_shape=[(pltpu.HBM if hbm else jax.ShapeDtypeStruct)(s, F32) for s in outs],
        grid=(1,),
        in_specs=[pl.BlockSpec(memory_space=pltpu.SMEM)] + [spec(a.shape) for a in arrays],
        out_specs=[spec(s) for s in outs],
        scratch_shapes=[pltpu.SemaphoreType.DMA((copies,))] if copies else [],
        compiler_params=pltpu.CompilerParams(
            dimension_semantics=("arbitrary",), vmem_limit_bytes=(4 if copies else 20) << 20),
        cost_estimate=pl.CostEstimate(
            flops=0, transcendentals=0,
            bytes_accessed=4 * sum(math.prod(s) for s in [a.shape for a in arrays] + list(outs))),
        name=body.__name__,
    )(args[0], *arrays)

def copy_all(pairs, sems):
    copies = [pltpu.make_async_copy(a, b, sems.at[n]) for n, (a, b) in enumerate(pairs)]
    for c in copies:
        c.start()
    for c in copies:
        c.wait()

def travel(array, step, stage):
    pairs = []
    for y in range(4):
        for x in range(4):
            for core in range(2):
                ty, tx = (y + step) % 4, x
                if core != stage:
                    ty, tx = y, (x + step) % 4
                pairs.append(((y * 4 + x) * 2 + core, (ty * 4 + tx) * 2 + core))
    return lax.ppermute(array, PLACE, pairs)

def mirror(array, flip):
    return lax.ppermute(array, "z", [(i, i ^ flip) for i in range(4)])

def swap(array):
    return lax.ppermute(array, "head", SWAP)

def after(array, *others):
    return lax.optimization_barrier((array, *others))[0]

def place():
    core, y, x = (lax.axis_index(a) for a in ("head", "y", "x"))
    return core, jnp.where(core == 0, y, x), jnp.where(core == 0, x, y)

def chosen(table, first, second, core, j):
    block = jnp.where(core == 0, first * 4 + second, second * 4 + first)
    other = jnp.maximum(table[block, 1 + j], 0)
    y, x = other // 4, other % 4
    return jnp.where(core == 0, y, x), jnp.where(core == 0, x, y)

def assemble(spot, keys, values, other, full, sems):
    core = spot[0]
    half = T // 2
    for i, ref in enumerate((keys, values)):
        @pl.when(core == i)
        def _(ref=ref):
            pltpu.make_async_copy(ref, full.at[pl.ds(pl.multiple_of(core * half, half), half)], sems.at[0]).start()
    pltpu.make_async_copy(other, full.at[pl.ds(pl.multiple_of((1 - core) * half, half), half)], sems.at[1]).start()
    for n in range(2):
        pltpu.make_async_copy(other, full.at[pl.ds(n * half, half)], sems.at[n]).wait()

def pick(table, *refs):
    core, here, there = place()
    along, out, sems = refs[0:4], refs[4:7], refs[7]
    waits = []
    for step in (1, 2, 3):
        for j in range(2):
            first, _ = chosen(table, here, (there + step) % 4, core, j)
            for i in range(4):
                @pl.when((here - first) % 4 == i)
                def _(source=along[i], target=out[step - 1].at[j], n=len(waits)):
                    pltpu.make_async_copy(source, target, sems.at[n]).start()
            waits.append((along[0], out[step - 1].at[j]))
    for n, (source, target) in enumerate(waits):
        pltpu.make_async_copy(source, target, sems.at[n]).wait()

def join(table, *refs):
    core, here, there = place()
    along, got, (mine, send), sems = refs[0:4], refs[4:7], refs[7:9], refs[9]
    waits = []
    for j in range(2):
        first, second = chosen(table, here, there, core, j)
        near, off = (here - first) % 4, (there - second) % 4
        for c, out in ((core, mine), (1 - core, send)):
            for i in range(2):
                cols = pl.ds(pl.multiple_of((2 * c + i) * W, W), W)
                target, n = out.at[j, i], len(waits)
                for k in range(4):
                    @pl.when((off == 0) & (near == k))
                    def _(source=along[k].at[:, cols], target=target, n=n):
                        pltpu.make_async_copy(source, target, sems.at[n]).start()
                for k in range(3):
                    @pl.when(off == k + 1)
                    def _(source=got[k].at[j, :, cols], target=target, n=n):
                        pltpu.make_async_copy(source, target, sems.at[n]).start()
                waits.append((along[0].at[:, cols], target))
    for n, (source, target) in enumerate(waits):
        pltpu.make_async_copy(source, target, sems.at[n]).wait()

def arrange(spot, mine, other, same, cross, sems):
    head = spot[1]
    copy_all([(ref.at[j, h], out.at[j, n]) for j in range(2)
              for n, ref in enumerate((mine, other))
              for h, out in ((head, same), (1 - head, cross))], sems)

def spread(spot, mine, added, passed, passed2, keep, send):
    head = spot[1]
    for j in range(mine.shape[0]):
        for n, out in ((0, keep), (1, send)):
            out[j, head] = mine[j, n] + added[j, n]
            out[j, 1 - head] = passed[j, n] + passed2[j, n]

def gather_heads(spot, keep, other, full, sems):
    core = spot[0]
    copy_all([(ref.at[j], full.at[j, pl.ds(2 * c, 2)]) for j in range(2)
              for c, ref in ((core, keep), (1 - core, other))], sems)

def collect(table, *refs):
    core, here, there = place()
    got, out = refs[0:4], refs[4:8]
    for ref in out:
        ref[...] = jnp.zeros_like(ref)
    for step in range(4):
        for j in range(2):
            first, second = chosen(table, here, (there - step) % 4, core, j)
            for i in range(4):
                @pl.when((second == there) & ((here - first) % 4 == i))
                def _(source=got[step], ref=out[i], j=j):
                    ref[...] += source[j]

def shards(queries, keys, values, cotangent, selected):
    core, z = lax.axis_index("head"), lax.axis_index("z")
    head = z // 2
    mine = lax.dynamic_slice(selected, (lax.axis_index("y") * 4 + lax.axis_index("x"), 1), (1, 2))[0]
    info = jnp.concatenate([jnp.stack([z, head]), (mine >= 0).astype(jnp.int32), core[None]])
    spot = jnp.stack([core, head])
    far = 1 - head
    q_far, do_far = (
        mirror(lax.dynamic_slice_in_dim(a, far * 4 * W, 4 * W, 1), 3)
        for a in (queries, cotangent)
    )
    got = swap(jnp.where(core == 0, values, keys))
    (full,) = glue(assemble, (spot, keys, values, got), (FULL,), 2)
    own = lax.all_gather(full, "z", axis=0)
    own_other = swap(lax.dynamic_slice_in_dim(own, (2 * (1 - core) + head) * W, W, 2))

    along = [full] + [travel(full, s, 0) for s in (1, 2, 3)]
    sent = glue(pick, (selected, *along), ((2,) + FULL,) * 3, 6, hbm=True)
    got = [travel(sent[s - 1], s, 1) for s in (1, 2, 3)]
    kept, send = glue(join, (after(selected, q_far, do_far), *along, *got), (PAIR, PAIR), 8)
    same, cross = glue(arrange, (spot, kept, swap(send)), (PAIR, PAIR), 8)
    pieces = [same] + [mirror(a, flip) for a, flip in ((same, 1), (cross, 2), (cross, 3))]

    p, m, l, ot = call_own_forward(info, queries, q_far, own, own_other)
    out = call_picked(info, queries, q_far, cotangent, do_far, pieces, m, l, ot)
    o_near, o_far, dq, c, rd = out[:5]
    last = call_own_backward(info, queries, q_far, cotangent, do_far, own, own_other, p, c, rd, dq)

    def reduced(g, *others):
        arrived = [g[0]] + [mirror(g[flip], flip) for flip in (1, 2, 3)]
        arrived[3] = after(arrived[3], *others)
        keep, send = glue(spread, (spot, *arrived), (g[0].shape,) * 2, 0)
        return keep, swap(send)

    (terms,) = glue(gather_heads, (spot, *reduced(out[5:9], last[0])), ((2,) + HEADS,), 4)
    arrived = [terms] + [travel(terms, s, 1) for s in (1, 2, 3)]
    sums = glue(collect, (selected, *arrived), (HEADS,) * 4, 0)
    low, high = reduced([a[None] for a in last[2:6]])
    total = sums[0] + sum(travel(sums[s], 4 - s, 0) for s in (1, 2, 3))
    total = total + jnp.where(
        core == 0, jnp.concatenate([low[0], high[0]], 0), jnp.concatenate([high[0], low[0]], 0)
    )

    half = T // 2

    def tokens(which):
        a = lax.dynamic_slice_in_dim(total, which * half, half, 1)
        return jnp.concatenate([a[h] for h in range(4)], 1)

    keep, back = tokens(core), swap(tokens(1 - core))

    def sides(a, b):
        return jnp.where(head == 0, jnp.concatenate([a, b], 1), jnp.concatenate([b, a], 1))

    return (
        sides(o_near, mirror(o_far, 3)),
        sides(last[0], mirror(last[1], 3)),
        jnp.where(core == 0, keep, back),
        jnp.where(core == 0, back, keep),
    )

def solution(mesh):
    grid = Mesh(mesh.devices.reshape(4, 4, 4, 2), ("y", "x", "z", "head"))
    tokens = ("y", "x", "z")
    wide, narrow = P(tokens, "head"), P(tokens + ("head",), None)
    return jax.shard_map(
        shards,
        mesh=grid,
        in_specs=(wide, narrow, narrow, wide, P()),
        out_specs=(wide, wide, narrow, narrow),
        check_vma=False,
    )
```

```python
import math

import jax
import jax.numpy as jnp
from jax import lax
from jax.experimental import pallas as pl
from jax.experimental.pallas import tpu as pltpu
from jax.sharding import Mesh, PartitionSpec as P

W = 128
T = 256

SCALE = 1.0 / math.sqrt(W)
LOG2E = math.log2(math.e)
LN2 = math.log(2.0)
BF = jnp.bfloat16
F32 = jnp.float32
BLK = 4 * T
HP = 2
STEPS = 4 // HP
R = HP * T

def split(x):
    hi = x.astype(BF)
    return hi, (x - hi.astype(F32)).astype(BF)

def twice(x, axis):
    return jnp.concatenate([x, x], axis=axis)

def mm(a, b):
    return lax.dot_general(a, b, (((1,), (0,)), ((), ())), preferred_element_type=F32)

def turned(x):
    return jnp.concatenate([x[:, i * W:(i + 1) * W].T for i in range(HP)], axis=1)

def upright(x):
    return jnp.concatenate([x[:, i * T:(i + 1) * T].T for i in range(HP)], axis=1)

def stacked(x):
    return jnp.concatenate([x[:, i * W:(i + 1) * W] for i in range(HP)], axis=0)

def left(x):
    hi, lo = split(x)
    return jnp.concatenate([hi, hi, lo, lo], axis=0)

def right(x):
    hi, lo = split(x)
    return twice(jnp.concatenate([hi, lo], axis=1), 0)

def fill(x, rows, cat, tr):
    hi, lo = split(x)
    if cat is not None:
        cat[rows, 0:W] = hi
        cat[rows, W:2 * W] = lo
    if tr is not None:
        hit, lot = split(x.T)
        tr[0:W, rows] = hit
        tr[W:2 * W, rows] = lot

def values_sum(tr, hi, lo):
    a = mm(tr, hi)
    return a[0:W] + a[W:2 * W] + mm(tr[0:W], lo)

def halves(x):
    return x[:, 0:W] + x[:, W:2 * W]

def own_quarter(info, mine_ref, other_ref, c):
    core = info[4]
    a, b = mine_ref[c, 2 * core + info[1]], other_ref[c]
    return jnp.where(core == 0, a, b), jnp.where(core == 0, b, a)

def near_far(u, near, far):
    return jnp.where(u == 0, near[...], far[...])

def own_forward(info, ql_ref, qr_ref, mine_ref, other_ref, p_ref, m_ref, l_ref, ot_ref, kc, vt):
    u = pl.program_id(0)

    @pl.when((u == 0) & (pl.program_id(1) == 0))
    def _():
        for c in range(4):
            k, v = own_quarter(info, mine_ref, other_ref, c)
            fill(k, slice(c * T, (c + 1) * T), kc, None)
            fill(v, slice(c * T, (c + 1) * T), None, vt)

    quarter = jnp.where(u == 0, info[0], 3 - info[0])
    q = left(turned(near_far(u, ql_ref, qr_ref)) * (SCALE * LOG2E))
    s = mm(twice(kc[...], 1), q)
    token = lax.broadcasted_iota(jnp.int32, (BLK, R), 1) & (T - 1)
    ahead = lax.broadcasted_iota(jnp.int32, (BLK, R), 0) - token
    s = jnp.where(ahead <= quarter * T, s, -jnp.inf)
    m = jnp.max(s, axis=0, keepdims=True)
    p = jnp.exp2(s - m)
    p_ref[0] = p
    m_ref[0] = m
    l_ref[0] = jnp.sum(p, axis=0, keepdims=True)
    hi, lo = split(p)
    ot_ref[0] = values_sum(vt[...], hi, lo)

def picked(info, ql_ref, qr_ref, dl_ref, dr_ref, s0, s1, s2, s3,
           m0_ref, l0_ref, ot0_ref, ol_ref, or_ref, dq_ref, c_ref, rd_ref, g0, g1, g2, g3,
           kc, vc, kt, vt, s_sc, phi, plo, dk_acc, dv_acc):
    u, step = pl.program_id(0), pl.program_id(1)

    @pl.when((u == 0) & (step == 0))
    def _():
        for j in range(2):
            for x in range(4):
                rows = slice((j * 4 + x) * T, (j * 4 + x + 1) * T)
                piece = (s0, s1, s2, s3)[x]
                fill(piece[j, info[4]], rows, kc, kt)
                fill(piece[j, 1 - info[4]], rows, vc, vt)
        dk_acc[...] = jnp.zeros_like(dk_acc)
        dv_acc[...] = jnp.zeros_like(dv_acc)

    q = near_far(u, ql_ref, qr_ref) * (SCALE * LOG2E)
    do = near_far(u, dl_ref, dr_ref)
    qt = left(turned(q))
    m0 = m0_ref[0]
    m = m0
    for j in range(2):
        rows = slice(j * BLK, (j + 1) * BLK)
        s = mm(twice(kc[rows, :], 1), qt)
        s = jnp.where(info[2 + j] > 0, s, -jnp.inf)
        s_sc[rows, :] = s
        m = jnp.maximum(m, jnp.max(s, axis=0, keepdims=True))
    shrink = jnp.exp2(m0 - m)
    l = l0_ref[0] * shrink
    ot = ot0_ref[0] * shrink
    for j in range(2):
        rows = slice(j * BLK, (j + 1) * BLK)
        p = jnp.exp2(s_sc[rows, :] - m)
        s_sc[rows, :] = p
        hi, lo = split(p)
        phi[rows, :] = hi
        plo[rows, :] = lo
        l = l + jnp.sum(p, axis=0, keepdims=True)
        ot = ot + values_sum(vt[:, rows], hi, lo)
    inv = 1.0 / l
    ot = ot * inv
    dot = turned(do) * inv
    rd = jnp.sum(dot * ot, axis=0, keepdims=True)
    c_ref[0] = inv * shrink
    rd_ref[0] = rd * shrink
    o = upright(ot)

    @pl.when(u == 0)
    def _():
        ol_ref[...] = o

    @pl.when(u == 1)
    def _():
        or_ref[...] = o

    dt = left(dot)
    d2 = right(stacked(upright(dot)))
    q2 = right(stacked(q))
    dq = jnp.zeros((W, R), F32)
    for j in range(2):
        rows = slice(j * BLK, (j + 1) * BLK)
        dp = mm(twice(vc[rows, :], 1), dt)
        hi, lo = split(s_sc[rows, :] * (dp - rd))
        dq = dq + values_sum(kt[:, rows], hi, lo)
        dv_acc[rows, :] += halves(mm(jnp.concatenate([phi[rows, :], plo[rows, :]], axis=1), d2))
        dk_acc[rows, :] += halves(mm(jnp.concatenate([hi, lo], axis=1), q2))
    dq_ref[0] = dq

    @pl.when((u == 1) & (step == STEPS - 1))
    def _():
        for j in range(2):
            for x, out in enumerate((g0, g1, g2, g3)):
                rows = slice((j * 4 + x) * T, (j * 4 + x + 1) * T)
                out[j, info[4]] = dk_acc[rows, :] * LN2
                out[j, 1 - info[4]] = dv_acc[rows, :]

def own_backward(info, ql_ref, qr_ref, dl_ref, dr_ref, mine_ref, other_ref, p_ref, c_ref, rd_ref, dq_ref,
                 gl_ref, gr_ref, h0, h1, h2, h3, vc, kt, dk_acc, dv_acc):
    u, step = pl.program_id(0), pl.program_id(1)

    @pl.when((u == 0) & (step == 0))
    def _():
        for c in range(4):
            k, v = own_quarter(info, mine_ref, other_ref, c)
            fill(k, slice(c * T, (c + 1) * T), None, kt)
            fill(v, slice(c * T, (c + 1) * T), vc, None)
        dk_acc[...] = jnp.zeros_like(dk_acc)
        dv_acc[...] = jnp.zeros_like(dv_acc)

    q = near_far(u, ql_ref, qr_ref) * (SCALE * LOG2E)
    dot = turned(near_far(u, dl_ref, dr_ref)) * c_ref[0]
    p = p_ref[0]
    hi, lo = split(p)
    dv_acc[...] += halves(mm(jnp.concatenate([hi, lo], axis=1), right(stacked(upright(dot)))))
    dp = mm(twice(vc[...], 1), left(dot))
    hi, lo = split(p * (dp - rd_ref[0]))
    dk_acc[...] += halves(mm(jnp.concatenate([hi, lo], axis=1), right(stacked(q))))
    dq = upright(dq_ref[0] + values_sum(kt[...], hi, lo)) * SCALE

    @pl.when(u == 0)
    def _():
        gl_ref[...] = dq

    @pl.when(u == 1)
    def _():
        gr_ref[...] = dq

    @pl.when((u == 1) & (step == STEPS - 1))
    def _():
        for x, out in enumerate((h0, h1, h2, h3)):
            rows = pl.ds(pl.multiple_of((info[0] ^ x) * T, T), T)
            out[info[4]] = dk_acc[rows, :] * LN2
            out[1 - info[4]] = dv_acc[rows, :]

def tile(shape):
    return pl.BlockSpec((1,) + shape[1:], lambda u, h, i: (u * STEPS + h, 0, 0))

def whole(shape):
    return pl.BlockSpec(shape, lambda u, h, i: (0,) * len(shape))

NEAR = pl.BlockSpec((T, HP * W), lambda u, h, i: (0, i[1] * STEPS + h))
FAR = pl.BlockSpec((T, HP * W), lambda u, h, i: (0, h))
FIRST = pl.BlockSpec((T, HP * W), lambda u, h, i: (0, jnp.where(u == 0, h, STEPS - 1)))
SECOND = pl.BlockSpec((T, HP * W), lambda u, h, i: (0, jnp.where(u == 0, 0, h)))
PROBS, ROW, TURNED = (2 * STEPS, BLK, R), (2 * STEPS, 1, R), (2 * STEPS, W, R)
HALF, PIECE, PAIR = (T, 4 * W), (2, T, W), (2, 2, T, W)

def in_hbm(*arrays):
    return [pltpu.with_memory_space_constraint(a, pltpu.HBM) for a in arrays]

def kernel(body, ins, outs, out_shapes, scratch, flops, limit):
    return pl.pallas_call(
        body,
        out_shape=[pltpu.HBM(s, F32) for s in out_shapes],
        grid_spec=pltpu.PrefetchScalarGridSpec(
            num_scalar_prefetch=1,
            grid=(2, STEPS),
            in_specs=ins,
            out_specs=outs,
            scratch_shapes=[pltpu.VMEM(s, d) for s, d in scratch],
        ),
        compiler_params=pltpu.CompilerParams(
            dimension_semantics=("arbitrary", "arbitrary"), vmem_limit_bytes=limit << 20),
        cost_estimate=pl.CostEstimate(
            flops=flops, transcendentals=0, bytes_accessed=16 << 20),
        name=body.__name__,
    )

UNIT = 2 * 2048 * BLK * W * 4

def call_own_forward(info, q, q_far, mine, other):
    return kernel(
        own_forward,
        [NEAR, FAR, whole(mine.shape), whole(other.shape)],
        [tile(PROBS), tile(ROW), tile(ROW), tile(TURNED)],
        [PROBS, ROW, ROW, TURNED],
        [((BLK, 2 * W), BF), ((2 * W, BLK), BF)],
        2 * UNIT, 30,
    )(info, *in_hbm(q), q_far, *in_hbm(mine), other)

def call_picked(info, q, q_far, do, do_far, pieces, m, l, ot):
    return kernel(
        picked,
        [NEAR, FAR, NEAR, FAR] + [whole(PAIR)] * 4 + [tile(ROW), tile(ROW), tile(TURNED)],
        [FIRST, SECOND, tile(TURNED), tile(ROW), tile(ROW)] + [whole(PAIR)] * 4,
        [HALF, HALF, TURNED, ROW, ROW] + [PAIR] * 4,
        [((2 * BLK, 2 * W), BF), ((2 * BLK, 2 * W), BF), ((2 * W, 2 * BLK), BF), ((2 * W, 2 * BLK), BF),
         ((2 * BLK, R), F32), ((2 * BLK, R), BF), ((2 * BLK, R), BF),
         ((2 * BLK, W), F32), ((2 * BLK, W), F32)],
        10 * UNIT, 52,
    )(info, *in_hbm(q), q_far, *in_hbm(do), do_far, *pieces, *in_hbm(m, l, ot))

def call_own_backward(info, q, q_far, do, do_far, mine, other, p, c, rd, dq):
    return kernel(
        own_backward,
        [NEAR, FAR, NEAR, FAR, whole(mine.shape), whole(other.shape), tile(PROBS), tile(ROW), tile(ROW), tile(TURNED)],
        [FIRST, SECOND] + [whole(PIECE)] * 4,
        [HALF, HALF] + [PIECE] * 4,
        [((BLK, 2 * W), BF), ((2 * W, BLK), BF), ((BLK, W), F32), ((BLK, W), F32)],
        3 * UNIT, 40,
    )(info, *in_hbm(q), q_far, *in_hbm(do), do_far, *in_hbm(mine), other, *in_hbm(p, c, rd, dq))

HEADS = (4, T, W)
SWAP = [(0, 1), (1, 0)]
PLACE = ("y", "x", "head")

def glue(body, args, outs, copies, hbm=False):
    spec = lambda shape: pl.BlockSpec(shape, lambda i: (0,) * len(shape))
    if copies:
        spec = lambda shape: pl.BlockSpec(memory_space=pl.ANY)
    arrays = args[1:]
    return pl.pallas_call(
        body,
        out_shape=[(pltpu.HBM if hbm else jax.ShapeDtypeStruct)(s, F32) for s in outs],
        grid=(1,),
        in_specs=[pl.BlockSpec(memory_space=pltpu.SMEM)] + [spec(a.shape) for a in arrays],
        out_specs=[spec(s) for s in outs],
        scratch_shapes=[pltpu.SemaphoreType.DMA((copies,))] if copies else [],
        compiler_params=pltpu.CompilerParams(
            dimension_semantics=("arbitrary",), vmem_limit_bytes=(4 if copies else 20) << 20),
        cost_estimate=pl.CostEstimate(
            flops=0, transcendentals=0,
            bytes_accessed=4 * sum(math.prod(s) for s in [a.shape for a in arrays] + list(outs))),
        name=body.__name__,
    )(args[0], *arrays)

def copy_all(pairs, sems):
    copies = [pltpu.make_async_copy(a, b, sems.at[n]) for n, (a, b) in enumerate(pairs)]
    for c in copies:
        c.start()
    for c in copies:
        c.wait()

def travel(array, step, stage):
    pairs = []
    for y in range(4):
        for x in range(4):
            for core in range(2):
                ty, tx = (y + step) % 4, x
                if core != stage:
                    ty, tx = y, (x + step) % 4
                pairs.append(((y * 4 + x) * 2 + core, (ty * 4 + tx) * 2 + core))
    return lax.ppermute(array, PLACE, pairs)

def mirror(array, flip):
    return lax.ppermute(array, "z", [(i, i ^ flip) for i in range(4)])

def swap(array):
    return lax.ppermute(array, "head", SWAP)

def after(array, *others):
    return lax.optimization_barrier((array, *others))[0]

def place():
    core, y, x = (lax.axis_index(a) for a in ("head", "y", "x"))
    return core, jnp.where(core == 0, y, x), jnp.where(core == 0, x, y)

def chosen(table, first, second, core, j):
    block = jnp.where(core == 0, first * 4 + second, second * 4 + first)
    other = jnp.maximum(table[block, 1 + j], 0)
    y, x = other // 4, other % 4
    return jnp.where(core == 0, y, x), jnp.where(core == 0, x, y)

def assemble(spot, keys, values, other, full, sems):
    core = spot[0]
    half = T // 2
    here, there = (pl.ds(pl.multiple_of(c * half, half), half) for c in (core, 1 - core))
    for h in range(4):
        cols = slice(h * W, (h + 1) * W)
        for i, ref in enumerate((keys, values)):
            @pl.when(core == i)
            def _(ref=ref, cols=cols, h=h):
                pltpu.make_async_copy(ref.at[:, cols], full.at[h, here], sems.at[h]).start()
        pltpu.make_async_copy(other.at[:, cols], full.at[h, there], sems.at[4 + h]).start()
    for h in range(4):
        cols = slice(h * W, (h + 1) * W)
        pltpu.make_async_copy(keys.at[:, cols], full.at[h, here], sems.at[h]).wait()
        pltpu.make_async_copy(other.at[:, cols], full.at[h, there], sems.at[4 + h]).wait()

def pick(table, *refs):
    core, here, there = place()
    along, out, sems = refs[0:4], refs[4:7], refs[7]
    waits = []
    for step in (1, 2, 3):
        for j in range(2):
            first, _ = chosen(table, here, (there + step) % 4, core, j)
            for i in range(4):
                @pl.when((here - first) % 4 == i)
                def _(source=along[i], target=out[step - 1].at[j], n=len(waits)):
                    pltpu.make_async_copy(source, target, sems.at[n]).start()
            waits.append((along[0], out[step - 1].at[j]))
    for n, (source, target) in enumerate(waits):
        pltpu.make_async_copy(source, target, sems.at[n]).wait()

def join(table, *refs):
    core, here, there = place()
    along, got, (mine, send), sems = refs[0:4], refs[4:7], refs[7:9], refs[9]
    waits = []
    for j in range(2):
        first, second = chosen(table, here, there, core, j)
        near, off = (here - first) % 4, (there - second) % 4
        for c, out in ((core, mine), (1 - core, send)):
            heads, target, n = pl.ds(2 * c, 2), out.at[j], len(waits)
            for k in range(4):
                @pl.when((off == 0) & (near == k))
                def _(source=along[k].at[heads], target=target, n=n):
                    pltpu.make_async_copy(source, target, sems.at[n]).start()
            for k in range(3):
                @pl.when(off == k + 1)
                def _(source=got[k].at[j, heads], target=target, n=n):
                    pltpu.make_async_copy(source, target, sems.at[n]).start()
            waits.append((along[0].at[heads], target))
    for n, (source, target) in enumerate(waits):
        pltpu.make_async_copy(source, target, sems.at[n]).wait()

def arrange(spot, mine, other, same, cross, sems):
    head = spot[1]
    copy_all([(ref.at[j, h], out.at[j, n]) for j in range(2)
              for n, ref in enumerate((mine, other))
              for h, out in ((head, same), (1 - head, cross))], sems)

def spread(spot, mine, added, passed, passed2, keep, send):
    head = spot[1]
    for j in range(mine.shape[0]):
        for n, out in ((0, keep), (1, send)):
            out[j, head] = mine[j, n] + added[j, n]
            out[j, 1 - head] = passed[j, n] + passed2[j, n]

def gather_heads(spot, keep, other, full, sems):
    core = spot[0]
    copy_all([(ref.at[j], full.at[j, pl.ds(2 * c, 2)]) for j in range(2)
              for c, ref in ((core, keep), (1 - core, other))], sems)

def collect(table, *refs):
    core, here, there = place()
    got, out = refs[0:4], refs[4:8]
    for ref in out:
        ref[...] = jnp.zeros_like(ref)
    for step in range(4):
        for j in range(2):
            first, second = chosen(table, here, (there - step) % 4, core, j)
            for i in range(4):
                @pl.when((second == there) & ((here - first) % 4 == i))
                def _(source=got[step], ref=out[i], j=j):
                    ref[...] += source[j]

def shards(queries, keys, values, cotangent, selected):
    core, z = lax.axis_index("head"), lax.axis_index("z")
    head = z // 2
    mine = lax.dynamic_slice(selected, (lax.axis_index("y") * 4 + lax.axis_index("x"), 1), (1, 2))[0]
    info = jnp.concatenate([jnp.stack([z, head]), (mine >= 0).astype(jnp.int32), core[None]])
    spot = jnp.stack([core, head])
    far = 1 - head
    q_far, do_far = (
        mirror(lax.dynamic_slice_in_dim(a, far * 4 * W, 4 * W, 1), 3)
        for a in (queries, cotangent)
    )
    got = swap(jnp.where(core == 0, values, keys))
    (full,) = glue(assemble, (spot, *in_hbm(keys, values), got), (HEADS,), 8)
    own = lax.all_gather(full, "z", axis=0)
    own_other = swap(lax.dynamic_index_in_dim(own, 2 * (1 - core) + head, 1, keepdims=False))

    along = [full] + [travel(full, s, 0) for s in (1, 2, 3)]
    sent = glue(pick, (selected, *along), ((2,) + HEADS,) * 3, 6, hbm=True)
    got = [travel(sent[s - 1], s, 1) for s in (1, 2, 3)]
    kept, send = glue(join, (after(selected, q_far, do_far), *along, *got), (PAIR, PAIR), 4)
    same, cross = glue(arrange, (spot, kept, swap(send)), (PAIR, PAIR), 8)
    pieces = [same] + [mirror(a, flip) for a, flip in ((same, 1), (cross, 2), (cross, 3))]

    p, m, l, ot = call_own_forward(info, queries, q_far, own, own_other)
    out = call_picked(info, queries, q_far, cotangent, do_far, pieces, m, l, ot)
    o_near, o_far, dq, c, rd = out[:5]
    last = call_own_backward(info, queries, q_far, cotangent, do_far, own, own_other, p, c, rd, dq)

    def reduced(g, *others):
        arrived = [g[0]] + [mirror(g[flip], flip) for flip in (1, 2, 3)]
        arrived[3] = after(arrived[3], *others)
        keep, send = glue(spread, (spot, *arrived), (g[0].shape,) * 2, 0)
        return keep, swap(send)

    (terms,) = glue(gather_heads, (spot, *reduced(out[5:9], last[0])), ((2,) + HEADS,), 4)
    arrived = [terms] + [travel(terms, s, 1) for s in (1, 2, 3)]
    o_far, dq_far = mirror(o_far, 3), mirror(last[1], 3)
    sums = glue(collect, (after(selected, o_far, dq_far), *arrived), (HEADS,) * 4, 0)
    low, high = reduced([a[None] for a in last[2:6]])
    total = sums[0] + sum(travel(sums[s], 4 - s, 0) for s in (1, 2, 3))
    total = total + jnp.where(
        core == 0, jnp.concatenate([low[0], high[0]], 0), jnp.concatenate([high[0], low[0]], 0)
    )

    half = T // 2

    def tokens(which):
        a = lax.dynamic_slice_in_dim(total, which * half, half, 1)
        return jnp.concatenate([a[h] for h in range(4)], 1)

    keep, back = tokens(core), swap(tokens(1 - core))

    def sides(a, b):
        return jnp.where(head == 0, jnp.concatenate([a, b], 1), jnp.concatenate([b, a], 1))

    return (
        sides(o_near, o_far),
        sides(last[0], dq_far),
        jnp.where(core == 0, keep, back),
        jnp.where(core == 0, back, keep),
    )

def solution(mesh):
    grid = Mesh(mesh.devices.reshape(4, 4, 4, 2), ("y", "x", "z", "head"))
    tokens = ("y", "x", "z")
    wide, narrow = P(tokens, "head"), P(tokens + ("head",), None)
    return jax.shard_map(
        shards,
        mesh=grid,
        in_specs=(wide, narrow, narrow, wide, P()),
        out_specs=(wide, wide, narrow, narrow),
        check_vma=False,
    )
```

```python
import math

import jax
import jax.numpy as jnp
from jax import lax
from jax.experimental import pallas as pl
from jax.experimental.pallas import tpu as pltpu
from jax.sharding import Mesh, PartitionSpec as P

W = 128
T = 256

SCALE = 1.0 / math.sqrt(W)
LOG2E = math.log2(math.e)
LN2 = math.log(2.0)
BF = jnp.bfloat16
F32 = jnp.float32
BLK = 4 * T
HP = 2
STEPS = 4 // HP
R = HP * T

def split(x):
    hi = x.astype(BF)
    return hi, (x - hi.astype(F32)).astype(BF)

def twice(x, axis):
    return jnp.concatenate([x, x], axis=axis)

def mm(a, b):
    return lax.dot_general(a, b, (((1,), (0,)), ((), ())), preferred_element_type=F32)

def turned(x):
    return jnp.concatenate([x[:, i * W:(i + 1) * W].T for i in range(HP)], axis=1)

def upright(x):
    return jnp.concatenate([x[:, i * T:(i + 1) * T].T for i in range(HP)], axis=1)

def stacked(x):
    return jnp.concatenate([x[:, i * W:(i + 1) * W] for i in range(HP)], axis=0)

def left(x):
    hi, lo = split(x)
    return jnp.concatenate([hi, hi, lo, lo], axis=0)

def right(x):
    hi, lo = split(x)
    return twice(jnp.concatenate([hi, lo], axis=1), 0)

def fill(x, rows, cat, tr):
    hi, lo = split(x)
    if cat is not None:
        cat[rows, 0:W] = hi
        cat[rows, W:2 * W] = lo
    if tr is not None:
        hit, lot = split(x.T)
        tr[0:W, rows] = hit
        tr[W:2 * W, rows] = lot

def values_sum(tr, hi, lo):
    a = mm(tr, hi)
    return a[0:W] + a[W:2 * W] + mm(tr[0:W], lo)

def halves(x):
    return x[:, 0:W] + x[:, W:2 * W]

def own_quarter(info, mine_ref, other_ref, c):
    core = info[4]
    a, b = mine_ref[c, 2 * core + info[1]], other_ref[c]
    return jnp.where(core == 0, a, b), jnp.where(core == 0, b, a)

def near_far(u, near, far):
    return jnp.where(u == 0, near[...], far[...])

def own_forward(info, ql_ref, qr_ref, mine_ref, other_ref, p_ref, m_ref, l_ref, ot_ref, kc, vt):
    u = pl.program_id(0)

    @pl.when((u == 0) & (pl.program_id(1) == 0))
    def _():
        for c in range(4):
            k, v = own_quarter(info, mine_ref, other_ref, c)
            fill(k, slice(c * T, (c + 1) * T), kc, None)
            fill(v, slice(c * T, (c + 1) * T), None, vt)

    quarter = jnp.where(u == 0, info[0], 3 - info[0])
    q = left(turned(near_far(u, ql_ref, qr_ref)) * (SCALE * LOG2E))
    s = mm(twice(kc[...], 1), q)
    token = lax.broadcasted_iota(jnp.int32, (BLK, R), 1) & (T - 1)
    ahead = lax.broadcasted_iota(jnp.int32, (BLK, R), 0) - token
    s = jnp.where(ahead <= quarter * T, s, -jnp.inf)
    m = jnp.max(s, axis=0, keepdims=True)
    p = jnp.exp2(s - m)
    p_ref[0] = p
    m_ref[0] = m
    l_ref[0] = jnp.sum(p, axis=0, keepdims=True)
    hi, lo = split(p)
    ot_ref[0] = values_sum(vt[...], hi, lo)

def picked(info, ql_ref, qr_ref, dl_ref, dr_ref, s0, s1, s2, s3,
           m0_ref, l0_ref, ot0_ref, ol_ref, or_ref, dq_ref, c_ref, rd_ref, g0, g1, g2, g3,
           kc, vc, kt, vt, s_sc, phi, plo, dk_acc, dv_acc):
    u, step = pl.program_id(0), pl.program_id(1)

    @pl.when((u == 0) & (step == 0))
    def _():
        for j in range(2):
            for x in range(4):
                rows = slice((j * 4 + x) * T, (j * 4 + x + 1) * T)
                piece = (s0, s1, s2, s3)[x]
                fill(piece[j, info[4]], rows, kc, kt)
                fill(piece[j, 1 - info[4]], rows, vc, vt)
        dk_acc[...] = jnp.zeros_like(dk_acc)
        dv_acc[...] = jnp.zeros_like(dv_acc)

    q = near_far(u, ql_ref, qr_ref) * (SCALE * LOG2E)
    do = near_far(u, dl_ref, dr_ref)
    qt = left(turned(q))
    m0 = m0_ref[0]
    m = m0
    for j in range(2):
        rows = slice(j * BLK, (j + 1) * BLK)
        s = mm(twice(kc[rows, :], 1), qt)
        s = jnp.where(info[2 + j] > 0, s, -jnp.inf)
        s_sc[rows, :] = s
        m = jnp.maximum(m, jnp.max(s, axis=0, keepdims=True))
    shrink = jnp.exp2(m0 - m)
    l = l0_ref[0] * shrink
    ot = ot0_ref[0] * shrink
    for j in range(2):
        rows = slice(j * BLK, (j + 1) * BLK)
        p = jnp.exp2(s_sc[rows, :] - m)
        s_sc[rows, :] = p
        hi, lo = split(p)
        phi[rows, :] = hi
        plo[rows, :] = lo
        l = l + jnp.sum(p, axis=0, keepdims=True)
        ot = ot + values_sum(vt[:, rows], hi, lo)
    inv = 1.0 / l
    ot = ot * inv
    dot = turned(do) * inv
    rd = jnp.sum(dot * ot, axis=0, keepdims=True)
    c_ref[0] = inv * shrink
    rd_ref[0] = rd * shrink
    o = upright(ot)

    @pl.when(u == 0)
    def _():
        ol_ref[...] = o

    @pl.when(u == 1)
    def _():
        or_ref[...] = o

    dt = left(dot)
    d2 = right(stacked(upright(dot)))
    q2 = right(stacked(q))
    dq = jnp.zeros((W, R), F32)
    for j in range(2):
        rows = slice(j * BLK, (j + 1) * BLK)
        dp = mm(twice(vc[rows, :], 1), dt)
        hi, lo = split(s_sc[rows, :] * (dp - rd))
        dq = dq + values_sum(kt[:, rows], hi, lo)
        dv_acc[rows, :] += halves(mm(jnp.concatenate([phi[rows, :], plo[rows, :]], axis=1), d2))
        dk_acc[rows, :] += halves(mm(jnp.concatenate([hi, lo], axis=1), q2))
    dq_ref[0] = dq

    @pl.when((u == 1) & (step == STEPS - 1))
    def _():
        for j in range(2):
            for x, out in enumerate((g0, g1, g2, g3)):
                rows = slice((j * 4 + x) * T, (j * 4 + x + 1) * T)
                out[j, info[4]] = dk_acc[rows, :] * LN2
                out[j, 1 - info[4]] = dv_acc[rows, :]

def own_backward(info, ql_ref, qr_ref, dl_ref, dr_ref, mine_ref, other_ref, p_ref, c_ref, rd_ref, dq_ref,
                 gl_ref, gr_ref, h0, h1, h2, h3, vc, kt, dk_acc, dv_acc):
    u, step = pl.program_id(0), pl.program_id(1)

    @pl.when((u == 0) & (step == 0))
    def _():
        for c in range(4):
            k, v = own_quarter(info, mine_ref, other_ref, c)
            fill(k, slice(c * T, (c + 1) * T), None, kt)
            fill(v, slice(c * T, (c + 1) * T), vc, None)
        dk_acc[...] = jnp.zeros_like(dk_acc)
        dv_acc[...] = jnp.zeros_like(dv_acc)

    q = near_far(u, ql_ref, qr_ref) * (SCALE * LOG2E)
    dot = turned(near_far(u, dl_ref, dr_ref)) * c_ref[0]
    p = p_ref[0]
    hi, lo = split(p)
    dv_acc[...] += halves(mm(jnp.concatenate([hi, lo], axis=1), right(stacked(upright(dot)))))
    dp = mm(twice(vc[...], 1), left(dot))
    hi, lo = split(p * (dp - rd_ref[0]))
    dk_acc[...] += halves(mm(jnp.concatenate([hi, lo], axis=1), right(stacked(q))))
    dq = upright(dq_ref[0] + values_sum(kt[...], hi, lo)) * SCALE

    @pl.when(u == 0)
    def _():
        gl_ref[...] = dq

    @pl.when(u == 1)
    def _():
        gr_ref[...] = dq

    @pl.when((u == 1) & (step == STEPS - 1))
    def _():
        for x, out in enumerate((h0, h1, h2, h3)):
            rows = pl.ds(pl.multiple_of((info[0] ^ x) * T, T), T)
            out[info[4]] = dk_acc[rows, :] * LN2
            out[1 - info[4]] = dv_acc[rows, :]

def tile(shape):
    return pl.BlockSpec((1,) + shape[1:], lambda u, h, i: (u * STEPS + h, 0, 0))

def whole(shape):
    return pl.BlockSpec(shape, lambda u, h, i: (0,) * len(shape))

NEAR = pl.BlockSpec((T, HP * W), lambda u, h, i: (0, i[1] * STEPS + h))
FAR = pl.BlockSpec((T, HP * W), lambda u, h, i: (0, h))
FIRST = pl.BlockSpec((T, HP * W), lambda u, h, i: (0, jnp.where(u == 0, h, STEPS - 1)))
SECOND = pl.BlockSpec((T, HP * W), lambda u, h, i: (0, jnp.where(u == 0, 0, h)))
PROBS, ROW, TURNED = (2 * STEPS, BLK, R), (2 * STEPS, 1, R), (2 * STEPS, W, R)
HALF, PIECE, PAIR = (T, 4 * W), (2, T, W), (2, 2, T, W)

def in_hbm(*arrays):
    return [pltpu.with_memory_space_constraint(a, pltpu.HBM) for a in arrays]

def kernel(body, ins, outs, out_shapes, scratch, flops, limit):
    return pl.pallas_call(
        body,
        out_shape=[pltpu.HBM(s, F32) for s in out_shapes],
        grid_spec=pltpu.PrefetchScalarGridSpec(
            num_scalar_prefetch=1,
            grid=(2, STEPS),
            in_specs=ins,
            out_specs=outs,
            scratch_shapes=[pltpu.VMEM(s, d) for s, d in scratch],
        ),
        compiler_params=pltpu.CompilerParams(
            dimension_semantics=("arbitrary", "arbitrary"), vmem_limit_bytes=limit << 20),
        cost_estimate=pl.CostEstimate(
            flops=flops, transcendentals=0, bytes_accessed=16 << 20),
        name=body.__name__,
    )

UNIT = 2 * 2048 * BLK * W * 4

def call_own_forward(info, q, q_far, mine, other):
    return kernel(
        own_forward,
        [NEAR, FAR, whole(mine.shape), whole(other.shape)],
        [tile(PROBS), tile(ROW), tile(ROW), tile(TURNED)],
        [PROBS, ROW, ROW, TURNED],
        [((BLK, 2 * W), BF), ((2 * W, BLK), BF)],
        2 * UNIT, 30,
    )(info, *in_hbm(q), q_far, *in_hbm(mine), other)

def call_picked(info, q, q_far, do, do_far, pieces, m, l, ot):
    return kernel(
        picked,
        [NEAR, FAR, NEAR, FAR] + [whole(PAIR)] * 4 + [tile(ROW), tile(ROW), tile(TURNED)],
        [FIRST, SECOND, tile(TURNED), tile(ROW), tile(ROW)] + [whole(PAIR)] * 4,
        [HALF, HALF, TURNED, ROW, ROW] + [PAIR] * 4,
        [((2 * BLK, 2 * W), BF), ((2 * BLK, 2 * W), BF), ((2 * W, 2 * BLK), BF), ((2 * W, 2 * BLK), BF),
         ((2 * BLK, R), F32), ((2 * BLK, R), BF), ((2 * BLK, R), BF),
         ((2 * BLK, W), F32), ((2 * BLK, W), F32)],
        10 * UNIT, 52,
    )(info, *in_hbm(q), q_far, *in_hbm(do), do_far, *pieces, *in_hbm(m, l, ot))

def call_own_backward(info, q, q_far, do, do_far, mine, other, p, c, rd, dq):
    return kernel(
        own_backward,
        [NEAR, FAR, NEAR, FAR, whole(mine.shape), whole(other.shape), tile(PROBS), tile(ROW), tile(ROW), tile(TURNED)],
        [FIRST, SECOND] + [whole(PIECE)] * 4,
        [HALF, HALF] + [PIECE] * 4,
        [((BLK, 2 * W), BF), ((2 * W, BLK), BF), ((BLK, W), F32), ((BLK, W), F32)],
        3 * UNIT, 40,
    )(info, *in_hbm(q), q_far, *in_hbm(do), do_far, *in_hbm(mine), other, *in_hbm(p, c, rd, dq))

HEADS = (4, T, W)
SWAP = [(0, 1), (1, 0)]
PLACE = ("y", "x", "head")

def glue(body, args, outs):
    spec = lambda shape: pl.BlockSpec(shape, lambda i: (0,) * len(shape))
    arrays = args[1:]
    return pl.pallas_call(
        body,
        out_shape=[jax.ShapeDtypeStruct(s, F32) for s in outs],
        grid=(1,),
        in_specs=[pl.BlockSpec(memory_space=pltpu.SMEM)] + [spec(a.shape) for a in arrays],
        out_specs=[spec(s) for s in outs],
        compiler_params=pltpu.CompilerParams(
            dimension_semantics=("arbitrary",), vmem_limit_bytes=20 << 20),
        cost_estimate=pl.CostEstimate(
            flops=0, transcendentals=0,
            bytes_accessed=4 * sum(math.prod(s) for s in [a.shape for a in arrays] + list(outs))),
        name=body.__name__,
    )(args[0], *arrays)

def travel(array, step, stage):
    pairs = []
    for y in range(4):
        for x in range(4):
            for core in range(2):
                ty, tx = (y + step) % 4, x
                if core != stage:
                    ty, tx = y, (x + step) % 4
                pairs.append(((y * 4 + x) * 2 + core, (ty * 4 + tx) * 2 + core))
    return lax.ppermute(array, PLACE, pairs)

def mirror(array, flip):
    return lax.ppermute(array, "z", [(i, i ^ flip) for i in range(4)])

def swap(array):
    return lax.ppermute(array, "head", SWAP)

def after(array, *others):
    return lax.optimization_barrier((array, *others))[0]

def place():
    core, y, x = (lax.axis_index(a) for a in ("head", "y", "x"))
    return core, jnp.where(core == 0, y, x), jnp.where(core == 0, x, y)

def chosen(table, first, second, core, j):
    block = jnp.where(core == 0, first * 4 + second, second * 4 + first)
    other = jnp.maximum(table[block, 1 + j], 0)
    y, x = other // 4, other % 4
    return jnp.where(core == 0, y, x), jnp.where(core == 0, x, y)

def assemble(spot, keys, values, other, full):
    core = spot[0]
    half = T // 2
    here, there = (pl.ds(pl.multiple_of(c * half, half), half) for c in (core, 1 - core))
    for h in range(4):
        cols = slice(h * W, (h + 1) * W)
        full[h, here] = jnp.where(core == 0, keys[:, cols], values[:, cols])
        full[h, there] = other[:, cols]

def pick(table, *refs):
    core, here, there = place()
    along, out = refs[0:4], refs[4:7]
    for step in (1, 2, 3):
        for j in range(2):
            first, _ = chosen(table, here, (there + step) % 4, core, j)
            for i in range(4):
                @pl.when((here - first) % 4 == i)
                def _(source=along[i], ref=out[step - 1], j=j):
                    ref[j] = source[...]

def join(table, *refs):
    core, here, there = place()
    along, got, (mine, send) = refs[0:4], refs[4:7], refs[7:9]
    for j in range(2):
        first, second = chosen(table, here, there, core, j)
        near, off = (here - first) % 4, (there - second) % 4
        for c, out in ((core, mine), (1 - core, send)):
            heads = pl.ds(2 * c, 2)
            for k in range(4):
                @pl.when((off == 0) & (near == k))
                def _(source=along[k], out=out, heads=heads, j=j):
                    out[j] = source[heads]
            for k in range(3):
                @pl.when(off == k + 1)
                def _(source=got[k], out=out, heads=heads, j=j):
                    out[j] = source[j, heads]

def arrange(spot, mine, other, same, cross):
    head = spot[1]
    for j in range(2):
        for n, ref in enumerate((mine, other)):
            same[j, n] = ref[j, head]
            cross[j, n] = ref[j, 1 - head]

def spread(spot, mine, added, passed, passed2, keep, send):
    head = spot[1]
    for j in range(mine.shape[0]):
        for n, out in ((0, keep), (1, send)):
            out[j, head] = mine[j, n] + added[j, n]
            out[j, 1 - head] = passed[j, n] + passed2[j, n]

def gather_heads(spot, keep, other, full):
    core = spot[0]
    for j in range(2):
        full[j, pl.ds(2 * core, 2)] = keep[j]
        full[j, pl.ds(2 * (1 - core), 2)] = other[j]

def collect(table, *refs):
    core, here, there = place()
    got, out = refs[0:4], refs[4:8]
    for ref in out:
        ref[...] = jnp.zeros_like(ref)
    for step in range(4):
        for j in range(2):
            first, second = chosen(table, here, (there - step) % 4, core, j)
            for i in range(4):
                @pl.when((second == there) & ((here - first) % 4 == i))
                def _(source=got[step], ref=out[i], j=j):
                    ref[...] += source[j]

def shards(queries, keys, values, cotangent, selected):
    core, z = lax.axis_index("head"), lax.axis_index("z")
    head = z // 2
    mine = lax.dynamic_slice(selected, (lax.axis_index("y") * 4 + lax.axis_index("x"), 1), (1, 2))[0]
    info = jnp.concatenate([jnp.stack([z, head]), (mine >= 0).astype(jnp.int32), core[None]])
    spot = jnp.stack([core, head])
    far = 1 - head
    q_far, do_far = (
        mirror(lax.dynamic_slice_in_dim(a, far * 4 * W, 4 * W, 1), 3)
        for a in (queries, cotangent)
    )
    got = swap(jnp.where(core == 0, values, keys))
    (full,) = glue(assemble, (spot, *in_hbm(keys, values), got), (HEADS,))
    own = lax.all_gather(full, "z", axis=0)
    own_other = swap(lax.dynamic_index_in_dim(own, 2 * (1 - core) + head, 1, keepdims=False))

    along = [full] + [travel(full, s, 0) for s in (1, 2, 3)]
    sent = glue(pick, (selected, *along), ((2,) + HEADS,) * 3)
    got = [travel(sent[s - 1], s, 1) for s in (1, 2, 3)]
    kept, send = glue(join, (after(selected, q_far, do_far), *along, *got), (PAIR, PAIR))
    same, cross = glue(arrange, (spot, kept, swap(send)), (PAIR, PAIR))
    pieces = [same] + [mirror(a, flip) for a, flip in ((same, 1), (cross, 2), (cross, 3))]

    p, m, l, ot = call_own_forward(info, queries, q_far, own, own_other)
    out = call_picked(info, queries, q_far, cotangent, do_far, pieces, m, l, ot)
    o_near, o_far, dq, c, rd = out[:5]
    last = call_own_backward(info, queries, q_far, cotangent, do_far, own, own_other, p, c, rd, dq)

    def reduced(g, *others):
        arrived = [g[0]] + [mirror(g[flip], flip) for flip in (1, 2, 3)]
        arrived[3] = after(arrived[3], *others)
        keep, send = glue(spread, (spot, *arrived), (g[0].shape,) * 2)
        return keep, swap(send)

    (terms,) = glue(gather_heads, (spot, *reduced(out[5:9], last[0])), ((2,) + HEADS,))
    arrived = [terms] + [travel(terms, s, 1) for s in (1, 2, 3)]
    o_far, dq_far = mirror(o_far, 3), mirror(last[1], 3)
    sums = glue(collect, (after(selected, o_far), *arrived), (HEADS,) * 4)
    low, high = reduced([a[None] for a in last[2:6]], dq_far)
    total = sums[0] + sum(travel(sums[s], 4 - s, 0) for s in (1, 2, 3))
    total = total + jnp.where(
        core == 0, jnp.concatenate([low[0], high[0]], 0), jnp.concatenate([high[0], low[0]], 0)
    )

    half = T // 2

    def tokens(which):
        a = lax.dynamic_slice_in_dim(total, which * half, half, 1)
        return jnp.concatenate([a[h] for h in range(4)], 1)

    keep, back = tokens(core), swap(tokens(1 - core))

    def sides(a, b):
        return jnp.where(head == 0, jnp.concatenate([a, b], 1), jnp.concatenate([b, a], 1))

    return (
        sides(o_near, o_far),
        sides(last[0], dq_far),
        jnp.where(core == 0, keep, back),
        jnp.where(core == 0, back, keep),
    )

def solution(mesh):
    grid = Mesh(mesh.devices.reshape(4, 4, 4, 2), ("y", "x", "z", "head"))
    tokens = ("y", "x", "z")
    wide, narrow = P(tokens, "head"), P(tokens + ("head",), None)
    return jax.shard_map(
        shards,
        mesh=grid,
        in_specs=(wide, narrow, narrow, wide, P()),
        out_specs=(wide, wide, narrow, narrow),
        check_vma=False,
    )
```

```python
import math

import jax
import jax.numpy as jnp
from jax import lax
from jax.experimental import pallas as pl
from jax.experimental.pallas import tpu as pltpu
from jax.sharding import Mesh, PartitionSpec as P

W = 128
T = 256

SCALE = 1.0 / math.sqrt(W)
LOG2E = math.log2(math.e)
LN2 = math.log(2.0)
BF = jnp.bfloat16
F32 = jnp.float32
BLK = 4 * T
HP = 2
STEPS = 4 // HP
R = HP * T

def split(x):
    hi = x.astype(BF)
    return hi, (x - hi.astype(F32)).astype(BF)

def twice(x, axis):
    return jnp.concatenate([x, x], axis=axis)

def mm(a, b):
    return lax.dot_general(a, b, (((1,), (0,)), ((), ())), preferred_element_type=F32)

def turned(x):
    return jnp.concatenate([x[:, i * W:(i + 1) * W].T for i in range(HP)], axis=1)

def upright(x):
    return jnp.concatenate([x[:, i * T:(i + 1) * T].T for i in range(HP)], axis=1)

def stacked(x):
    return jnp.concatenate([x[:, i * W:(i + 1) * W] for i in range(HP)], axis=0)

def left(x):
    hi, lo = split(x)
    return jnp.concatenate([hi, hi, lo, lo], axis=0)

def right(x):
    hi, lo = split(x)
    return twice(jnp.concatenate([hi, lo], axis=1), 0)

def fill(x, rows, cat, tr):
    hi, lo = split(x)
    if cat is not None:
        cat[rows, 0:W] = hi
        cat[rows, W:2 * W] = lo
    if tr is not None:
        hit, lot = split(x.T)
        tr[0:W, rows] = hit
        tr[W:2 * W, rows] = lot

def values_sum(tr, hi, lo):
    a = mm(tr, hi)
    return a[0:W] + a[W:2 * W] + mm(tr[0:W], lo)

def halves(x):
    return x[:, 0:W] + x[:, W:2 * W]

def own_quarter(info, mine_ref, other_ref, c):
    core = info[4]
    a, b = mine_ref[c, 2 * core + info[1]], other_ref[c]
    return jnp.where(core == 0, a, b), jnp.where(core == 0, b, a)

def near_far(u, near, far):
    return jnp.where(u == 0, near[...], far[...])

def own_forward(info, ql_ref, qr_ref, mine_ref, other_ref, p_ref, m_ref, l_ref, ot_ref, kc, vt):
    u = pl.program_id(0)

    @pl.when((u == 0) & (pl.program_id(1) == 0))
    def _():
        for c in range(4):
            k, v = own_quarter(info, mine_ref, other_ref, c)
            fill(k, slice(c * T, (c + 1) * T), kc, None)
            fill(v, slice(c * T, (c + 1) * T), None, vt)

    quarter = jnp.where(u == 0, info[0], 3 - info[0])
    q = left(turned(near_far(u, ql_ref, qr_ref)) * (SCALE * LOG2E))
    s = mm(twice(kc[...], 1), q)
    token = lax.broadcasted_iota(jnp.int32, (BLK, R), 1) & (T - 1)
    ahead = lax.broadcasted_iota(jnp.int32, (BLK, R), 0) - token
    s = jnp.where(ahead <= quarter * T, s, -jnp.inf)
    m = jnp.max(s, axis=0, keepdims=True)
    p = jnp.exp2(s - m)
    p_ref[0] = p
    m_ref[0] = m
    l_ref[0] = jnp.sum(p, axis=0, keepdims=True)
    hi, lo = split(p)
    ot_ref[0] = values_sum(vt[...], hi, lo)

def picked(info, ql_ref, qr_ref, dl_ref, dr_ref, s0, s1, s2, s3,
           m0_ref, l0_ref, ot0_ref, ol_ref, or_ref, dq_ref, c_ref, rd_ref, g0, g1, g2, g3,
           kc, vc, kt, vt, s_sc, dk_acc, dv_acc):
    u, step = pl.program_id(0), pl.program_id(1)

    @pl.when((u == 0) & (step == 0))
    def _():
        for j in range(2):
            for x in range(4):
                rows = slice((j * 4 + x) * T, (j * 4 + x + 1) * T)
                piece = (s0, s1, s2, s3)[x]
                fill(piece[j, info[4]], rows, kc, kt)
                fill(piece[j, 1 - info[4]], rows, vc, vt)
        dk_acc[...] = jnp.zeros_like(dk_acc)
        dv_acc[...] = jnp.zeros_like(dv_acc)

    q = near_far(u, ql_ref, qr_ref) * (SCALE * LOG2E)
    do = near_far(u, dl_ref, dr_ref)
    qt = left(turned(q))
    m0 = m0_ref[0]
    m = m0
    for j in range(2):
        rows = slice(j * BLK, (j + 1) * BLK)
        s = mm(twice(kc[rows, :], 1), qt)
        s = jnp.where(info[2 + j] > 0, s, -jnp.inf)
        s_sc[rows, :] = s
        m = jnp.maximum(m, jnp.max(s, axis=0, keepdims=True))
    shrink = jnp.exp2(m0 - m)
    l = l0_ref[0] * shrink
    ot = ot0_ref[0] * shrink
    for j in range(2):
        rows = slice(j * BLK, (j + 1) * BLK)
        p = jnp.exp2(s_sc[rows, :] - m)
        s_sc[rows, :] = p
        hi, lo = split(p)
        l = l + jnp.sum(p, axis=0, keepdims=True)
        ot = ot + values_sum(vt[:, rows], hi, lo)
    inv = 1.0 / l
    ot = ot * inv
    dot = turned(do) * inv
    rd = jnp.sum(dot * ot, axis=0, keepdims=True)
    c_ref[0] = inv * shrink
    rd_ref[0] = rd * shrink
    o = upright(ot)

    @pl.when(u == 0)
    def _():
        ol_ref[...] = o

    @pl.when(u == 1)
    def _():
        or_ref[...] = o

    dt = left(dot)
    d2 = right(stacked(upright(dot)))
    q2 = right(stacked(q))
    dq = jnp.zeros((W, R), F32)
    for j in range(2):
        rows = slice(j * BLK, (j + 1) * BLK)
        p = s_sc[rows, :]
        p2 = jnp.concatenate(split(p), axis=1)
        dp = mm(twice(vc[rows, :], 1), dt)
        hi, lo = split(p * (dp - rd))
        dq = dq + values_sum(kt[:, rows], hi, lo)
        dv_acc[rows, :] += halves(mm(p2, d2))
        dk_acc[rows, :] += halves(mm(jnp.concatenate([hi, lo], axis=1), q2))
    dq_ref[0] = dq

    @pl.when((u == 1) & (step == STEPS - 1))
    def _():
        for j in range(2):
            for x, out in enumerate((g0, g1, g2, g3)):
                rows = slice((j * 4 + x) * T, (j * 4 + x + 1) * T)
                out[j, info[4]] = dk_acc[rows, :] * LN2
                out[j, 1 - info[4]] = dv_acc[rows, :]

def own_backward(info, ql_ref, qr_ref, dl_ref, dr_ref, mine_ref, other_ref, p_ref, c_ref, rd_ref, dq_ref,
                 gl_ref, gr_ref, h0, h1, h2, h3, vc, kt, dk_acc, dv_acc):
    u, step = pl.program_id(0), pl.program_id(1)

    @pl.when((u == 0) & (step == 0))
    def _():
        for c in range(4):
            k, v = own_quarter(info, mine_ref, other_ref, c)
            fill(k, slice(c * T, (c + 1) * T), None, kt)
            fill(v, slice(c * T, (c + 1) * T), vc, None)
        dk_acc[...] = jnp.zeros_like(dk_acc)
        dv_acc[...] = jnp.zeros_like(dv_acc)

    q = near_far(u, ql_ref, qr_ref) * (SCALE * LOG2E)
    dot = turned(near_far(u, dl_ref, dr_ref)) * c_ref[0]
    p = p_ref[0]
    hi, lo = split(p)
    dv_acc[...] += halves(mm(jnp.concatenate([hi, lo], axis=1), right(stacked(upright(dot)))))
    dp = mm(twice(vc[...], 1), left(dot))
    hi, lo = split(p * (dp - rd_ref[0]))
    dk_acc[...] += halves(mm(jnp.concatenate([hi, lo], axis=1), right(stacked(q))))
    dq = upright(dq_ref[0] + values_sum(kt[...], hi, lo)) * SCALE

    @pl.when(u == 0)
    def _():
        gl_ref[...] = dq

    @pl.when(u == 1)
    def _():
        gr_ref[...] = dq

    @pl.when((u == 1) & (step == STEPS - 1))
    def _():
        for x, out in enumerate((h0, h1, h2, h3)):
            rows = pl.ds(pl.multiple_of((info[0] ^ x) * T, T), T)
            out[info[4]] = dk_acc[rows, :] * LN2
            out[1 - info[4]] = dv_acc[rows, :]

def tile(shape):
    return pl.BlockSpec((1,) + shape[1:], lambda u, h, i: (u * STEPS + h, 0, 0))

def whole(shape):
    return pl.BlockSpec(shape, lambda u, h, i: (0,) * len(shape))

NEAR = pl.BlockSpec((T, HP * W), lambda u, h, i: (0, i[1] * STEPS + h))
FAR = pl.BlockSpec((T, HP * W), lambda u, h, i: (0, h))
FIRST = pl.BlockSpec((T, HP * W), lambda u, h, i: (0, jnp.where(u == 0, h, STEPS - 1)))
SECOND = pl.BlockSpec((T, HP * W), lambda u, h, i: (0, jnp.where(u == 0, 0, h)))
PROBS, ROW, TURNED = (2 * STEPS, BLK, R), (2 * STEPS, 1, R), (2 * STEPS, W, R)
HALF, PIECE, PAIR = (T, 4 * W), (2, T, W), (2, 2, T, W)

def in_hbm(*arrays):
    return [pltpu.with_memory_space_constraint(a, pltpu.HBM) for a in arrays]

def kernel(body, ins, outs, out_shapes, scratch, flops, limit):
    return pl.pallas_call(
        body,
        out_shape=[pltpu.HBM(s, F32) for s in out_shapes],
        grid_spec=pltpu.PrefetchScalarGridSpec(
            num_scalar_prefetch=1,
            grid=(2, STEPS),
            in_specs=ins,
            out_specs=outs,
            scratch_shapes=[pltpu.VMEM(s, d) for s, d in scratch],
        ),
        compiler_params=pltpu.CompilerParams(
            dimension_semantics=("arbitrary", "arbitrary"), vmem_limit_bytes=limit << 20),
        cost_estimate=pl.CostEstimate(
            flops=flops, transcendentals=0, bytes_accessed=16 << 20),
        name=body.__name__,
    )

UNIT = 2 * 2048 * BLK * W * 4

def call_own_forward(info, q, q_far, mine, other):
    return kernel(
        own_forward,
        [NEAR, FAR, whole(mine.shape), whole(other.shape)],
        [tile(PROBS), tile(ROW), tile(ROW), tile(TURNED)],
        [PROBS, ROW, ROW, TURNED],
        [((BLK, 2 * W), BF), ((2 * W, BLK), BF)],
        2 * UNIT, 30,
    )(info, *in_hbm(q), q_far, *in_hbm(mine), other)

def call_picked(info, q, q_far, do, do_far, pieces, m, l, ot):
    return kernel(
        picked,
        [NEAR, FAR, NEAR, FAR] + [whole(PAIR)] * 4 + [tile(ROW), tile(ROW), tile(TURNED)],
        [FIRST, SECOND, tile(TURNED), tile(ROW), tile(ROW)] + [whole(PAIR)] * 4,
        [HALF, HALF, TURNED, ROW, ROW] + [PAIR] * 4,
        [((2 * BLK, 2 * W), BF), ((2 * BLK, 2 * W), BF), ((2 * W, 2 * BLK), BF), ((2 * W, 2 * BLK), BF),
         ((2 * BLK, R), F32),
         ((2 * BLK, W), F32), ((2 * BLK, W), F32)],
        10 * UNIT, 52,
    )(info, *in_hbm(q), q_far, *in_hbm(do), do_far, *pieces, *in_hbm(m, l, ot))

def call_own_backward(info, q, q_far, do, do_far, mine, other, p, c, rd, dq):
    return kernel(
        own_backward,
        [NEAR, FAR, NEAR, FAR, whole(mine.shape), whole(other.shape), tile(PROBS), tile(ROW), tile(ROW), tile(TURNED)],
        [FIRST, SECOND] + [whole(PIECE)] * 4,
        [HALF, HALF] + [PIECE] * 4,
        [((BLK, 2 * W), BF), ((2 * W, BLK), BF), ((BLK, W), F32), ((BLK, W), F32)],
        3 * UNIT, 40,
    )(info, *in_hbm(q), q_far, *in_hbm(do), do_far, *in_hbm(mine), other, *in_hbm(p, c, rd, dq))

HEADS = (4, T, W)
SWAP = [(0, 1), (1, 0)]
PLACE = ("y", "x", "head")

def glue(body, args, outs):
    spec = lambda shape: pl.BlockSpec(shape, lambda i: (0,) * len(shape))
    arrays = args[1:]
    return pl.pallas_call(
        body,
        out_shape=[jax.ShapeDtypeStruct(s, F32) for s in outs],
        grid=(1,),
        in_specs=[pl.BlockSpec(memory_space=pltpu.SMEM)] + [spec(a.shape) for a in arrays],
        out_specs=[spec(s) for s in outs],
        compiler_params=pltpu.CompilerParams(
            dimension_semantics=("arbitrary",), vmem_limit_bytes=20 << 20),
        cost_estimate=pl.CostEstimate(
            flops=0, transcendentals=0,
            bytes_accessed=4 * sum(math.prod(s) for s in [a.shape for a in arrays] + list(outs))),
        name=body.__name__,
    )(args[0], *arrays)

def travel(array, step, stage):
    pairs = []
    for y in range(4):
        for x in range(4):
            for core in range(2):
                ty, tx = (y + step) % 4, x
                if core != stage:
                    ty, tx = y, (x + step) % 4
                pairs.append(((y * 4 + x) * 2 + core, (ty * 4 + tx) * 2 + core))
    return lax.ppermute(array, PLACE, pairs)

def mirror(array, flip):
    return lax.ppermute(array, "z", [(i, i ^ flip) for i in range(4)])

def swap(array):
    return lax.ppermute(array, "head", SWAP)

def after(array, *others):
    return lax.optimization_barrier((array, *others))[0]

def place():
    core, y, x = (lax.axis_index(a) for a in ("head", "y", "x"))
    return core, jnp.where(core == 0, y, x), jnp.where(core == 0, x, y)

def chosen(table, first, second, core, j):
    block = jnp.where(core == 0, first * 4 + second, second * 4 + first)
    other = jnp.maximum(table[block, 1 + j], 0)
    y, x = other // 4, other % 4
    return jnp.where(core == 0, y, x), jnp.where(core == 0, x, y)

def assemble(spot, keys, values, other, full):
    core = spot[0]
    half = T // 2
    here, there = (pl.ds(pl.multiple_of(c * half, half), half) for c in (core, 1 - core))
    for h in range(4):
        cols = slice(h * W, (h + 1) * W)
        full[h, here] = jnp.where(core == 0, keys[:, cols], values[:, cols])
        full[h, there] = other[:, cols]

def pick(table, *refs):
    core, here, there = place()
    along, out = refs[0:4], refs[4:7]
    for step in (1, 2, 3):
        for j in range(2):
            first, _ = chosen(table, here, (there + step) % 4, core, j)
            for i in range(4):
                @pl.when((here - first) % 4 == i)
                def _(source=along[i], ref=out[step - 1], j=j):
                    ref[j] = source[...]

def join(table, *refs):
    core, here, there = place()
    along, got, (mine, send) = refs[0:4], refs[4:7], refs[7:9]
    for j in range(2):
        first, second = chosen(table, here, there, core, j)
        near, off = (here - first) % 4, (there - second) % 4
        for c, out in ((core, mine), (1 - core, send)):
            heads = pl.ds(2 * c, 2)
            for k in range(4):
                @pl.when((off == 0) & (near == k))
                def _(source=along[k], out=out, heads=heads, j=j):
                    out[j] = source[heads]
            for k in range(3):
                @pl.when(off == k + 1)
                def _(source=got[k], out=out, heads=heads, j=j):
                    out[j] = source[j, heads]

def arrange(spot, mine, other, same, cross):
    head = spot[1]
    for j in range(2):
        for n, ref in enumerate((mine, other)):
            same[j, n] = ref[j, head]
            cross[j, n] = ref[j, 1 - head]

def spread(spot, mine, added, passed, passed2, keep, send):
    head = spot[1]
    for j in range(mine.shape[0]):
        for n, out in ((0, keep), (1, send)):
            out[j, head] = mine[j, n] + added[j, n]
            out[j, 1 - head] = passed[j, n] + passed2[j, n]

def gather_heads(spot, keep, other, full):
    core = spot[0]
    for j in range(2):
        full[j, pl.ds(2 * core, 2)] = keep[j]
        full[j, pl.ds(2 * (1 - core), 2)] = other[j]

def collect(table, *refs):
    core, here, there = place()
    got, out = refs[0:4], refs[4:8]
    for ref in out:
        ref[...] = jnp.zeros_like(ref)
    for step in range(4):
        for j in range(2):
            first, second = chosen(table, here, (there - step) % 4, core, j)
            for i in range(4):
                @pl.when((second == there) & ((here - first) % 4 == i))
                def _(source=got[step], ref=out[i], j=j):
                    ref[...] += source[j]

def shards(queries, keys, values, cotangent, selected):
    core, z = lax.axis_index("head"), lax.axis_index("z")
    head = z // 2
    mine = lax.dynamic_slice(selected, (lax.axis_index("y") * 4 + lax.axis_index("x"), 1), (1, 2))[0]
    info = jnp.concatenate([jnp.stack([z, head]), (mine >= 0).astype(jnp.int32), core[None]])
    spot = jnp.stack([core, head])
    far = 1 - head
    got = swap(jnp.where(core == 0, values, keys))
    (full,) = glue(assemble, (spot, *in_hbm(keys, values), got), (HEADS,))
    own = lax.all_gather(full, "z", axis=0)
    own_other = swap(lax.dynamic_index_in_dim(own, 2 * (1 - core) + head, 1, keepdims=False))

    along = [full] + [travel(full, s, 0) for s in (1, 2, 3)]

    def turned_over(array, *others):
        return mirror(lax.dynamic_slice_in_dim(after(array, *others), far * 4 * W, 4 * W, 1), 3)

    q_far = turned_over(queries, along[1])
    do_far = turned_over(cotangent, q_far)
    sent = glue(pick, (selected, *along), ((2,) + HEADS,) * 3)
    got = [travel(sent[s - 1], s, 1) for s in (1, 2, 3)]
    kept, send = glue(join, (after(selected, q_far, do_far), *along, *got), (PAIR, PAIR))
    same, cross = glue(arrange, (spot, kept, swap(send)), (PAIR, PAIR))
    pieces = [same] + [mirror(a, flip) for a, flip in ((same, 1), (cross, 2), (cross, 3))]

    p, m, l, ot = call_own_forward(info, queries, q_far, own, own_other)
    out = call_picked(info, queries, q_far, cotangent, do_far, pieces, m, l, ot)
    o_near, o_far, dq, c, rd = out[:5]
    last = call_own_backward(info, queries, q_far, cotangent, do_far, own, own_other, p, c, rd, dq)

    def reduced(g, *others):
        arrived = [g[0]] + [mirror(g[flip], flip) for flip in (1, 2, 3)]
        arrived[3] = after(arrived[3], *others)
        keep, send = glue(spread, (spot, *arrived), (g[0].shape,) * 2)
        return keep, swap(send)

    (terms,) = glue(gather_heads, (spot, *reduced(out[5:9], last[0])), ((2,) + HEADS,))
    arrived = [terms] + [travel(terms, s, 1) for s in (1, 2, 3)]
    o_far, dq_far = mirror(o_far, 3), mirror(last[1], 3)
    low, high = reduced([a[None] for a in last[2:6]])
    sums = glue(collect, (after(selected, o_far, low), *arrived), (HEADS,) * 4)
    total = after(sums[0], dq_far) + sum(travel(sums[s], 4 - s, 0) for s in (1, 2, 3))
    total = total + jnp.where(
        core == 0, jnp.concatenate([low[0], high[0]], 0), jnp.concatenate([high[0], low[0]], 0)
    )

    half = T // 2

    def tokens(which):
        a = lax.dynamic_slice_in_dim(total, which * half, half, 1)
        return jnp.concatenate([a[h] for h in range(4)], 1)

    keep, back = tokens(core), swap(tokens(1 - core))

    def sides(a, b):
        return jnp.where(head == 0, jnp.concatenate([a, b], 1), jnp.concatenate([b, a], 1))

    return (
        sides(o_near, o_far),
        sides(last[0], dq_far),
        jnp.where(core == 0, keep, back),
        jnp.where(core == 0, back, keep),
    )

def solution(mesh):
    grid = Mesh(mesh.devices.reshape(4, 4, 4, 2), ("y", "x", "z", "head"))
    tokens = ("y", "x", "z")
    wide, narrow = P(tokens, "head"), P(tokens + ("head",), None)
    return jax.shard_map(
        shards,
        mesh=grid,
        in_specs=(wide, narrow, narrow, wide, P()),
        out_specs=(wide, wide, narrow, narrow),
        check_vma=False,
    )
```

```python
import math

import jax
import jax.numpy as jnp
from jax import lax
from jax.experimental import pallas as pl
from jax.experimental.pallas import tpu as pltpu
from jax.sharding import Mesh, PartitionSpec as P

W = 128
T = 256

SCALE = 1.0 / math.sqrt(W)
LOG2E = math.log2(math.e)
LN2 = math.log(2.0)
BF = jnp.bfloat16
F32 = jnp.float32
BLK = 4 * T
HP = 2
STEPS = 4 // HP
R = HP * T

def split(x):
    hi = x.astype(BF)
    return hi, (x - hi.astype(F32)).astype(BF)

def twice(x, axis):
    return jnp.concatenate([x, x], axis=axis)

def mm(a, b):
    return lax.dot_general(a, b, (((1,), (0,)), ((), ())), preferred_element_type=F32)

def turned(x):
    return jnp.concatenate([x[:, i * W:(i + 1) * W].T for i in range(HP)], axis=1)

def upright(x):
    return jnp.concatenate([x[:, i * T:(i + 1) * T].T for i in range(HP)], axis=1)

def stacked(x):
    return jnp.concatenate([x[:, i * W:(i + 1) * W] for i in range(HP)], axis=0)

def left(x):
    hi, lo = split(x)
    return jnp.concatenate([hi, hi, lo, lo], axis=0)

def right(x):
    hi, lo = split(x)
    return twice(jnp.concatenate([hi, lo], axis=1), 0)

def fill(x, rows, cat, tr):
    hi, lo = split(x)
    if cat is not None:
        cat[rows, 0:W] = hi
        cat[rows, W:2 * W] = lo
    if tr is not None:
        hit, lot = split(x.T)
        tr[0:W, rows] = hit
        tr[W:2 * W, rows] = lot

def values_sum(tr, hi, lo):
    a = mm(tr, hi)
    return a[0:W] + a[W:2 * W] + mm(tr[0:W], lo)

def halves(x):
    return x[:, 0:W] + x[:, W:2 * W]

def own_quarter(info, mine_ref, other_ref, c):
    core = info[4]
    a, b = mine_ref[c, 2 * core + info[1]], other_ref[c]
    return jnp.where(core == 0, a, b), jnp.where(core == 0, b, a)

def near_far(u, near, far):
    return jnp.where(u == 0, near[...], far[...])

def own_forward(info, ql_ref, qr_ref, mine_ref, other_ref, p_ref, m_ref, l_ref, ot_ref, kc, vt):
    u = pl.program_id(0)

    @pl.when((u == 0) & (pl.program_id(1) == 0))
    def _():
        for c in range(4):
            k, v = own_quarter(info, mine_ref, other_ref, c)
            fill(k, slice(c * T, (c + 1) * T), kc, None)
            fill(v, slice(c * T, (c + 1) * T), None, vt)

    quarter = jnp.where(u == 0, info[0], 3 - info[0])
    q = left(turned(near_far(u, ql_ref, qr_ref)) * (SCALE * LOG2E))
    s = mm(twice(kc[...], 1), q)
    token = lax.broadcasted_iota(jnp.int32, (BLK, R), 1) & (T - 1)
    ahead = lax.broadcasted_iota(jnp.int32, (BLK, R), 0) - token
    s = jnp.where(ahead <= quarter * T, s, -jnp.inf)
    m = jnp.max(s, axis=0, keepdims=True)
    p = jnp.exp2(s - m)
    p_ref[0] = p
    m_ref[0] = m
    l_ref[0] = jnp.sum(p, axis=0, keepdims=True)
    hi, lo = split(p)
    ot_ref[0] = values_sum(vt[...], hi, lo)

def picked(info, ql_ref, qr_ref, dl_ref, dr_ref, s0, s1, s2, s3,
           m0_ref, l0_ref, ot0_ref, ol_ref, or_ref, dq_ref, c_ref, rd_ref, g0, g1, g2, g3,
           kc, vc, kt, vt, s_sc, dk_acc, dv_acc):
    u, step = pl.program_id(0), pl.program_id(1)

    @pl.when((u == 0) & (step == 0))
    def _():
        for j in range(2):
            for x in range(4):
                rows = slice((j * 4 + x) * T, (j * 4 + x + 1) * T)
                piece = (s0, s1, s2, s3)[x]
                fill(piece[j, info[4]], rows, kc, kt)
                fill(piece[j, 1 - info[4]], rows, vc, vt)
        dk_acc[...] = jnp.zeros_like(dk_acc)
        dv_acc[...] = jnp.zeros_like(dv_acc)

    q = near_far(u, ql_ref, qr_ref) * (SCALE * LOG2E)
    do = near_far(u, dl_ref, dr_ref)
    qt = left(turned(q))
    m0 = m0_ref[0]
    m = m0
    for j in range(2):
        rows = slice(j * BLK, (j + 1) * BLK)
        s = mm(twice(kc[rows, :], 1), qt)
        s = jnp.where(info[2 + j] > 0, s, -jnp.inf)
        s_sc[rows, :] = s
        m = jnp.maximum(m, jnp.max(s, axis=0, keepdims=True))
    shrink = jnp.exp2(m0 - m)
    l = l0_ref[0] * shrink
    ot = ot0_ref[0] * shrink
    for j in range(2):
        rows = slice(j * BLK, (j + 1) * BLK)
        p = jnp.exp2(s_sc[rows, :] - m)
        s_sc[rows, :] = p
        hi, lo = split(p)
        l = l + jnp.sum(p, axis=0, keepdims=True)
        ot = ot + values_sum(vt[:, rows], hi, lo)
    inv = 1.0 / l
    ot = ot * inv
    dot = turned(do) * inv
    rd = jnp.sum(dot * ot, axis=0, keepdims=True)
    c_ref[0] = inv * shrink
    rd_ref[0] = rd * shrink
    o = upright(ot)

    @pl.when(u == 0)
    def _():
        ol_ref[...] = o

    @pl.when(u == 1)
    def _():
        or_ref[...] = o

    dt = left(dot)
    d2 = right(stacked(upright(dot)))
    q2 = right(stacked(q))
    dq = jnp.zeros((W, R), F32)
    for j in range(2):
        rows = slice(j * BLK, (j + 1) * BLK)
        p = s_sc[rows, :]
        p2 = jnp.concatenate(split(p), axis=1)
        dp = mm(twice(vc[rows, :], 1), dt)
        hi, lo = split(p * (dp - rd))
        dq = dq + values_sum(kt[:, rows], hi, lo)
        dv_acc[rows, :] += halves(mm(p2, d2))
        dk_acc[rows, :] += halves(mm(jnp.concatenate([hi, lo], axis=1), q2))
    dq_ref[0] = dq

    @pl.when((u == 1) & (step == STEPS - 1))
    def _():
        for j in range(2):
            for x, out in enumerate((g0, g1, g2, g3)):
                rows = slice((j * 4 + x) * T, (j * 4 + x + 1) * T)
                out[j, info[4]] = dk_acc[rows, :] * LN2
                out[j, 1 - info[4]] = dv_acc[rows, :]

def own_backward(info, ql_ref, qr_ref, dl_ref, dr_ref, mine_ref, other_ref, p_ref, c_ref, rd_ref, dq_ref,
                 of_ref, gl_ref, far_ref, h0, h1, h2, h3, vc, kt, dk_acc, dv_acc):
    u, step = pl.program_id(0), pl.program_id(1)

    @pl.when((u == 0) & (step == 0))
    def _():
        for c in range(4):
            k, v = own_quarter(info, mine_ref, other_ref, c)
            fill(k, slice(c * T, (c + 1) * T), None, kt)
            fill(v, slice(c * T, (c + 1) * T), vc, None)
        dk_acc[...] = jnp.zeros_like(dk_acc)
        dv_acc[...] = jnp.zeros_like(dv_acc)

    q = near_far(u, ql_ref, qr_ref) * (SCALE * LOG2E)
    dot = turned(near_far(u, dl_ref, dr_ref)) * c_ref[0]
    p = p_ref[0]
    hi, lo = split(p)
    dv_acc[...] += halves(mm(jnp.concatenate([hi, lo], axis=1), right(stacked(upright(dot)))))
    dp = mm(twice(vc[...], 1), left(dot))
    hi, lo = split(p * (dp - rd_ref[0]))
    dk_acc[...] += halves(mm(jnp.concatenate([hi, lo], axis=1), right(stacked(q))))
    dq = upright(dq_ref[0] + values_sum(kt[...], hi, lo)) * SCALE

    @pl.when(u == 0)
    def _():
        gl_ref[...] = dq

    @pl.when(u == 1)
    def _():
        far_ref[0] = of_ref[...]
        far_ref[1] = dq

    @pl.when((u == 1) & (step == STEPS - 1))
    def _():
        for x, out in enumerate((h0, h1, h2, h3)):
            rows = pl.ds(pl.multiple_of((info[0] ^ x) * T, T), T)
            out[info[4]] = dk_acc[rows, :] * LN2
            out[1 - info[4]] = dv_acc[rows, :]

def tile(shape):
    return pl.BlockSpec((1,) + shape[1:], lambda u, h, i: (u * STEPS + h, 0, 0))

def whole(shape):
    return pl.BlockSpec(shape, lambda u, h, i: (0,) * len(shape))

NEAR = pl.BlockSpec((T, HP * W), lambda u, h, i: (0, i[1] * STEPS + h))
FAR, FAR2 = (pl.BlockSpec((None, T, HP * W), lambda u, h, i, n=n: (n, 0, h)) for n in range(2))
FIRST = pl.BlockSpec((T, HP * W), lambda u, h, i: (0, jnp.where(u == 0, h, STEPS - 1)))
SECOND = pl.BlockSpec((T, HP * W), lambda u, h, i: (0, jnp.where(u == 0, 0, h)))
BOTH = pl.BlockSpec((2, T, HP * W), lambda u, h, i: (0, 0, jnp.where(u == 0, 0, h)))
PROBS, ROW, TURNED = (2 * STEPS, BLK, R), (2 * STEPS, 1, R), (2 * STEPS, W, R)
HALF, PIECE, PAIR = (T, 4 * W), (2, T, W), (2, 2, T, W)

def in_hbm(*arrays):
    return [pltpu.with_memory_space_constraint(a, pltpu.HBM) for a in arrays]

def kernel(body, ins, outs, out_shapes, scratch, flops, limit):
    return pl.pallas_call(
        body,
        out_shape=[pltpu.HBM(s, F32) for s in out_shapes],
        grid_spec=pltpu.PrefetchScalarGridSpec(
            num_scalar_prefetch=1,
            grid=(2, STEPS),
            in_specs=ins,
            out_specs=outs,
            scratch_shapes=[pltpu.VMEM(s, d) for s, d in scratch],
        ),
        compiler_params=pltpu.CompilerParams(
            dimension_semantics=("arbitrary", "arbitrary"), vmem_limit_bytes=limit << 20),
        cost_estimate=pl.CostEstimate(
            flops=flops, transcendentals=0, bytes_accessed=16 << 20),
        name=body.__name__,
    )

UNIT = 2 * 2048 * BLK * W * 4

def call_own_forward(info, q, qd_far, mine, other):
    return kernel(
        own_forward,
        [NEAR, FAR, whole(mine.shape), whole(other.shape)],
        [tile(PROBS), tile(ROW), tile(ROW), tile(TURNED)],
        [PROBS, ROW, ROW, TURNED],
        [((BLK, 2 * W), BF), ((2 * W, BLK), BF)],
        2 * UNIT, 30,
    )(info, *in_hbm(q), qd_far, *in_hbm(mine), other)

def call_picked(info, q, do, qd_far, pieces, m, l, ot):
    return kernel(
        picked,
        [NEAR, FAR, NEAR, FAR2] + [whole(PAIR)] * 4 + [tile(ROW), tile(ROW), tile(TURNED)],
        [FIRST, SECOND, tile(TURNED), tile(ROW), tile(ROW)] + [whole(PAIR)] * 4,
        [HALF, HALF, TURNED, ROW, ROW] + [PAIR] * 4,
        [((2 * BLK, 2 * W), BF), ((2 * BLK, 2 * W), BF), ((2 * W, 2 * BLK), BF), ((2 * W, 2 * BLK), BF),
         ((2 * BLK, R), F32),
         ((2 * BLK, W), F32), ((2 * BLK, W), F32)],
        10 * UNIT, 52,
    )(info, *in_hbm(q), qd_far, *in_hbm(do), qd_far, *pieces, *in_hbm(m, l, ot))

def call_own_backward(info, q, do, qd_far, mine, other, p, c, rd, dq, o_far):
    return kernel(
        own_backward,
        [NEAR, FAR, NEAR, FAR2, whole(mine.shape), whole(other.shape), tile(PROBS), tile(ROW), tile(ROW),
         tile(TURNED), SECOND],
        [FIRST, BOTH] + [whole(PIECE)] * 4,
        [HALF, (2,) + HALF] + [PIECE] * 4,
        [((BLK, 2 * W), BF), ((2 * W, BLK), BF), ((BLK, W), F32), ((BLK, W), F32)],
        3 * UNIT, 40,
    )(info, *in_hbm(q), qd_far, *in_hbm(do), qd_far, *in_hbm(mine), other, *in_hbm(p, c, rd, dq, o_far))

HEADS = (4, T, W)
SWAP = [(0, 1), (1, 0)]
PLACE = ("y", "x", "head")

def glue(body, args, outs):
    spec = lambda shape: pl.BlockSpec(shape, lambda i: (0,) * len(shape))
    arrays = args[1:]
    return pl.pallas_call(
        body,
        out_shape=[jax.ShapeDtypeStruct(s, F32) for s in outs],
        grid=(1,),
        in_specs=[pl.BlockSpec(memory_space=pltpu.SMEM)] + [spec(a.shape) for a in arrays],
        out_specs=[spec(s) for s in outs],
        compiler_params=pltpu.CompilerParams(
            dimension_semantics=("arbitrary",), vmem_limit_bytes=20 << 20),
        cost_estimate=pl.CostEstimate(
            flops=0, transcendentals=0,
            bytes_accessed=4 * sum(math.prod(s) for s in [a.shape for a in arrays] + list(outs))),
        name=body.__name__,
    )(args[0], *arrays)

def travel(array, step, stage):
    pairs = []
    for y in range(4):
        for x in range(4):
            for core in range(2):
                ty, tx = (y + step) % 4, x
                if core != stage:
                    ty, tx = y, (x + step) % 4
                pairs.append(((y * 4 + x) * 2 + core, (ty * 4 + tx) * 2 + core))
    return lax.ppermute(array, PLACE, pairs)

def mirror(array, flip):
    return lax.ppermute(array, "z", [(i, i ^ flip) for i in range(4)])

def swap(array):
    return lax.ppermute(array, "head", SWAP)

def after(array, *others):
    return lax.optimization_barrier((array, *others))[0]

def place():
    core, y, x = (lax.axis_index(a) for a in ("head", "y", "x"))
    return core, jnp.where(core == 0, y, x), jnp.where(core == 0, x, y)

def chosen(table, first, second, core, j):
    block = jnp.where(core == 0, first * 4 + second, second * 4 + first)
    other = jnp.maximum(table[block, 1 + j], 0)
    y, x = other // 4, other % 4
    return jnp.where(core == 0, y, x), jnp.where(core == 0, x, y)

def assemble(spot, keys, values, other, full):
    core = spot[0]
    half = T // 2
    here, there = (pl.ds(pl.multiple_of(c * half, half), half) for c in (core, 1 - core))
    for h in range(4):
        cols = slice(h * W, (h + 1) * W)
        full[h, here] = jnp.where(core == 0, keys[:, cols], values[:, cols])
        full[h, there] = other[:, cols]

def pick(table, *refs):
    core, here, there = place()
    along, out = refs[0:4], refs[4:7]
    for step in (1, 2, 3):
        for j in range(2):
            first, _ = chosen(table, here, (there + step) % 4, core, j)
            for i in range(4):
                @pl.when((here - first) % 4 == i)
                def _(source=along[i], ref=out[step - 1], j=j):
                    ref[j] = source[...]

def join(table, *refs):
    core, here, there = place()
    along, got, (mine, send) = refs[0:4], refs[4:7], refs[7:9]
    for j in range(2):
        first, second = chosen(table, here, there, core, j)
        near, off = (here - first) % 4, (there - second) % 4
        for c, out in ((core, mine), (1 - core, send)):
            heads = pl.ds(2 * c, 2)
            for k in range(4):
                @pl.when((off == 0) & (near == k))
                def _(source=along[k], out=out, heads=heads, j=j):
                    out[j] = source[heads]
            for k in range(3):
                @pl.when(off == k + 1)
                def _(source=got[k], out=out, heads=heads, j=j):
                    out[j] = source[j, heads]

def arrange(spot, mine, other, same, cross):
    head = spot[1]
    for j in range(2):
        for n, ref in enumerate((mine, other)):
            same[j, n] = ref[j, head]
            cross[j, n] = ref[j, 1 - head]

def spread(spot, mine, added, passed, passed2, keep, send):
    head = spot[1]
    for j in range(mine.shape[0]):
        for n, out in ((0, keep), (1, send)):
            out[j, head] = mine[j, n] + added[j, n]
            out[j, 1 - head] = passed[j, n] + passed2[j, n]

def gather_heads(spot, keep, other, full):
    core = spot[0]
    for j in range(2):
        full[j, pl.ds(2 * core, 2)] = keep[j]
        full[j, pl.ds(2 * (1 - core), 2)] = other[j]

def collect(table, *refs):
    core, here, there = place()
    got, out = refs[0:4], refs[4:8]
    for ref in out:
        ref[...] = jnp.zeros_like(ref)
    for step in range(4):
        for j in range(2):
            first, second = chosen(table, here, (there - step) % 4, core, j)
            for i in range(4):
                @pl.when((second == there) & ((here - first) % 4 == i))
                def _(source=got[step], ref=out[i], j=j):
                    ref[...] += source[j]

def shards(queries, keys, values, cotangent, selected):
    core, z = lax.axis_index("head"), lax.axis_index("z")
    head = z // 2
    mine = lax.dynamic_slice(selected, (lax.axis_index("y") * 4 + lax.axis_index("x"), 1), (1, 2))[0]
    info = jnp.concatenate([jnp.stack([z, head]), (mine >= 0).astype(jnp.int32), core[None]])
    spot = jnp.stack([core, head])
    far = 1 - head
    got = swap(jnp.where(core == 0, values, keys))
    (full,) = glue(assemble, (spot, *in_hbm(keys, values), got), (HEADS,))
    own = lax.all_gather(full, "z", axis=0)
    own_other = swap(lax.dynamic_index_in_dim(own, 2 * (1 - core) + head, 1, keepdims=False))

    along = [full] + [travel(full, s, 0) for s in (1, 2, 3)]

    queries_late, cotangent_late = lax.optimization_barrier((queries, cotangent, along[1]))[:2]
    qd_far = mirror(
        jnp.stack([lax.dynamic_slice_in_dim(a, far * 4 * W, 4 * W, 1)
                   for a in (queries_late, cotangent_late)]), 3)
    sent = glue(pick, (selected, *along), ((2,) + HEADS,) * 3)
    got = [travel(sent[s - 1], s, 1) for s in (1, 2, 3)]
    kept, send = glue(join, (after(selected, qd_far), *along, *got), (PAIR, PAIR))
    same, cross = glue(arrange, (spot, kept, swap(send)), (PAIR, PAIR))
    pieces = [same] + [mirror(a, flip) for a, flip in ((same, 1), (cross, 2), (cross, 3))]

    p, m, l, ot = call_own_forward(info, queries, qd_far, own, own_other)
    out = call_picked(info, queries, cotangent, qd_far, pieces, m, l, ot)
    o_near, o_far, dq, c, rd = out[:5]
    last = call_own_backward(
        info, queries, cotangent, qd_far, own, own_other, p, c, rd, dq, o_far)

    def reduced(g, *others):
        arrived = [g[0]] + [mirror(g[flip], flip) for flip in (1, 2, 3)]
        arrived[3] = after(arrived[3], *others)
        keep, send = glue(spread, (spot, *arrived), (g[0].shape,) * 2)
        return keep, swap(send)

    (terms,) = glue(gather_heads, (spot, *reduced(out[5:9], last[0])), ((2,) + HEADS,))
    arrived = [terms] + [travel(terms, s, 1) for s in (1, 2, 3)]
    back_far = mirror(last[1], 3)
    low, high = reduced([a[None] for a in last[2:6]])
    sums = glue(collect, (after(selected, low), *arrived), (HEADS,) * 4)
    total = after(sums[0], back_far) + sum(travel(sums[s], 4 - s, 0) for s in (1, 2, 3))
    total = total + jnp.where(
        core == 0, jnp.concatenate([low[0], high[0]], 0), jnp.concatenate([high[0], low[0]], 0)
    )

    half = T // 2

    def tokens(which):
        a = lax.dynamic_slice_in_dim(total, which * half, half, 1)
        return jnp.concatenate([a[h] for h in range(4)], 1)

    keep, back = tokens(core), swap(tokens(1 - core))

    def sides(a, b):
        return jnp.where(head == 0, jnp.concatenate([a, b], 1), jnp.concatenate([b, a], 1))

    return (
        sides(o_near, back_far[0]),
        sides(last[0], back_far[1]),
        jnp.where(core == 0, keep, back),
        jnp.where(core == 0, back, keep),
    )

def solution(mesh):
    grid = Mesh(mesh.devices.reshape(4, 4, 4, 2), ("y", "x", "z", "head"))
    tokens = ("y", "x", "z")
    wide, narrow = P(tokens, "head"), P(tokens + ("head",), None)
    return jax.shard_map(
        shards,
        mesh=grid,
        in_specs=(wide, narrow, narrow, wide, P()),
        out_specs=(wide, wide, narrow, narrow),
        check_vma=False,
    )
```

```python
import math

import jax
import jax.numpy as jnp
from jax import lax
from jax.experimental import pallas as pl
from jax.experimental.pallas import tpu as pltpu
from jax.sharding import Mesh, PartitionSpec as P

W = 128
T = 256

SCALE = 1.0 / math.sqrt(W)
LOG2E = math.log2(math.e)
LN2 = math.log(2.0)
BF = jnp.bfloat16
F32 = jnp.float32
BLK = 4 * T
HP = 2
STEPS = 4 // HP
R = HP * T

def split(x):
    hi = x.astype(BF)
    return hi, (x - hi.astype(F32)).astype(BF)

def twice(x, axis):
    return jnp.concatenate([x, x], axis=axis)

def mm(a, b):
    return lax.dot_general(a, b, (((1,), (0,)), ((), ())), preferred_element_type=F32)

def turned(x):
    return jnp.concatenate([x[:, i * W:(i + 1) * W].T for i in range(HP)], axis=1)

def upright(x):
    return jnp.concatenate([x[:, i * T:(i + 1) * T].T for i in range(HP)], axis=1)

def stacked(x):
    return jnp.concatenate([x[:, i * W:(i + 1) * W] for i in range(HP)], axis=0)

def left(x):
    hi, lo = split(x)
    return jnp.concatenate([hi, hi, lo, lo], axis=0)

def right(x):
    hi, lo = split(x)
    return twice(jnp.concatenate([hi, lo], axis=1), 0)

def fill(x, rows, cat, tr):
    hi, lo = split(x)
    if cat is not None:
        cat[rows, 0:W] = hi
        cat[rows, W:2 * W] = lo
    if tr is not None:
        hit, lot = split(x.T)
        tr[0:W, rows] = hit
        tr[W:2 * W, rows] = lot

def values_sum(tr, hi, lo):
    a = mm(tr, hi)
    return a[0:W] + a[W:2 * W] + mm(tr[0:W], lo)

def halves(x):
    return x[:, 0:W] + x[:, W:2 * W]

def own_quarter(info, mine_ref, other_ref, c):
    core = info[4]
    a, b = mine_ref[c, 2 * core + info[1]], other_ref[c]
    return jnp.where(core == 0, a, b), jnp.where(core == 0, b, a)

def near_far(u, near, far):
    return jnp.where(u == 0, near[...], far[...])

def own_forward(info, ql_ref, qr_ref, mine_ref, other_ref, p_ref, m_ref, l_ref, ot_ref, kc, vt):
    u = pl.program_id(0)

    @pl.when((u == 0) & (pl.program_id(1) == 0))
    def _():
        for c in range(4):
            k, v = own_quarter(info, mine_ref, other_ref, c)
            fill(k, slice(c * T, (c + 1) * T), kc, None)
            fill(v, slice(c * T, (c + 1) * T), None, vt)

    quarter = jnp.where(u == 0, info[0], 3 - info[0])
    q = left(turned(near_far(u, ql_ref, qr_ref)) * (SCALE * LOG2E))
    s = mm(twice(kc[...], 1), q)
    token = lax.broadcasted_iota(jnp.int32, (BLK, R), 1) & (T - 1)
    ahead = lax.broadcasted_iota(jnp.int32, (BLK, R), 0) - token
    s = jnp.where(ahead <= quarter * T, s, -jnp.inf)
    m = jnp.max(s, axis=0, keepdims=True)
    p = jnp.exp2(s - m)
    p_ref[0] = p
    m_ref[0] = m
    l_ref[0] = jnp.sum(p, axis=0, keepdims=True)
    hi, lo = split(p)
    ot_ref[0] = values_sum(vt[...], hi, lo)

def picked(info, ql_ref, qr_ref, dl_ref, dr_ref, s0, s1, s2, s3,
           m0_ref, l0_ref, ot0_ref, ol_ref, or_ref, dq_ref, c_ref, rd_ref, g0, g1, g2, g3,
           kc, vc, kt, vt, s_sc, dk_acc, dv_acc):
    u, step = pl.program_id(0), pl.program_id(1)

    @pl.when((u == 0) & (step == 0))
    def _():
        for j in range(2):
            for x in range(4):
                rows = slice((j * 4 + x) * T, (j * 4 + x + 1) * T)
                piece = (s0, s1, s2, s3)[x]
                fill(piece[j, info[4]], rows, kc, kt)
                fill(piece[j, 1 - info[4]], rows, vc, vt)
        dk_acc[...] = jnp.zeros_like(dk_acc)
        dv_acc[...] = jnp.zeros_like(dv_acc)

    q = near_far(u, ql_ref, qr_ref) * (SCALE * LOG2E)
    do = near_far(u, dl_ref, dr_ref)
    qt = left(turned(q))
    m0 = m0_ref[0]
    m = m0
    for j in range(2):
        rows = slice(j * BLK, (j + 1) * BLK)
        s = mm(twice(kc[rows, :], 1), qt)
        s = jnp.where(info[2 + j] > 0, s, -jnp.inf)
        s_sc[rows, :] = s
        m = jnp.maximum(m, jnp.max(s, axis=0, keepdims=True))
    shrink = jnp.exp2(m0 - m)
    l = l0_ref[0] * shrink
    ot = ot0_ref[0] * shrink
    for j in range(2):
        rows = slice(j * BLK, (j + 1) * BLK)
        p = jnp.exp2(s_sc[rows, :] - m)
        s_sc[rows, :] = p
        hi, lo = split(p)
        l = l + jnp.sum(p, axis=0, keepdims=True)
        ot = ot + values_sum(vt[:, rows], hi, lo)
    inv = 1.0 / l
    ot = ot * inv
    dot = turned(do) * inv
    rd = jnp.sum(dot * ot, axis=0, keepdims=True)
    c_ref[0] = inv * shrink
    rd_ref[0] = rd * shrink
    o = upright(ot)

    @pl.when(u == 0)
    def _():
        ol_ref[...] = o

    @pl.when(u == 1)
    def _():
        or_ref[...] = o

    dt = left(dot)
    d2 = right(stacked(upright(dot)))
    q2 = right(stacked(q))
    dq = jnp.zeros((W, R), F32)
    for j in range(2):
        rows = slice(j * BLK, (j + 1) * BLK)
        p = s_sc[rows, :]
        p2 = jnp.concatenate(split(p), axis=1)
        dp = mm(twice(vc[rows, :], 1), dt)
        hi, lo = split(p * (dp - rd))
        dq = dq + values_sum(kt[:, rows], hi, lo)
        dv_acc[rows, :] += halves(mm(p2, d2))
        dk_acc[rows, :] += halves(mm(jnp.concatenate([hi, lo], axis=1), q2))
    dq_ref[0] = dq

    @pl.when((u == 1) & (step == STEPS - 1))
    def _():
        for j in range(2):
            for x, out in enumerate((g0, g1, g2, g3)):
                rows = slice((j * 4 + x) * T, (j * 4 + x + 1) * T)
                out[j, info[4]] = dk_acc[rows, :] * LN2
                out[j, 1 - info[4]] = dv_acc[rows, :]

def own_backward(info, ql_ref, qr_ref, dl_ref, dr_ref, mine_ref, other_ref, p_ref, c_ref, rd_ref, dq_ref,
                 of_ref, gl_ref, far_ref, h0, h1, h2, h3, vc, kt, dk_acc, dv_acc):
    u, step = pl.program_id(0), pl.program_id(1)

    @pl.when((u == 0) & (step == 0))
    def _():
        for c in range(4):
            k, v = own_quarter(info, mine_ref, other_ref, c)
            fill(k, slice(c * T, (c + 1) * T), None, kt)
            fill(v, slice(c * T, (c + 1) * T), vc, None)
        dk_acc[...] = jnp.zeros_like(dk_acc)
        dv_acc[...] = jnp.zeros_like(dv_acc)

    q = near_far(u, ql_ref, qr_ref) * (SCALE * LOG2E)
    dot = turned(near_far(u, dl_ref, dr_ref)) * c_ref[0]
    p = p_ref[0]
    hi, lo = split(p)
    dv_acc[...] += halves(mm(jnp.concatenate([hi, lo], axis=1), right(stacked(upright(dot)))))
    dp = mm(twice(vc[...], 1), left(dot))
    hi, lo = split(p * (dp - rd_ref[0]))
    dk_acc[...] += halves(mm(jnp.concatenate([hi, lo], axis=1), right(stacked(q))))
    dq = upright(dq_ref[0] + values_sum(kt[...], hi, lo)) * SCALE

    @pl.when(u == 0)
    def _():
        gl_ref[...] = dq

    @pl.when(u == 1)
    def _():
        far_ref[0] = of_ref[...]
        far_ref[1] = dq

    @pl.when((u == 1) & (step == STEPS - 1))
    def _():
        for x, out in enumerate((h0, h1, h2, h3)):
            rows = pl.ds(pl.multiple_of((info[0] ^ x) * T, T), T)
            out[info[4]] = dk_acc[rows, :] * LN2
            out[1 - info[4]] = dv_acc[rows, :]

def tile(shape):
    return pl.BlockSpec((1,) + shape[1:], lambda u, h, i: (u * STEPS + h, 0, 0))

def whole(shape):
    return pl.BlockSpec(shape, lambda u, h, i: (0,) * len(shape))

NEAR = pl.BlockSpec((T, HP * W), lambda u, h, i: (0, i[1] * STEPS + h))
FAR = pl.BlockSpec((T, HP * W), lambda u, h, i: (0, h))
FIRST = pl.BlockSpec((T, HP * W), lambda u, h, i: (0, jnp.where(u == 0, h, STEPS - 1)))
SECOND = pl.BlockSpec((T, HP * W), lambda u, h, i: (0, jnp.where(u == 0, 0, h)))
BOTH = pl.BlockSpec((2, T, HP * W), lambda u, h, i: (0, 0, jnp.where(u == 0, 0, h)))
PROBS, ROW, TURNED = (2 * STEPS, BLK, R), (2 * STEPS, 1, R), (2 * STEPS, W, R)
HALF, PIECE, PAIR = (T, 4 * W), (2, T, W), (2, 2, T, W)

def in_hbm(*arrays):
    return [pltpu.with_memory_space_constraint(a, pltpu.HBM) for a in arrays]

def kernel(body, ins, outs, out_shapes, scratch, flops, limit):
    return pl.pallas_call(
        body,
        out_shape=[pltpu.HBM(s, F32) for s in out_shapes],
        grid_spec=pltpu.PrefetchScalarGridSpec(
            num_scalar_prefetch=1,
            grid=(2, STEPS),
            in_specs=ins,
            out_specs=outs,
            scratch_shapes=[pltpu.VMEM(s, d) for s, d in scratch],
        ),
        compiler_params=pltpu.CompilerParams(
            dimension_semantics=("arbitrary", "arbitrary"), vmem_limit_bytes=limit << 20),
        cost_estimate=pl.CostEstimate(
            flops=flops, transcendentals=0, bytes_accessed=16 << 20),
        name=body.__name__,
    )

UNIT = 2 * 2048 * BLK * W * 4

def call_own_forward(info, q, q_far, mine, other):
    return kernel(
        own_forward,
        [NEAR, FAR, whole(mine.shape), whole(other.shape)],
        [tile(PROBS), tile(ROW), tile(ROW), tile(TURNED)],
        [PROBS, ROW, ROW, TURNED],
        [((BLK, 2 * W), BF), ((2 * W, BLK), BF)],
        2 * UNIT, 30,
    )(info, *in_hbm(q), q_far, *in_hbm(mine), other)

def call_picked(info, q, q_far, do, do_far, pieces, m, l, ot):
    return kernel(
        picked,
        [NEAR, FAR, NEAR, FAR] + [whole(PAIR)] * 4 + [tile(ROW), tile(ROW), tile(TURNED)],
        [FIRST, SECOND, tile(TURNED), tile(ROW), tile(ROW)] + [whole(PAIR)] * 4,
        [HALF, HALF, TURNED, ROW, ROW] + [PAIR] * 4,
        [((2 * BLK, 2 * W), BF), ((2 * BLK, 2 * W), BF), ((2 * W, 2 * BLK), BF), ((2 * W, 2 * BLK), BF),
         ((2 * BLK, R), F32),
         ((2 * BLK, W), F32), ((2 * BLK, W), F32)],
        10 * UNIT, 52,
    )(info, *in_hbm(q), q_far, *in_hbm(do), do_far, *pieces, *in_hbm(m, l, ot))

def call_own_backward(info, q, q_far, do, do_far, mine, other, p, c, rd, dq, o_far):
    return kernel(
        own_backward,
        [NEAR, FAR, NEAR, FAR, whole(mine.shape), whole(other.shape), tile(PROBS), tile(ROW), tile(ROW),
         tile(TURNED), SECOND],
        [FIRST, BOTH] + [whole(PIECE)] * 4,
        [HALF, (2,) + HALF] + [PIECE] * 4,
        [((BLK, 2 * W), BF), ((2 * W, BLK), BF), ((BLK, W), F32), ((BLK, W), F32)],
        3 * UNIT, 40,
    )(info, *in_hbm(q), q_far, *in_hbm(do), do_far, *in_hbm(mine), other, *in_hbm(p, c, rd, dq, o_far))

HEADS = (4, T, W)
SWAP = [(0, 1), (1, 0)]
PLACE = ("y", "x", "head")

def glue(body, args, outs):
    spec = lambda shape: pl.BlockSpec(shape, lambda i: (0,) * len(shape))
    arrays = args[1:]
    return pl.pallas_call(
        body,
        out_shape=[jax.ShapeDtypeStruct(s, F32) for s in outs],
        grid=(1,),
        in_specs=[pl.BlockSpec(memory_space=pltpu.SMEM)] + [spec(a.shape) for a in arrays],
        out_specs=[spec(s) for s in outs],
        compiler_params=pltpu.CompilerParams(
            dimension_semantics=("arbitrary",), vmem_limit_bytes=20 << 20),
        cost_estimate=pl.CostEstimate(
            flops=0, transcendentals=0,
            bytes_accessed=4 * sum(math.prod(s) for s in [a.shape for a in arrays] + list(outs))),
        name=body.__name__,
    )(args[0], *arrays)

def travel(array, step, stage):
    pairs = []
    for y in range(4):
        for x in range(4):
            for core in range(2):
                ty, tx = (y + step) % 4, x
                if core != stage:
                    ty, tx = y, (x + step) % 4
                pairs.append(((y * 4 + x) * 2 + core, (ty * 4 + tx) * 2 + core))
    return lax.ppermute(array, PLACE, pairs)

def mirror(array, flip):
    return lax.ppermute(array, "z", [(i, i ^ flip) for i in range(4)])

def swap(array):
    return lax.ppermute(array, "head", SWAP)

def after(array, *others):
    return lax.optimization_barrier((array, *others))[0]

def place():
    core, y, x = (lax.axis_index(a) for a in ("head", "y", "x"))
    return core, jnp.where(core == 0, y, x), jnp.where(core == 0, x, y)

def chosen(table, first, second, core, j):
    block = jnp.where(core == 0, first * 4 + second, second * 4 + first)
    other = jnp.maximum(table[block, 1 + j], 0)
    y, x = other // 4, other % 4
    return jnp.where(core == 0, y, x), jnp.where(core == 0, x, y)

def assemble(spot, keys, values, other, full):
    core = spot[0]
    half = T // 2
    here, there = (pl.ds(pl.multiple_of(c * half, half), half) for c in (core, 1 - core))
    for h in range(4):
        cols = slice(h * W, (h + 1) * W)
        full[h, here] = jnp.where(core == 0, keys[:, cols], values[:, cols])
        full[h, there] = other[:, cols]

def pick(table, *refs):
    core, here, there = place()
    along, out = refs[0:4], refs[4:7]
    for step in (1, 2, 3):
        for j in range(2):
            first, _ = chosen(table, here, (there + step) % 4, core, j)
            for i in range(4):
                @pl.when((here - first) % 4 == i)
                def _(source=along[i], ref=out[step - 1], j=j):
                    ref[j] = source[...]

def join(table, *refs):
    core, here, there = place()
    along, got, (mine, send) = refs[0:4], refs[4:7], refs[7:9]
    for j in range(2):
        first, second = chosen(table, here, there, core, j)
        near, off = (here - first) % 4, (there - second) % 4
        for c, out in ((core, mine), (1 - core, send)):
            heads = pl.ds(2 * c, 2)
            for k in range(4):
                @pl.when((off == 0) & (near == k))
                def _(source=along[k], out=out, heads=heads, j=j):
                    out[j] = source[heads]
            for k in range(3):
                @pl.when(off == k + 1)
                def _(source=got[k], out=out, heads=heads, j=j):
                    out[j] = source[j, heads]

def arrange(spot, mine, other, same, cross):
    head = spot[1]
    for j in range(2):
        for n, ref in enumerate((mine, other)):
            same[j, n] = ref[j, head]
            cross[j, n] = ref[j, 1 - head]

def spread(spot, mine, added, passed, passed2, keep, send):
    head = spot[1]
    for j in range(mine.shape[0]):
        for n, out in ((0, keep), (1, send)):
            out[j, head] = mine[j, n] + added[j, n]
            out[j, 1 - head] = passed[j, n] + passed2[j, n]

def gather_heads(spot, keep, other, full):
    core = spot[0]
    for j in range(2):
        full[j, pl.ds(2 * core, 2)] = keep[j]
        full[j, pl.ds(2 * (1 - core), 2)] = other[j]

def collect(table, *refs):
    core, here, there = place()
    got, out = refs[0:4], refs[4:8]
    for ref in out:
        ref[...] = jnp.zeros_like(ref)
    for step in range(4):
        for j in range(2):
            first, second = chosen(table, here, (there - step) % 4, core, j)
            for i in range(4):
                @pl.when((second == there) & ((here - first) % 4 == i))
                def _(source=got[step], ref=out[i], j=j):
                    ref[...] += source[j]

def shards(queries, keys, values, cotangent, selected):
    core, z = lax.axis_index("head"), lax.axis_index("z")
    head = z // 2
    mine = lax.dynamic_slice(selected, (lax.axis_index("y") * 4 + lax.axis_index("x"), 1), (1, 2))[0]
    info = jnp.concatenate([jnp.stack([z, head]), (mine >= 0).astype(jnp.int32), core[None]])
    spot = jnp.stack([core, head])
    far = 1 - head
    got = swap(jnp.where(core == 0, values, keys))
    (full,) = glue(assemble, (spot, *in_hbm(keys, values), got), (HEADS,))
    own = lax.all_gather(full, "z", axis=0)

    along = [full] + [travel(full, s, 0) for s in (1, 2, 3)]

    def turned_over(array, *others):
        return mirror(lax.dynamic_slice_in_dim(after(array, *others), far * 4 * W, 4 * W, 1), 3)

    q_far = turned_over(queries, along[1])
    do_far = turned_over(cotangent, q_far)
    sent = glue(pick, (selected, *along), ((2,) + HEADS,) * 3)
    got = [travel(sent[s - 1], s, 1) for s in (1, 2, 3)]
    kept, send = glue(join, (after(selected, q_far), *along, *got), (PAIR, PAIR))
    same, cross = glue(arrange, (spot, kept, swap(send)), (PAIR, PAIR))
    own_other = swap(lax.dynamic_index_in_dim(own, 2 * (1 - core) + head, 1, keepdims=False))
    pieces = [same] + [mirror(a, flip) for a, flip in ((same, 1), (cross, 2), (cross, 3))]

    p, m, l, ot = call_own_forward(after(info, do_far), queries, q_far, own, own_other)
    out = call_picked(info, queries, q_far, cotangent, do_far, pieces, m, l, ot)
    o_near, o_far, dq, c, rd = out[:5]
    last = call_own_backward(
        info, queries, q_far, cotangent, do_far, own, own_other, p, c, rd, dq, o_far)

    def reduced(g, *others):
        arrived = [g[0]] + [mirror(g[flip], flip) for flip in (1, 2, 3)]
        arrived[3] = after(arrived[3], *others)
        keep, send = glue(spread, (spot, *arrived), (g[0].shape,) * 2)
        return keep, swap(send)

    (terms,) = glue(gather_heads, (spot, *reduced(out[5:9], last[0])), ((2,) + HEADS,))
    arrived = [terms] + [travel(terms, s, 1) for s in (1, 2, 3)]
    low, high = reduced([a[None] for a in last[2:6]])
    back_far = mirror(after(last[1], low), 3)
    sums = glue(collect, (after(selected, low), *arrived), (HEADS,) * 4)
    total = after(sums[0], back_far) + sum(travel(sums[s], 4 - s, 0) for s in (1, 2, 3))
    total = total + jnp.where(
        core == 0, jnp.concatenate([low[0], high[0]], 0), jnp.concatenate([high[0], low[0]], 0)
    )

    half = T // 2

    def tokens(which):
        a = lax.dynamic_slice_in_dim(total, which * half, half, 1)
        return jnp.concatenate([a[h] for h in range(4)], 1)

    keep, back = tokens(core), swap(tokens(1 - core))

    def sides(a, b):
        return jnp.where(head == 0, jnp.concatenate([a, b], 1), jnp.concatenate([b, a], 1))

    return (
        sides(o_near, back_far[0]),
        sides(last[0], back_far[1]),
        jnp.where(core == 0, keep, back),
        jnp.where(core == 0, back, keep),
    )

def solution(mesh):
    grid = Mesh(mesh.devices.reshape(4, 4, 4, 2), ("y", "x", "z", "head"))
    tokens = ("y", "x", "z")
    wide, narrow = P(tokens, "head"), P(tokens + ("head",), None)
    return jax.shard_map(
        shards,
        mesh=grid,
        in_specs=(wide, narrow, narrow, wide, P()),
        out_specs=(wide, wide, narrow, narrow),
        check_vma=False,
    )
```

```python
import math

import jax
import jax.numpy as jnp
from jax import lax
from jax.experimental import pallas as pl
from jax.experimental.pallas import tpu as pltpu
from jax.sharding import Mesh, PartitionSpec as P

W = 128
T = 256

SCALE = 1.0 / math.sqrt(W)
LOG2E = math.log2(math.e)
LN2 = math.log(2.0)
BF = jnp.bfloat16
F32 = jnp.float32
BLK = 4 * T
HP = 2
STEPS = 4 // HP
R = HP * T

def split(x):
    hi = x.astype(BF)
    return hi, (x - hi.astype(F32)).astype(BF)

def twice(x, axis):
    return jnp.concatenate([x, x], axis=axis)

def mm(a, b):
    return lax.dot_general(a, b, (((1,), (0,)), ((), ())), preferred_element_type=F32)

def turned(x):
    return jnp.concatenate([x[:, i * W:(i + 1) * W].T for i in range(HP)], axis=1)

def upright(x):
    return jnp.concatenate([x[:, i * T:(i + 1) * T].T for i in range(HP)], axis=1)

def stacked(x):
    return jnp.concatenate([x[:, i * W:(i + 1) * W] for i in range(HP)], axis=0)

def left(x):
    hi, lo = split(x)
    return jnp.concatenate([hi, hi, lo, lo], axis=0)

def right(x):
    hi, lo = split(x)
    return twice(jnp.concatenate([hi, lo], axis=1), 0)

def fill(x, rows, cat, tr):
    hi, lo = split(x)
    if cat is not None:
        cat[rows, 0:W] = hi
        cat[rows, W:2 * W] = lo
    if tr is not None:
        hit, lot = split(x.T)
        tr[0:W, rows] = hit
        tr[W:2 * W, rows] = lot

def values_sum(tr, hi, lo):
    a = mm(tr, hi)
    return a[0:W] + a[W:2 * W] + mm(tr[0:W], lo)

def halves(x):
    return x[:, 0:W] + x[:, W:2 * W]

def own_quarter(info, mine_ref, other_ref, c):
    core = info[4]
    a, b = mine_ref[c, 2 * core + info[1]], other_ref[c]
    return jnp.where(core == 0, a, b), jnp.where(core == 0, b, a)

def near_far(u, near, far):
    return jnp.where(u == 0, near[...], far[...])

def own_forward(info, ql_ref, qr_ref, mine_ref, other_ref, p_ref, m_ref, l_ref, ot_ref, kc, vt):
    u = pl.program_id(0)

    @pl.when((u == 0) & (pl.program_id(1) == 0))
    def _():
        for c in range(4):
            k, v = own_quarter(info, mine_ref, other_ref, c)
            fill(k, slice(c * T, (c + 1) * T), kc, None)
            fill(v, slice(c * T, (c + 1) * T), None, vt)

    quarter = jnp.where(u == 0, info[0], 3 - info[0])
    q = left(turned(near_far(u, ql_ref, qr_ref)) * (SCALE * LOG2E))
    s = mm(twice(kc[...], 1), q)
    token = lax.broadcasted_iota(jnp.int32, (BLK, R), 1) & (T - 1)
    ahead = lax.broadcasted_iota(jnp.int32, (BLK, R), 0) - token
    s = jnp.where(ahead <= quarter * T, s, -jnp.inf)
    m = jnp.max(s, axis=0, keepdims=True)
    p = jnp.exp2(s - m)
    p_ref[0] = p
    m_ref[0] = m
    l_ref[0] = jnp.sum(p, axis=0, keepdims=True)
    hi, lo = split(p)
    ot_ref[0] = values_sum(vt[...], hi, lo)

def picked(info, ql_ref, qr_ref, dl_ref, dr_ref, s0, s1, s2, s3,
           m0_ref, l0_ref, ot0_ref, ol_ref, or_ref, dq_ref, c_ref, rd_ref, g0, g1, g2, g3,
           kc, vc, kt, vt, s_sc, dk_acc, dv_acc):
    u, step = pl.program_id(0), pl.program_id(1)

    @pl.when((u == 0) & (step == 0))
    def _():
        for j in range(2):
            for x in range(4):
                rows = slice((j * 4 + x) * T, (j * 4 + x + 1) * T)
                piece = (s0, s1, s2, s3)[x]
                fill(piece[j, info[4]], rows, kc, kt)
                fill(piece[j, 1 - info[4]], rows, vc, vt)
        dk_acc[...] = jnp.zeros_like(dk_acc)
        dv_acc[...] = jnp.zeros_like(dv_acc)

    q = near_far(u, ql_ref, qr_ref) * (SCALE * LOG2E)
    do = near_far(u, dl_ref, dr_ref)
    qt = left(turned(q))
    m0 = m0_ref[0]
    m = m0
    for j in range(2):
        rows = slice(j * BLK, (j + 1) * BLK)
        s = mm(twice(kc[rows, :], 1), qt)
        s = jnp.where(info[2 + j] > 0, s, -jnp.inf)
        s_sc[rows, :] = s
        m = jnp.maximum(m, jnp.max(s, axis=0, keepdims=True))
    shrink = jnp.exp2(m0 - m)
    l = l0_ref[0] * shrink
    ot = ot0_ref[0] * shrink
    for j in range(2):
        rows = slice(j * BLK, (j + 1) * BLK)
        p = jnp.exp2(s_sc[rows, :] - m)
        s_sc[rows, :] = p
        hi, lo = split(p)
        l = l + jnp.sum(p, axis=0, keepdims=True)
        ot = ot + values_sum(vt[:, rows], hi, lo)
    inv = 1.0 / l
    ot = ot * inv
    dot = turned(do) * inv
    rd = jnp.sum(dot * ot, axis=0, keepdims=True)
    c_ref[0] = inv * shrink
    rd_ref[0] = rd * shrink
    o = upright(ot)

    @pl.when(u == 0)
    def _():
        ol_ref[...] = o

    @pl.when(u == 1)
    def _():
        or_ref[...] = o

    dt = left(dot)
    d2 = right(stacked(upright(dot)))
    q2 = right(stacked(q))
    dq = jnp.zeros((W, R), F32)
    for j in range(2):
        rows = slice(j * BLK, (j + 1) * BLK)
        p = s_sc[rows, :]
        p2 = jnp.concatenate(split(p), axis=1)
        dp = mm(twice(vc[rows, :], 1), dt)
        hi, lo = split(p * (dp - rd))
        dq = dq + values_sum(kt[:, rows], hi, lo)
        dv_acc[rows, :] += halves(mm(p2, d2))
        dk_acc[rows, :] += halves(mm(jnp.concatenate([hi, lo], axis=1), q2))
    dq_ref[0] = dq

    @pl.when((u == 1) & (step == STEPS - 1))
    def _():
        for j in range(2):
            for x, out in enumerate((g0, g1, g2, g3)):
                rows = slice((j * 4 + x) * T, (j * 4 + x + 1) * T)
                out[j, info[4]] = dk_acc[rows, :] * LN2
                out[j, 1 - info[4]] = dv_acc[rows, :]

def own_backward(info, ql_ref, qr_ref, dl_ref, dr_ref, mine_ref, other_ref, p_ref, c_ref, rd_ref, dq_ref,
                 of_ref, gl_ref, far_ref, h0, h1, h2, h3, vc, kt, dk_acc, dv_acc):
    u, step = pl.program_id(0), pl.program_id(1)

    @pl.when((u == 0) & (step == 0))
    def _():
        for c in range(4):
            k, v = own_quarter(info, mine_ref, other_ref, c)
            fill(k, slice(c * T, (c + 1) * T), None, kt)
            fill(v, slice(c * T, (c + 1) * T), vc, None)
        dk_acc[...] = jnp.zeros_like(dk_acc)
        dv_acc[...] = jnp.zeros_like(dv_acc)

    q = near_far(u, ql_ref, qr_ref) * (SCALE * LOG2E)
    dot = turned(near_far(u, dl_ref, dr_ref)) * c_ref[0]
    p = p_ref[0]
    hi, lo = split(p)
    dv_acc[...] += halves(mm(jnp.concatenate([hi, lo], axis=1), right(stacked(upright(dot)))))
    dp = mm(twice(vc[...], 1), left(dot))
    hi, lo = split(p * (dp - rd_ref[0]))
    dk_acc[...] += halves(mm(jnp.concatenate([hi, lo], axis=1), right(stacked(q))))
    dq = upright(dq_ref[0] + values_sum(kt[...], hi, lo)) * SCALE

    @pl.when(u == 0)
    def _():
        gl_ref[...] = dq

    @pl.when(u == 1)
    def _():
        far_ref[0] = of_ref[...]
        far_ref[1] = dq

    @pl.when((u == 1) & (step == STEPS - 1))
    def _():
        for x, out in enumerate((h0, h1, h2, h3)):
            rows = pl.ds(pl.multiple_of((info[0] ^ x) * T, T), T)
            out[info[4]] = dk_acc[rows, :] * LN2
            out[1 - info[4]] = dv_acc[rows, :]

def tile(shape):
    return pl.BlockSpec((1,) + shape[1:], lambda u, h, i: (u * STEPS + h, 0, 0))

def whole(shape):
    return pl.BlockSpec(shape, lambda u, h, i: (0,) * len(shape))

NEAR = pl.BlockSpec((T, HP * W), lambda u, h, i: (0, i[1] * STEPS + h))
FAR = pl.BlockSpec((T, HP * W), lambda u, h, i: (0, h))
FIRST = pl.BlockSpec((T, HP * W), lambda u, h, i: (0, jnp.where(u == 0, h, STEPS - 1)))
SECOND = pl.BlockSpec((T, HP * W), lambda u, h, i: (0, jnp.where(u == 0, 0, h)))
BOTH = pl.BlockSpec((2, T, HP * W), lambda u, h, i: (0, 0, jnp.where(u == 0, 0, h)))
PROBS, ROW, TURNED = (2 * STEPS, BLK, R), (2 * STEPS, 1, R), (2 * STEPS, W, R)
HALF, PIECE, PAIR = (T, 4 * W), (2, T, W), (2, 2, T, W)

def in_hbm(*arrays):
    return [pltpu.with_memory_space_constraint(a, pltpu.HBM) for a in arrays]

def kernel(body, ins, outs, out_shapes, scratch, flops, limit):
    return pl.pallas_call(
        body,
        out_shape=[pltpu.HBM(s, F32) for s in out_shapes],
        grid_spec=pltpu.PrefetchScalarGridSpec(
            num_scalar_prefetch=1,
            grid=(2, STEPS),
            in_specs=ins,
            out_specs=outs,
            scratch_shapes=[pltpu.VMEM(s, d) for s, d in scratch],
        ),
        compiler_params=pltpu.CompilerParams(
            dimension_semantics=("arbitrary", "arbitrary"), vmem_limit_bytes=limit << 20),
        cost_estimate=pl.CostEstimate(
            flops=flops, transcendentals=0, bytes_accessed=16 << 20),
        name=body.__name__,
    )

UNIT = 2 * 2048 * BLK * W * 4

def call_own_forward(info, q, q_far, mine, other):
    return kernel(
        own_forward,
        [NEAR, FAR, whole(mine.shape), whole(other.shape)],
        [tile(PROBS), tile(ROW), tile(ROW), tile(TURNED)],
        [PROBS, ROW, ROW, TURNED],
        [((BLK, 2 * W), BF), ((2 * W, BLK), BF)],
        2 * UNIT, 30,
    )(info, *in_hbm(q), q_far, *in_hbm(mine), other)

def call_picked(info, q, q_far, do, do_far, pieces, m, l, ot):
    return kernel(
        picked,
        [NEAR, FAR, NEAR, FAR] + [whole(PAIR)] * 4 + [tile(ROW), tile(ROW), tile(TURNED)],
        [FIRST, SECOND, tile(TURNED), tile(ROW), tile(ROW)] + [whole(PAIR)] * 4,
        [HALF, HALF, TURNED, ROW, ROW] + [PAIR] * 4,
        [((2 * BLK, 2 * W), BF), ((2 * BLK, 2 * W), BF), ((2 * W, 2 * BLK), BF), ((2 * W, 2 * BLK), BF),
         ((2 * BLK, R), F32),
         ((2 * BLK, W), F32), ((2 * BLK, W), F32)],
        10 * UNIT, 52,
    )(info, *in_hbm(q), q_far, *in_hbm(do), do_far, *pieces, *in_hbm(m, l, ot))

def call_own_backward(info, q, q_far, do, do_far, mine, other, p, c, rd, dq, o_far):
    return kernel(
        own_backward,
        [NEAR, FAR, NEAR, FAR, whole(mine.shape), whole(other.shape), tile(PROBS), tile(ROW), tile(ROW),
         tile(TURNED), SECOND],
        [FIRST, BOTH] + [whole(PIECE)] * 4,
        [HALF, (2,) + HALF] + [PIECE] * 4,
        [((BLK, 2 * W), BF), ((2 * W, BLK), BF), ((BLK, W), F32), ((BLK, W), F32)],
        3 * UNIT, 40,
    )(info, *in_hbm(q), q_far, *in_hbm(do), do_far, *in_hbm(mine), other, *in_hbm(p, c, rd, dq, o_far))

HEADS = (4, T, W)
SWAP = [(0, 1), (1, 0)]
PLACE = ("y", "x", "head")

def glue(body, args, outs, space=jax.ShapeDtypeStruct):
    spec = lambda shape: pl.BlockSpec(shape, lambda i: (0,) * len(shape))
    arrays = args[1:]
    return pl.pallas_call(
        body,
        out_shape=[space(s, F32) for s in outs],
        grid=(1,),
        in_specs=[pl.BlockSpec(memory_space=pltpu.SMEM)] + [spec(a.shape) for a in arrays],
        out_specs=[spec(s) for s in outs],
        compiler_params=pltpu.CompilerParams(
            dimension_semantics=("arbitrary",), vmem_limit_bytes=20 << 20),
        cost_estimate=pl.CostEstimate(
            flops=0, transcendentals=0,
            bytes_accessed=4 * sum(math.prod(s) for s in [a.shape for a in arrays] + list(outs))),
        name=body.__name__,
    )(args[0], *arrays)

def travel(array, step, stage):
    pairs = []
    for y in range(4):
        for x in range(4):
            for core in range(2):
                ty, tx = (y + step) % 4, x
                if core != stage:
                    ty, tx = y, (x + step) % 4
                pairs.append(((y * 4 + x) * 2 + core, (ty * 4 + tx) * 2 + core))
    return lax.ppermute(array, PLACE, pairs)

def circle(arrays, stage, back=False):
    step = (lambda s: 4 - s) if back else (lambda s: s)
    two = travel(arrays[1], step(2), stage)
    return [travel(arrays[0], step(1), stage), two, travel(arrays[2], step(3), stage)]

def mirror(array, flip):
    return lax.ppermute(array, "z", [(i, i ^ flip) for i in range(4)])

def swap(array):
    return lax.ppermute(array, "head", SWAP)

def after(array, *others):
    return lax.optimization_barrier((array, *others))[0]

def place():
    core, y, x = (lax.axis_index(a) for a in ("head", "y", "x"))
    return core, jnp.where(core == 0, y, x), jnp.where(core == 0, x, y)

def chosen(table, first, second, core, j):
    block = jnp.where(core == 0, first * 4 + second, second * 4 + first)
    other = jnp.maximum(table[block, 1 + j], 0)
    y, x = other // 4, other % 4
    return jnp.where(core == 0, y, x), jnp.where(core == 0, x, y)

def assemble(spot, keys, values, other, full):
    core = spot[0]
    half = T // 2
    here, there = (pl.ds(pl.multiple_of(c * half, half), half) for c in (core, 1 - core))
    for h in range(4):
        cols = slice(h * W, (h + 1) * W)
        full[h, here] = jnp.where(core == 0, keys[:, cols], values[:, cols])
        full[h, there] = other[:, cols]

def pick(table, *refs):
    core, here, there = place()
    along, out = refs[0:4], refs[4:7]
    for step in (1, 2, 3):
        for j in range(2):
            first, _ = chosen(table, here, (there + step) % 4, core, j)
            for i in range(4):
                @pl.when((here - first) % 4 == i)
                def _(source=along[i], ref=out[step - 1], j=j):
                    ref[j] = source[...]

def join(table, *refs):
    core, here, there = place()
    along, got, (mine, send) = refs[0:4], refs[4:7], refs[7:9]
    for j in range(2):
        first, second = chosen(table, here, there, core, j)
        near, off = (here - first) % 4, (there - second) % 4
        for c, out in ((core, mine), (1 - core, send)):
            heads = pl.ds(2 * c, 2)
            for k in range(4):
                @pl.when((off == 0) & (near == k))
                def _(source=along[k], out=out, heads=heads, j=j):
                    out[j] = source[heads]
            for k in range(3):
                @pl.when(off == k + 1)
                def _(source=got[k], out=out, heads=heads, j=j):
                    out[j] = source[j, heads]

def arrange(spot, mine, other, same, cross):
    head = spot[1]
    for j in range(2):
        for n, ref in enumerate((mine, other)):
            same[j, n] = ref[j, head]
            cross[j, n] = ref[j, 1 - head]

def spread(spot, mine, added, passed, passed2, keep, send):
    head = spot[1]
    for j in range(mine.shape[0]):
        for n, out in ((0, keep), (1, send)):
            out[j, head] = mine[j, n] + added[j, n]
            out[j, 1 - head] = passed[j, n] + passed2[j, n]

def gather_heads(spot, keep, other, full):
    core = spot[0]
    for j in range(2):
        full[j, pl.ds(2 * core, 2)] = keep[j]
        full[j, pl.ds(2 * (1 - core), 2)] = other[j]

def collect(table, *refs):
    core, here, there = place()
    got, out = refs[0:4], refs[4:8]
    for ref in out:
        ref[...] = jnp.zeros_like(ref)
    for step in range(4):
        for j in range(2):
            first, second = chosen(table, here, (there - step) % 4, core, j)
            for i in range(4):
                @pl.when((second == there) & ((here - first) % 4 == i))
                def _(source=got[step], ref=out[i], j=j):
                    ref[...] += source[j]

def shards(queries, keys, values, cotangent, selected):
    core, z = lax.axis_index("head"), lax.axis_index("z")
    head = z // 2
    mine = lax.dynamic_slice(selected, (lax.axis_index("y") * 4 + lax.axis_index("x"), 1), (1, 2))[0]
    info = jnp.concatenate([jnp.stack([z, head]), (mine >= 0).astype(jnp.int32), core[None]])
    spot = jnp.stack([core, head])
    far = 1 - head
    got = swap(jnp.where(core == 0, values, keys))
    (full,) = glue(assemble, (spot, *in_hbm(keys, values), got), (HEADS,))
    own = lax.all_gather(full, "z", axis=0)

    along = [full] + circle([full] * 3, 0)

    def turned_over(array, *others):
        return mirror(lax.dynamic_slice_in_dim(after(array, *others), far * 4 * W, 4 * W, 1), 3)

    q_far = turned_over(queries, along[1])
    do_far = turned_over(cotangent, q_far)
    sent = glue(pick, (selected, *along), ((2,) + HEADS,) * 3)
    got = circle(sent, 1)
    kept, send = glue(join, (after(selected, q_far), *along, *got), (PAIR, PAIR))
    same, cross = glue(arrange, (spot, kept, swap(send)), (PAIR, PAIR))
    own_other = swap(lax.dynamic_index_in_dim(own, 2 * (1 - core) + head, 1, keepdims=False))
    pieces = [same] + [mirror(a, flip) for a, flip in ((same, 1), (cross, 2), (cross, 3))]

    p, m, l, ot = call_own_forward(after(info, do_far), queries, q_far, own, own_other)
    out = call_picked(info, queries, q_far, cotangent, do_far, pieces, m, l, ot)
    o_near, o_far, dq, c, rd = out[:5]
    last = call_own_backward(
        info, queries, q_far, cotangent, do_far, own, own_other, p, c, rd, dq, o_far)

    def reduced(g, *others):
        arrived = [g[0]] + [mirror(g[flip], flip) for flip in (1, 2, 3)]
        arrived[3] = after(arrived[3], *others)
        keep, send = glue(spread, (spot, *arrived), (g[0].shape,) * 2)
        return keep, swap(send)

    (terms,) = glue(gather_heads, (spot, *reduced(out[5:9], last[0])), ((2,) + HEADS,))
    arrived = [terms] + circle([terms] * 3, 1)
    low, high = reduced([a[None] for a in last[2:6]])
    back_far = mirror(after(last[1], low), 3)
    sums = glue(collect, (after(selected, low), *arrived), (HEADS,) * 4, pltpu.HBM)

    def sides(a, b):
        return jnp.where(head == 0, jnp.concatenate([a, b], 1), jnp.concatenate([b, a], 1))

    wide = sides(o_near, back_far[0]), sides(last[0], back_far[1])
    total = after(sums[0], *wide) + sum(circle(sums[1:], 0, True))
    total = total + jnp.where(
        core == 0, jnp.concatenate([low[0], high[0]], 0), jnp.concatenate([high[0], low[0]], 0)
    )

    half = T // 2

    def tokens(which):
        a = lax.dynamic_slice_in_dim(total, which * half, half, 1)
        return jnp.concatenate([a[h] for h in range(4)], 1)

    keep, back = tokens(core), swap(tokens(1 - core))

    return (
        *wide,
        jnp.where(core == 0, keep, back),
        jnp.where(core == 0, back, keep),
    )

def solution(mesh):
    grid = Mesh(mesh.devices.reshape(4, 4, 4, 2), ("y", "x", "z", "head"))
    tokens = ("y", "x", "z")
    wide, narrow = P(tokens, "head"), P(tokens + ("head",), None)
    return jax.shard_map(
        shards,
        mesh=grid,
        in_specs=(wide, narrow, narrow, wide, P()),
        out_specs=(wide, wide, narrow, narrow),
        check_vma=False,
    )
```

```python
import math

import jax
import jax.numpy as jnp
from jax import lax
from jax.experimental import pallas as pl
from jax.experimental.pallas import tpu as pltpu
from jax.sharding import Mesh, PartitionSpec as P

W = 128
T = 256

SCALE = 1.0 / math.sqrt(W)
LOG2E = math.log2(math.e)
LN2 = math.log(2.0)
BF = jnp.bfloat16
F32 = jnp.float32
BLK = 4 * T
HP = 2
STEPS = 4 // HP
R = HP * T

def split(x):
    hi = x.astype(BF)
    return hi, (x - hi.astype(F32)).astype(BF)

def twice(x, axis):
    return jnp.concatenate([x, x], axis=axis)

def mm(a, b):
    return lax.dot_general(a, b, (((1,), (0,)), ((), ())), preferred_element_type=F32)

def turned(x):
    return jnp.concatenate([x[:, i * W:(i + 1) * W].T for i in range(HP)], axis=1)

def upright(x):
    return jnp.concatenate([x[:, i * T:(i + 1) * T].T for i in range(HP)], axis=1)

def stacked(x):
    return jnp.concatenate([x[:, i * W:(i + 1) * W] for i in range(HP)], axis=0)

def left(x):
    hi, lo = split(x)
    return jnp.concatenate([hi, hi, lo, lo], axis=0)

def right(x):
    hi, lo = split(x)
    return twice(jnp.concatenate([hi, lo], axis=1), 0)

def fill(x, rows, cat, tr):
    hi, lo = split(x)
    if cat is not None:
        cat[rows, 0:W] = hi
        cat[rows, W:2 * W] = lo
    if tr is not None:
        hit, lot = split(x.T)
        tr[0:W, rows] = hit
        tr[W:2 * W, rows] = lot

def values_sum(tr, hi, lo):
    a = mm(tr, hi)
    return a[0:W] + a[W:2 * W] + mm(tr[0:W], lo)

def halves(x):
    return x[:, 0:W] + x[:, W:2 * W]

def own_quarter(info, mine_ref, other_ref, c):
    core = info[4]
    a, b = mine_ref[c, 2 * core + info[1]], other_ref[c]
    return jnp.where(core == 0, a, b), jnp.where(core == 0, b, a)

def near_far(u, near, far):
    return jnp.where(u == 0, near[...], far[...])

def own_forward(info, ql_ref, qr_ref, mine_ref, other_ref, p_ref, m_ref, l_ref, ot_ref, kc, vt):
    u = pl.program_id(0)

    @pl.when((u == 0) & (pl.program_id(1) == 0))
    def _():
        for c in range(4):
            k, v = own_quarter(info, mine_ref, other_ref, c)
            fill(k, slice(c * T, (c + 1) * T), kc, None)
            fill(v, slice(c * T, (c + 1) * T), None, vt)

    quarter = jnp.where(u == 0, info[0], 3 - info[0])
    q = left(turned(near_far(u, ql_ref, qr_ref)) * (SCALE * LOG2E))
    s = mm(twice(kc[...], 1), q)
    token = lax.broadcasted_iota(jnp.int32, (BLK, R), 1) & (T - 1)
    ahead = lax.broadcasted_iota(jnp.int32, (BLK, R), 0) - token
    s = jnp.where(ahead <= quarter * T, s, -jnp.inf)
    m = jnp.max(s, axis=0, keepdims=True)
    p = jnp.exp2(s - m)
    p_ref[0] = p
    m_ref[0] = m
    l_ref[0] = jnp.sum(p, axis=0, keepdims=True)
    hi, lo = split(p)
    ot_ref[0] = values_sum(vt[...], hi, lo)

def picked(info, ql_ref, qr_ref, dl_ref, dr_ref, s0, s1, s2, s3,
           m0_ref, l0_ref, ot0_ref, ol_ref, or_ref, dq_ref, c_ref, rd_ref, g0, g1, g2, g3,
           kc, vc, kt, vt, s_sc, dk_acc, dv_acc):
    u, step = pl.program_id(0), pl.program_id(1)

    @pl.when((u == 0) & (step == 0))
    def _():
        for j in range(2):
            for x in range(4):
                rows = slice((j * 4 + x) * T, (j * 4 + x + 1) * T)
                piece = (s0, s1, s2, s3)[x]
                fill(piece[j, info[4]], rows, kc, kt)
                fill(piece[j, 1 - info[4]], rows, vc, vt)
        dk_acc[...] = jnp.zeros_like(dk_acc)
        dv_acc[...] = jnp.zeros_like(dv_acc)

    q = near_far(u, ql_ref, qr_ref) * (SCALE * LOG2E)
    do = near_far(u, dl_ref, dr_ref)
    qt = left(turned(q))
    m0 = m0_ref[0]
    m = m0
    for j in range(2):
        rows = slice(j * BLK, (j + 1) * BLK)
        s = mm(twice(kc[rows, :], 1), qt)
        s = jnp.where(info[2 + j] > 0, s, -jnp.inf)
        s_sc[rows, :] = s
        m = jnp.maximum(m, jnp.max(s, axis=0, keepdims=True))
    shrink = jnp.exp2(m0 - m)
    l = l0_ref[0] * shrink
    ot = ot0_ref[0] * shrink
    for j in range(2):
        rows = slice(j * BLK, (j + 1) * BLK)
        p = jnp.exp2(s_sc[rows, :] - m)
        s_sc[rows, :] = p
        hi, lo = split(p)
        l = l + jnp.sum(p, axis=0, keepdims=True)
        ot = ot + values_sum(vt[:, rows], hi, lo)
    inv = 1.0 / l
    ot = ot * inv
    dot = turned(do) * inv
    rd = jnp.sum(dot * ot, axis=0, keepdims=True)
    c_ref[0] = inv * shrink
    rd_ref[0] = rd * shrink
    o = upright(ot)

    @pl.when(u == 0)
    def _():
        ol_ref[...] = o

    @pl.when(u == 1)
    def _():
        or_ref[...] = o

    dt = left(dot)
    d2 = right(stacked(upright(dot)))
    q2 = right(stacked(q))
    dq = jnp.zeros((W, R), F32)
    for j in range(2):
        rows = slice(j * BLK, (j + 1) * BLK)
        p = s_sc[rows, :]
        p2 = jnp.concatenate(split(p), axis=1)
        dp = mm(twice(vc[rows, :], 1), dt)
        hi, lo = split(p * (dp - rd))
        dq = dq + values_sum(kt[:, rows], hi, lo)
        dv_acc[rows, :] += halves(mm(p2, d2))
        dk_acc[rows, :] += halves(mm(jnp.concatenate([hi, lo], axis=1), q2))
    dq_ref[0] = dq

    @pl.when((u == 1) & (step == STEPS - 1))
    def _():
        for j in range(2):
            for x, out in enumerate((g0, g1, g2, g3)):
                rows = slice((j * 4 + x) * T, (j * 4 + x + 1) * T)
                out[j, info[4]] = dk_acc[rows, :] * LN2
                out[j, 1 - info[4]] = dv_acc[rows, :]

def own_backward(info, ql_ref, qr_ref, dl_ref, dr_ref, mine_ref, other_ref, p_ref, c_ref, rd_ref, dq_ref,
                 of_ref, gl_ref, far_ref, h0, h1, h2, h3, vc, kt, dk_acc, dv_acc):
    u, step = pl.program_id(0), pl.program_id(1)

    @pl.when((u == 0) & (step == 0))
    def _():
        for c in range(4):
            k, v = own_quarter(info, mine_ref, other_ref, c)
            fill(k, slice(c * T, (c + 1) * T), None, kt)
            fill(v, slice(c * T, (c + 1) * T), vc, None)
        dk_acc[...] = jnp.zeros_like(dk_acc)
        dv_acc[...] = jnp.zeros_like(dv_acc)

    q = near_far(u, ql_ref, qr_ref) * (SCALE * LOG2E)
    dot = turned(near_far(u, dl_ref, dr_ref)) * c_ref[0]
    p = p_ref[0]
    hi, lo = split(p)
    dv_acc[...] += halves(mm(jnp.concatenate([hi, lo], axis=1), right(stacked(upright(dot)))))
    dp = mm(twice(vc[...], 1), left(dot))
    hi, lo = split(p * (dp - rd_ref[0]))
    dk_acc[...] += halves(mm(jnp.concatenate([hi, lo], axis=1), right(stacked(q))))
    dq = upright(dq_ref[0] + values_sum(kt[...], hi, lo)) * SCALE

    @pl.when(u == 0)
    def _():
        gl_ref[...] = dq

    @pl.when(u == 1)
    def _():
        far_ref[0] = of_ref[...]
        far_ref[1] = dq

    @pl.when((u == 1) & (step == STEPS - 1))
    def _():
        for x, out in enumerate((h0, h1, h2, h3)):
            rows = pl.ds(pl.multiple_of((info[0] ^ x) * T, T), T)
            out[info[4]] = dk_acc[rows, :] * LN2
            out[1 - info[4]] = dv_acc[rows, :]

def tile(shape):
    return pl.BlockSpec((1,) + shape[1:], lambda u, h, i: (u * STEPS + h, 0, 0))

def whole(shape):
    return pl.BlockSpec(shape, lambda u, h, i: (0,) * len(shape))

NEAR = pl.BlockSpec((T, HP * W), lambda u, h, i: (0, i[1] * STEPS + h))
FAR = pl.BlockSpec((T, HP * W), lambda u, h, i: (0, h))
FIRST = pl.BlockSpec((T, HP * W), lambda u, h, i: (0, jnp.where(u == 0, h, STEPS - 1)))
SECOND = pl.BlockSpec((T, HP * W), lambda u, h, i: (0, jnp.where(u == 0, 0, h)))
BOTH = pl.BlockSpec((2, T, HP * W), lambda u, h, i: (0, 0, jnp.where(u == 0, 0, h)))
PROBS, ROW, TURNED = (2 * STEPS, BLK, R), (2 * STEPS, 1, R), (2 * STEPS, W, R)
HALF, PIECE, PAIR = (T, 4 * W), (2, T, W), (2, 2, T, W)

def in_hbm(*arrays):
    return [pltpu.with_memory_space_constraint(a, pltpu.HBM) for a in arrays]

def kernel(body, ins, outs, out_shapes, scratch, flops, limit):
    return pl.pallas_call(
        body,
        out_shape=[pltpu.HBM(s, F32) for s in out_shapes],
        grid_spec=pltpu.PrefetchScalarGridSpec(
            num_scalar_prefetch=1,
            grid=(2, STEPS),
            in_specs=ins,
            out_specs=outs,
            scratch_shapes=[pltpu.VMEM(s, d) for s, d in scratch],
        ),
        compiler_params=pltpu.CompilerParams(
            dimension_semantics=("arbitrary", "arbitrary"), vmem_limit_bytes=limit << 20),
        cost_estimate=pl.CostEstimate(
            flops=flops, transcendentals=0, bytes_accessed=16 << 20),
        name=body.__name__,
    )

UNIT = 2 * 2048 * BLK * W * 4

def call_own_forward(info, q, q_far, mine, other):
    return kernel(
        own_forward,
        [NEAR, FAR, whole(mine.shape), whole(other.shape)],
        [tile(PROBS), tile(ROW), tile(ROW), tile(TURNED)],
        [PROBS, ROW, ROW, TURNED],
        [((BLK, 2 * W), BF), ((2 * W, BLK), BF)],
        2 * UNIT, 30,
    )(info, *in_hbm(q), q_far, *in_hbm(mine), other)

def call_picked(info, q, q_far, do, do_far, pieces, m, l, ot):
    return kernel(
        picked,
        [NEAR, FAR, NEAR, FAR] + [whole(PAIR)] * 4 + [tile(ROW), tile(ROW), tile(TURNED)],
        [FIRST, SECOND, tile(TURNED), tile(ROW), tile(ROW)] + [whole(PAIR)] * 4,
        [HALF, HALF, TURNED, ROW, ROW] + [PAIR] * 4,
        [((2 * BLK, 2 * W), BF), ((2 * BLK, 2 * W), BF), ((2 * W, 2 * BLK), BF), ((2 * W, 2 * BLK), BF),
         ((2 * BLK, R), F32),
         ((2 * BLK, W), F32), ((2 * BLK, W), F32)],
        10 * UNIT, 52,
    )(info, *in_hbm(q), q_far, *in_hbm(do), do_far, *pieces, *in_hbm(m, l, ot))

def call_own_backward(info, q, q_far, do, do_far, mine, other, p, c, rd, dq, o_far):
    return kernel(
        own_backward,
        [NEAR, FAR, NEAR, FAR, whole(mine.shape), whole(other.shape), tile(PROBS), tile(ROW), tile(ROW),
         tile(TURNED), SECOND],
        [FIRST, BOTH] + [whole(PIECE)] * 4,
        [HALF, (2,) + HALF] + [PIECE] * 4,
        [((BLK, 2 * W), BF), ((2 * W, BLK), BF), ((BLK, W), F32), ((BLK, W), F32)],
        3 * UNIT, 40,
    )(info, *in_hbm(q), q_far, *in_hbm(do), do_far, *in_hbm(mine), other, *in_hbm(p, c, rd, dq, o_far))

HEADS = (4, T, W)
SWAP = [(0, 1), (1, 0)]
PLACE = ("y", "x", "head")

def glue(body, args, outs, space=jax.ShapeDtypeStruct):
    spec = lambda shape: pl.BlockSpec(shape, lambda i: (0,) * len(shape))
    arrays = args[1:]
    return pl.pallas_call(
        body,
        out_shape=[space(s, F32) for s in outs],
        grid=(1,),
        in_specs=[pl.BlockSpec(memory_space=pltpu.SMEM)] + [spec(a.shape) for a in arrays],
        out_specs=[spec(s) for s in outs],
        compiler_params=pltpu.CompilerParams(
            dimension_semantics=("arbitrary",), vmem_limit_bytes=20 << 20),
        cost_estimate=pl.CostEstimate(
            flops=0, transcendentals=0,
            bytes_accessed=4 * sum(math.prod(s) for s in [a.shape for a in arrays] + list(outs))),
        name=body.__name__,
    )(args[0], *arrays)

def travel(array, step, stage):
    pairs = []
    for y in range(4):
        for x in range(4):
            for core in range(2):
                ty, tx = (y + step) % 4, x
                if core != stage:
                    ty, tx = y, (x + step) % 4
                pairs.append(((y * 4 + x) * 2 + core, (ty * 4 + tx) * 2 + core))
    return lax.ppermute(array, PLACE, pairs)

def circle(arrays, stage, back=False):
    step = (lambda s: 4 - s) if back else (lambda s: s)
    two = travel(arrays[1], step(2), stage)
    return [travel(arrays[0], step(1), stage), two, travel(arrays[2], step(3), stage)]

def mirror(array, flip):
    return lax.ppermute(array, "z", [(i, i ^ flip) for i in range(4)])

def swap(array):
    return lax.ppermute(array, "head", SWAP)

def after(array, *others):
    return lax.optimization_barrier((array, *others))[0]

def place():
    core, y, x = (lax.axis_index(a) for a in ("head", "y", "x"))
    return core, jnp.where(core == 0, y, x), jnp.where(core == 0, x, y)

def chosen(table, first, second, core, j):
    block = jnp.where(core == 0, first * 4 + second, second * 4 + first)
    other = jnp.maximum(table[block, 1 + j], 0)
    y, x = other // 4, other % 4
    return jnp.where(core == 0, y, x), jnp.where(core == 0, x, y)

def assemble(spot, keys, values, other, full):
    core = spot[0]
    half = T // 2
    here, there = (pl.ds(pl.multiple_of(c * half, half), half) for c in (core, 1 - core))
    for h in range(4):
        cols = slice(h * W, (h + 1) * W)
        full[h, here] = jnp.where(core == 0, keys[:, cols], values[:, cols])
        full[h, there] = other[:, cols]

def pick(table, *refs):
    core, here, there = place()
    along, out = refs[0:4], refs[4:7]
    for step in (1, 2, 3):
        for j in range(2):
            first, _ = chosen(table, here, (there + step) % 4, core, j)
            for i in range(4):
                @pl.when((here - first) % 4 == i)
                def _(source=along[i], ref=out[step - 1], j=j):
                    ref[j] = source[...]

def join(table, *refs):
    core, here, there = place()
    along, got, (mine, send) = refs[0:4], refs[4:7], refs[7:9]
    for j in range(2):
        first, second = chosen(table, here, there, core, j)
        near, off = (here - first) % 4, (there - second) % 4
        for c, out in ((core, mine), (1 - core, send)):
            heads = pl.ds(2 * c, 2)
            for k in range(4):
                @pl.when((off == 0) & (near == k))
                def _(source=along[k], out=out, heads=heads, j=j):
                    out[j] = source[heads]
            for k in range(3):
                @pl.when(off == k + 1)
                def _(source=got[k], out=out, heads=heads, j=j):
                    out[j] = source[j, heads]

def arrange(spot, mine, other, same, cross):
    head = spot[1]
    for j in range(2):
        for n, ref in enumerate((mine, other)):
            same[j, n] = ref[j, head]
            cross[j, n] = ref[j, 1 - head]

def spread(spot, mine, added, passed, passed2, keep, send):
    head = spot[1]
    for j in range(mine.shape[0]):
        for n, out in ((0, keep), (1, send)):
            out[j, head] = mine[j, n] + added[j, n]
            out[j, 1 - head] = passed[j, n] + passed2[j, n]

def gather_heads(spot, keep, other, full):
    core = spot[0]
    for j in range(2):
        full[j, pl.ds(2 * core, 2)] = keep[j]
        full[j, pl.ds(2 * (1 - core), 2)] = other[j]

def collect(table, *refs):
    core, here, there = place()
    got, out = refs[0:4], refs[4:8]
    for ref in out:
        ref[...] = jnp.zeros_like(ref)
    for step in range(4):
        for j in range(2):
            first, second = chosen(table, here, (there - step) % 4, core, j)
            for i in range(4):
                @pl.when((second == there) & ((here - first) % 4 == i))
                def _(source=got[step], ref=out[i], j=j):
                    ref[...] += source[j]

def shards(queries, keys, values, cotangent, selected):
    core, z = lax.axis_index("head"), lax.axis_index("z")
    head = z // 2
    mine = lax.dynamic_slice(selected, (lax.axis_index("y") * 4 + lax.axis_index("x"), 1), (1, 2))[0]
    info = jnp.concatenate([jnp.stack([z, head]), (mine >= 0).astype(jnp.int32), core[None]])
    spot = jnp.stack([core, head])
    far = 1 - head
    got = swap(jnp.where(core == 0, values, keys))
    (full,) = glue(assemble, (spot, *in_hbm(keys, values), got), (HEADS,))
    own = lax.all_gather(full, "z", axis=0)

    along = [full] + circle([full] * 3, 0)

    def turned_over(array, *others):
        return mirror(lax.dynamic_slice_in_dim(after(array, *others), far * 4 * W, 4 * W, 1), 3)

    q_far = turned_over(queries, along[1])
    do_far = turned_over(cotangent, q_far)
    sent = glue(pick, (selected, *along), ((2,) + HEADS,) * 3)
    got = circle(sent, 1)
    kept, send = glue(join, (after(selected, q_far), *along, *got), (PAIR, PAIR))
    same, cross = glue(arrange, (spot, kept, swap(send)), (PAIR, PAIR))
    own_other = swap(lax.dynamic_index_in_dim(own, 2 * (1 - core) + head, 1, keepdims=False))
    pieces = [same] + [mirror(a, flip) for a, flip in ((same, 1), (cross, 2), (cross, 3))]

    p, m, l, ot = call_own_forward(after(info, do_far), queries, q_far, own, own_other)
    out = call_picked(info, queries, q_far, cotangent, do_far, pieces, m, l, ot)
    o_near, o_far, dq, c, rd = out[:5]
    last = call_own_backward(
        info, queries, q_far, cotangent, do_far, own, own_other, p, c, rd, dq, o_far)

    def reduced(g, *others):
        arrived = [g[0]] + [mirror(g[flip], flip) for flip in (1, 2, 3)]
        arrived[3] = after(arrived[3], *others)
        keep, send = glue(spread, (spot, *arrived), (g[0].shape,) * 2)
        return keep, swap(send)

    (terms,) = glue(gather_heads, (spot, *reduced(out[5:9], last[0])), ((2,) + HEADS,))
    arrived = [terms] + circle([terms] * 3, 1)
    low, high = reduced([after(a, terms)[None] for a in last[2:6]])
    back_far = mirror(after(last[1], low), 3)
    sums = glue(collect, (after(selected, low), *arrived), (HEADS,) * 4, pltpu.HBM)

    def sides(a, b):
        return jnp.where(head == 0, jnp.concatenate([a, b], 1), jnp.concatenate([b, a], 1))

    wide = sides(o_near, back_far[0]), sides(last[0], back_far[1])
    total = after(sums[0], *wide) + sum(circle(sums[1:], 0, True))
    total = total + jnp.where(
        core == 0, jnp.concatenate([low[0], high[0]], 0), jnp.concatenate([high[0], low[0]], 0)
    )

    half = T // 2

    def tokens(which):
        a = lax.dynamic_slice_in_dim(total, which * half, half, 1)
        return jnp.concatenate([a[h] for h in range(4)], 1)

    keep, back = tokens(core), swap(tokens(1 - core))

    return (
        *wide,
        jnp.where(core == 0, keep, back),
        jnp.where(core == 0, back, keep),
    )

def solution(mesh):
    grid = Mesh(mesh.devices.reshape(4, 4, 4, 2), ("y", "x", "z", "head"))
    tokens = ("y", "x", "z")
    wide, narrow = P(tokens, "head"), P(tokens + ("head",), None)
    return jax.shard_map(
        shards,
        mesh=grid,
        in_specs=(wide, narrow, narrow, wide, P()),
        out_specs=(wide, wide, narrow, narrow),
        check_vma=False,
    )
```
